32 devices in a mesh: rep: 16 (over z, y, core), grp: 2 (over x).
Axes of the slice: x: 2, y: 2, z: 4, core: 2. Of those that a mesh axis runs over, the one named last changes fastest.
Arguments:
- images: bfloat16 [256, 197, 512], P(('rep', 'grp')), may hold values from -6 to 6
- ln1_gain: bfloat16 [512], P('grp'), may hold values from 0.5 to 1.5
- ln1_bias: bfloat16 [512], P('grp'), may hold values from -1.1953125 to 1.1953125
- qkv_weight: bfloat16 [512, 1536], P('grp'), may hold values from -0.31640625 to 0.31640625
- out_weight: bfloat16 [512, 512], P('grp'), may hold values from -1 to 1
- ln2_gain: bfloat16 [512], P('grp'), may hold values from 0.5 to 1.5
- ln2_bias: bfloat16 [512], P('grp'), may hold values from -1.1953125 to 1.1953125
- router_weight: bfloat16 [512, 8], P('grp'), may hold values from -0.19824219 to 0.19824219
- expert_in: bfloat16 [8, 512, 2048], P(None, 'grp'), may hold values from -0.25 to 0.25
- expert_out: bfloat16 [8, 2048, 512], P(None, 'grp'), may hold values from -0.79296875 to 0.79296875
- routes: int32 [256, 197, 2], P(('rep', 'grp')), may hold values from 0 to 7, all different within a row; in each aligned block of 1576 rows (0 to 1575, 1576 to 3151, ..., all dimensions but the last counted through in order) at most 788 rows name the same one
- cotangent: bfloat16 [256, 197, 512], P(('rep', 'grp')), may hold values from -6 to 6
Outputs:
- layer_out: bfloat16 [256, 197, 512], P(('rep', 'grp'))
- input_grad: bfloat16 [256, 197, 512], P(('rep', 'grp'))
- clipped_qk: float32 [512, 1024], P('grp')
- grad_ln1_gain: float32 [512], P('grp')
- grad_ln1_bias: float32 [512], P('grp')
- grad_qkv_weight: float32 [512, 1536], P('grp')
- grad_out_weight: float32 [512, 512], P('grp')
- grad_ln2_gain: float32 [512], P('grp')
- grad_ln2_bias: float32 [512], P('grp')
- grad_router_weight: float32 [512, 8], P('grp')
- grad_expert_in: float32 [8, 512, 2048], P(None, 'grp')
- grad_expert_out: float32 [8, 2048, 512], P(None, 'grp')
The draws below stay inside these ranges and needn't reach their ends.
Inputs may be any that keep to these rules, and one draw needn't show every extreme that they name: `routes`: each token names 2 different experts; among the tokens of one device no expert is named by more than 788 pairs.
All inputs are finite; a program needn't handle non-finite values.
Results may differ from the reference program's by a relative error of at most 0.014.
Values may be sent and summed in bfloat16 or wider, within the bound.
No kernel may reach another device: no remote copies, remote signals or barrier semaphores. Data moves between devices by JAX's collectives and lax.ppermute only.
A program may use at most 320 MiB of HBM per device.

```python
import math
import jax
import jax.numpy as jnp
import numpy as np
from jax import lax

D = 512
HEADS = 8
HEAD_DIM = 64
FF = 2048
E = 8
TOP = 2
SEQ = 197
IMG_DEV = 8
CAP = 591
MOST = 788
IMAGES = 256


def block_scale(stream_key, extent, shards, least, largest):
    level = 1.0
    for axis_at, parts in shards:
        steps = jax.random.uniform(jax.random.fold_in(jax.random.fold_in(stream_key, 6), axis_at), (parts,), jnp.float32, least / len(shards), largest / len(shards))
        level = level * jnp.repeat(jnp.exp(steps), extent[axis_at] // parts).reshape((-1,) + (1,) * (len(extent) - 1 - axis_at))
    return level


def assign_block(stream_key, own, number, rows, count, top, bound, slope):
    order = jax.random.permutation(stream_key, count)
    packed, ordinary = shares(count, rows * top, bound, slope, True), shares(count, rows * top, bound, slope, False)
    places = jnp.arange(count)

    def named(tallies, rotation):
        used = int((tallies > 0).sum())
        fixed = max(1, used // 4)
        shifted = fixed + (places - fixed + rotation * (used - fixed)) % max(1, count - fixed)
        return jnp.zeros((count,), jnp.int32).at[order[jnp.where(places < fixed, places, shifted)]].set(jnp.asarray(tallies, jnp.int32))

    tallies = jnp.where(number % 4 == 0, named(packed, number // 4), named(ordinary, number - number // 4 - 1))
    mixed = jax.random.permutation(jax.random.fold_in(own, 3), count)
    giver, sink = mixed[0:count // 2 * 2:2], mixed[1:count // 2 * 2:2]
    room = jnp.minimum(tallies[giver] - 1, bound - tallies[sink]) // 2
    room = jnp.where((giver == order[0]) | (sink == order[0]) | (tallies[sink] == 0), 0, jnp.maximum(room, 0))
    shifted = jax.random.randint(jax.random.fold_in(own, 4), (count // 2,), 0, 1 << 20) % (room + 1)
    tallies = tallies.at[giver].add(-shifted).at[sink].add(shifted)
    items = jnp.searchsorted(jnp.cumsum(tallies), jnp.arange(rows * top), side="right").astype(jnp.int32)
    grid = items.reshape(top, rows).T
    grid = grid[jax.random.permutation(jax.random.fold_in(own, 1), rows)]
    rotation = jax.random.randint(jax.random.fold_in(own, 2), (rows, 1), 0, top)
    return jnp.take_along_axis(grid, (jnp.arange(top)[None, :] + rotation) % top, axis=1)


def shares(amount, total, limit, lean, full):
    loads = [(1 << 20) // math.isqrt(grade ** lean) + 1 for grade in range(1, amount + 1)]
    largest = limit if full else min(limit, max(-(-total // amount), total * loads[0] // sum(loads)))
    least = 1 if total - largest >= amount - 1 else 0
    counts, surplus = [largest] + [least] * (amount - 1), total - largest - least * (amount - 1)
    while surplus > 0:
        movable = [i for i in range(1, amount) if counts[i] < largest] or [i for i in range(1, amount) if counts[i] < limit]
        mass, budget = sum([loads[i] for i in movable]), surplus
        for i in movable:
            addition = min(limit - counts[i], max(1, budget * loads[i] // mass), surplus)
            counts[i] = counts[i] + addition
            surplus = surplus - addition
    return np.array(counts)


def normal_values(rng, shape, scale, limit, pieces=(), kind=jnp.bfloat16):
    values = scale * jax.random.normal(rng, shape, jnp.float32)
    if pieces:
        values = values * block_scale(rng, shape, pieces, -0.22, 0.18)
    return jnp.clip(values, -limit, limit).astype(kind)


def setup_inputs(seed: int = 0) -> dict:
    splits = jax.random.split(jax.random.key(seed), 13)
    images = normal_values(splits[0], (IMAGES, SEQ, D), 1.0, 6.0, ((0, 32),))
    ln1_gain = jnp.clip(1.0 + 0.1 * jax.random.normal(splits[1], (D,), jnp.float32), 0.5, 1.5).astype(jnp.bfloat16)
    ln1_bias = normal_values(splits[2], (D,), 0.3, 1.1953125, ((0, 2),))
    qkv_weight = normal_values(splits[3], (D, 3 * D), (1.2 * D ** -0.5), 0.31640625, ((0, 2),))
    out_weight = normal_values(splits[4], (D, D), (D // 16) ** -0.5, 1.0, ((0, 2),))
    ln2_gain = jnp.clip(1.0 + 0.1 * jax.random.normal(splits[5], (D,), jnp.float32), 0.5, 1.5).astype(jnp.bfloat16)
    ln2_bias = normal_values(splits[6], (D,), 0.3, 1.1953125, ((0, 2),))
    router_weight = normal_values(splits[7], (D, E), (0.75 * D ** -0.5), 0.19824219, ((0, 2),))
    expert_in = normal_values(splits[8], (E, D, FF), D ** -0.5, 0.25, ((1, 2),))
    expert_out = normal_values(splits[9], (E, FF, D), (6.0 * FF ** -0.5), 0.79296875, ((1, 2),))
    routes_keys = jax.random.split(jax.random.fold_in(splits[10], 1), IMAGES * SEQ // (IMG_DEV * SEQ))
    routes_turns = jax.random.permutation(jax.random.fold_in(splits[10], 3), IMAGES * SEQ // (IMG_DEV * SEQ))
    routes = jax.vmap(lambda own, number: assign_block(jax.random.fold_in(splits[10], 2), own, number, IMG_DEV * SEQ, E, TOP, MOST, 1))(routes_keys, routes_turns).reshape((IMAGES, SEQ, TOP))
    cotangent = normal_values(splits[11], (IMAGES, SEQ, D), 1.0, 6.0, ((0, 32),))
    return {"images": images, "ln1_gain": ln1_gain, "ln1_bias": ln1_bias, "qkv_weight": qkv_weight, "out_weight": out_weight, "ln2_gain": ln2_gain, "ln2_bias": ln2_bias, "router_weight": router_weight, "expert_in": expert_in, "expert_out": expert_out, "routes": routes, "cotangent": cotangent}


norm_eps = 1e-06
clip_limit = 3.0
highest = lax.Precision.HIGHEST

@jax.custom_vjp
def low(v):
    return lax.optimization_barrier(v.astype(jnp.bfloat16)).astype(jnp.float32)

@jax.custom_vjp
def low_back(v):
    return v

def low_keep(v):
    return (low(v), None)

def low_pass(kept, grad):
    return (grad,)

def back_keep(v):
    return (v, None)

def back_low(kept, grad):
    return (low(grad),)
low.defvjp(low_keep, low_pass)
low_back.defvjp(back_keep, back_low)

def layer_norm(rows, gain, shift):
    center = lax.optimization_barrier(jnp.mean(rows, axis=-1, keepdims=True))
    spread = rows - center
    variance = lax.optimization_barrier(jnp.mean(spread * spread, axis=-1, keepdims=True))
    return spread * lax.rsqrt(variance + norm_eps) * gain + shift

def slot_table(route_rows):
    order_ids = jnp.transpose(route_rows).reshape(-1)
    expert_ids = jnp.arange(E, dtype=jnp.int32)
    one_hot = (order_ids[:, None] == expert_ids[None, :]).astype(jnp.int32)
    earlier = jnp.cumsum(one_hot, axis=0) - one_hot
    position = lax.optimization_barrier(jnp.sum(earlier * one_hot, axis=1))
    kept_pair = position < CAP
    flat_index = jnp.where(kept_pair, order_ids * CAP + position, E * CAP).astype(jnp.int32)
    return flat_index

def block_forward(params, image_rows, route_rows):
    gain_one, bias_one, qkv_w, out_w, gain_two, bias_two, router_w, first_w, second_w = params
    tokens = image_rows.reshape(-1, D)
    normed = low(layer_norm(tokens, gain_one, bias_one))
    qkv = low(low_back(jnp.dot(normed, qkv_w, precision=highest)))
    qkv = qkv.reshape(IMG_DEV, SEQ, 3, HEADS, HEAD_DIM)
    query = qkv[:, :, 0]
    key_rows = qkv[:, :, 1]
    value_rows = qkv[:, :, 2]
    scores = low_back(jnp.einsum('bqhd,bkhd->bhqk', query, key_rows, precision=highest) * HEAD_DIM ** (-0.5))
    head_max = lax.optimization_barrier(jnp.max(scores, axis=(0, 2, 3)))
    probs = low(jax.nn.softmax(scores, axis=-1))
    mixed = jnp.einsum('bhqk,bkhd->bqhd', probs, value_rows, precision=highest)
    mixed = low(low_back(mixed.reshape(-1, D)))
    branch = low_back(jnp.dot(mixed, out_w, precision=highest))
    middle = tokens + branch
    hidden = low(layer_norm(middle, gain_two, bias_two))
    logits = low_back(jnp.dot(hidden, router_w, precision=highest))
    router_p = jax.nn.softmax(logits, axis=-1)
    gates = jnp.transpose(jnp.take_along_axis(router_p, route_rows, axis=1))
    flat_index = slot_table(route_rows)
    buffer_rows = jnp.zeros((E * CAP + 1, D), jnp.float32)
    slots_in = buffer_rows.at[flat_index].set(jnp.tile(hidden, (TOP, 1)))[:E * CAP].reshape(E, CAP, D)
    pre_act = low_back(jnp.einsum('ecd,edf->ecf', slots_in, first_w, precision=highest))
    activ = low(jax.nn.gelu(pre_act, approximate=True))
    expert_res = low_back(jnp.einsum('ecf,efd->ecd', activ, second_w, precision=highest)).reshape(E * CAP, D)
    extended = jnp.concatenate([expert_res, jnp.zeros((1, D), jnp.float32)], axis=0)
    pair_out = jnp.take(extended, flat_index, axis=0).reshape(TOP, -1, D)
    combined = lax.optimization_barrier(jnp.sum(gates[:, :, None] * pair_out, axis=0))
    result = middle + combined
    return (result.reshape(IMG_DEV, SEQ, D), head_max)

def reference(images, ln1_gain, ln1_bias, qkv_weight, out_weight, ln2_gain, ln2_bias, router_weight, expert_in, expert_out, routes, cotangent):
    params = (ln1_gain.astype(jnp.float32), ln1_bias.astype(jnp.float32), qkv_weight.astype(jnp.float32), out_weight.astype(jnp.float32), ln2_gain.astype(jnp.float32), ln2_bias.astype(jnp.float32), router_weight.astype(jnp.float32), expert_in.astype(jnp.float32), expert_out.astype(jnp.float32))
    block_count = IMAGES // IMG_DEV
    image_blocks = images.astype(jnp.float32).reshape(block_count, IMG_DEV, SEQ, D)
    route_blocks = routes.reshape(block_count, IMG_DEV * SEQ, TOP)

    def whole(weights, inputs):

        def one_block(pair):
            return block_forward(weights, pair[0], pair[1])
        return lax.map(jax.checkpoint(one_block), (inputs, route_blocks))
    (result, head_max), pullback = jax.vjp(whole, params, image_blocks)
    upstream = cotangent.astype(jnp.float32).reshape(block_count, IMG_DEV, SEQ, D)
    param_grads, image_grads = pullback((upstream, jnp.zeros_like(head_max)))
    overall = lax.optimization_barrier(jnp.max(head_max, axis=0))
    clip = jnp.sqrt(clip_limit / jnp.maximum(overall, clip_limit))
    column_scale = jnp.tile(jnp.repeat(clip, HEAD_DIM), 2)
    clipped = params[2][:, :2 * D] * column_scale[None, :]
    return (result.reshape(IMAGES, SEQ, D).astype(jnp.bfloat16), image_grads.reshape(IMAGES, SEQ, D).astype(jnp.bfloat16), clipped, param_grads[0], param_grads[1], param_grads[2], param_grads[3], param_grads[4], param_grads[5], param_grads[6], param_grads[7], param_grads[8])
```

```python
import functools
import math

import jax
import jax.numpy as jnp
from jax import lax
from jax.experimental import pallas as pl
from jax.experimental.pallas import tpu as pltpu
from jax.sharding import PartitionSpec as P

D = 512
HEADS = 8
HEAD_DIM = 64
FF = 2048
E = 8
TOP = 2
SEQ = 197
CAP = 591
ROWS = 208
SLOTS = 640
WIN = 128
AUX = 128
WIDE = 2 * D + AUX
NORM_EPS = 1e-06
CLIP_LIMIT = 3.0
SCALE = HEAD_DIM ** (-0.5)
LOW = -1e30
F32 = jnp.float32
BF16 = jnp.bfloat16
I32 = jnp.int32


def dot(a, b):
    return lax.dot_general(a, b, (((1,), (0,)), ((), ())), preferred_element_type=F32)


def dot_nt(a, b):
    return lax.dot_general(a, b, (((1,), (1,)), ((), ())), preferred_element_type=F32)


def dot_tn(a, b):
    return lax.dot_general(a, b, (((0,), (0,)), ((), ())), preferred_element_type=F32)


def params(*semantics):
    return pltpu.CompilerParams(dimension_semantics=semantics, vmem_limit_bytes=60 * 1024 * 1024)


def lanes(shape):
    return lax.broadcasted_iota(I32, shape, len(shape) - 1)


def subs(shape):
    return lax.broadcasted_iota(I32, shape, len(shape) - 2)


def route_kernel(routes_ref, slot_ref, slot_t_ref, starts_ref, work):
    images = routes_ref.shape[0]
    lane = lanes((ROWS, 128))
    strict = (lanes((ROWS, ROWS)) < subs((ROWS, ROWS))).astype(BF16)
    work[...] = jnp.full_like(work, -100)
    hots = []
    befores = []
    run = jnp.zeros((1, 128), F32)
    for b in range(images):
        work[0:SEQ, 0:TOP] = routes_ref[b]
        both = work[...]
        hot = ((both[:, 0:1] == lane) & (lane < E)) | (both[:, 1:2] + E == lane) & (lane >= E) & (lane < 2 * E)
        hot = hot.astype(F32)
        hots.append(hot)
        befores.append(dot(strict, hot.astype(BF16)) + run)
        run = run + jnp.sum(hot, axis=0, keepdims=True)
    first = jnp.where(lanes((1, 128)) < E, run, 0.0)
    shift = pltpu.roll(first, E, 1)
    base = jnp.zeros((1, 128), F32)
    starts = jnp.zeros((16, 128), F32)
    row = subs((16, 128))
    for b in range(images):
        kept = jnp.where(befores[b] + shift < CAP, hots[b], 0.0)
        kept = kept + pltpu.roll(kept, 128 - E, 1)
        kept = jnp.where(lane < E, kept, 0.0)
        place = dot(strict, kept.astype(BF16)) + base
        slot = jnp.where(kept > 0.0, place, -1000.0)
        slot_ref[b] = slot.astype(I32)
        slot_t_ref[b] = jnp.transpose(slot)[0:E, :].astype(I32)
        starts = jnp.where(row == b, base, starts)
        base = base + jnp.sum(kept, axis=0, keepdims=True)
    starts_ref[...] = jnp.where(row == images, base, starts).astype(I32)


def route_tables(routes):
    images = routes.shape[0]
    return pl.pallas_call(
        route_kernel,
        out_shape=(
            jax.ShapeDtypeStruct((images, ROWS, 128), I32),
            jax.ShapeDtypeStruct((images, E, ROWS), I32),
            jax.ShapeDtypeStruct((16, 128), I32),
        ),
        scratch_shapes=[pltpu.VMEM((ROWS, 128), I32)],
        compiler_params=params(),
        name="routing",
    )(routes)


def windows(starts, b):
    firsts, needs = [], []
    passes = jnp.int32(0)
    for e in range(E):
        start = starts[b, e]
        first = (start // 16) * 16
        need = starts[b + 1, e] - first
        firsts.append(first)
        needs.append(need)
        passes = jnp.maximum(passes, (need + WIN - 1) // WIN)
    return firsts, needs, passes


def norm_stats(rows):
    center = jnp.mean(rows, axis=-1, keepdims=True)
    spread = rows - center
    rs = lax.rsqrt(jnp.mean(spread * spread, axis=-1, keepdims=True) + NORM_EPS)
    return spread * rs, rs


def head_lane(half):
    lane = lanes((ROWS, 128))
    return (lane < HEAD_DIM) if half == 0 else (lane >= HEAD_DIM)


def front_kernel(
    starts, img_ref, cot_ref, slot_t_ref, ln_ref, qkvw_ref, outw_ref, rw_ref,
    qkv_ref, mixed_ref, middle_ref, rp_ref, lse_ref, hmax_ref, slots_ref,
    xb, rhs, oh,
):
    b = pl.program_id(0)

    @pl.when(b == 0)
    def _():
        xb[...] = jnp.zeros_like(xb)
        rhs[...] = jnp.zeros_like(rhs)
        slots_ref[...] = jnp.zeros_like(slots_ref)
        hmax_ref[...] = jnp.full_like(hmax_ref, LOW)

    xb[0:SEQ, :] = img_ref[0].astype(F32)
    x = xb[...]
    n1, _ = norm_stats(x)
    normed = (n1 * ln_ref[0:1, :] + ln_ref[1:2, :]).astype(BF16)
    qkv = dot(normed, qkvw_ref[...]).astype(BF16)
    qkv_ref[0] = qkv
    zero = jnp.zeros((ROWS, 128), BF16)
    cols = lanes((ROWS, ROWS))
    real = subs((ROWS, 1)) < SEQ
    lane = lanes((ROWS, 128))
    lse_all = jnp.zeros((ROWS, 128), F32)
    peaks = jnp.full((ROWS, 128), LOW, F32)
    parts = []
    for pair in range(HEADS // 2):
        q = qkv[:, 128 * pair : 128 * pair + 128]
        k = qkv[:, D + 128 * pair : D + 128 * pair + 128]
        v = qkv[:, 2 * D + 128 * pair : 2 * D + 128 * pair + 128]
        total = None
        for half in range(2):
            mine = head_lane(half)
            s = dot_nt(q, jnp.where(mine, k, zero)) * SCALE
            s = jnp.where(cols < SEQ, s, LOW)
            top = jnp.max(s, axis=-1, keepdims=True)
            powers = jnp.exp(s - top)
            norm = jnp.sum(powers, axis=-1, keepdims=True)
            probs = (powers / norm).astype(BF16)
            part = dot(probs, jnp.where(mine, v, zero))
            total = part if total is None else total + part
            h = 2 * pair + half
            lse_all = jnp.where(lane == h, top + jnp.log(norm), lse_all)
            peaks = jnp.where((lane == h) & real, top, peaks)
        parts.append(total.astype(BF16))
    mixed = jnp.concatenate(parts, axis=1)
    mixed_ref[0] = mixed
    lse_ref[0] = jnp.transpose(lse_all)[0:HEADS, :]
    hmax_ref[...] = jnp.maximum(hmax_ref[...], jnp.max(peaks, axis=0, keepdims=True))
    middle = x + dot(mixed, outw_ref[...])
    middle_ref[0] = middle
    n2, _ = norm_stats(middle)
    hidden = (n2 * ln_ref[2:3, :] + ln_ref[3:4, :]).astype(BF16)
    logits = jnp.where(lane < E, dot(hidden, rw_ref[...]), LOW)
    powers = jnp.exp(logits - jnp.max(logits, axis=-1, keepdims=True))
    rp = powers / jnp.sum(powers, axis=-1, keepdims=True)
    rp_ref[0] = rp
    high = rp.astype(BF16).astype(F32)
    rhs[:, 0:D] = hidden
    rhs[0:SEQ, D : 2 * D] = cot_ref[0]
    rhs[:, 2 * D : WIDE] = (high + pltpu.roll(rp - high, E, 1)).astype(BF16)

    firsts, needs, passes = windows(starts, b)
    place = subs((WIN, ROWS))

    def one_pass(p, carry):
        offs = []
        for e in range(E):
            begin = firsts[e] + p * WIN
            off = pl.multiple_of(jnp.minimum(begin, SLOTS - WIN), 16)
            offs.append(off)
            named = slot_t_ref[0, e : e + 1, :]
            ok = (named >= begin) & (named < begin + WIN)
            hit = jnp.where(ok, named - off, -1) == place
            oh[WIN * e : WIN * e + WIN, :] = hit.astype(F32).astype(BF16)
        picked = dot(oh[...], rhs[...]).astype(BF16)
        for e in range(E):

            @pl.when(p * WIN < needs[e])
            def _():
                slots_ref[e, pl.ds(offs[e], WIN), :] += picked[WIN * e : WIN * e + WIN, :]

        return carry

    lax.fori_loop(0, passes, one_pass, 0)


def front(starts, images, cot, slot_t, ln, qkvw, outw, rw):
    n = images.shape[0]
    whole = lambda shape: pl.BlockSpec(shape, lambda b, s: (0,) * len(shape), pipeline_mode=pl.Buffered(1))
    item = lambda *shape: pl.BlockSpec((1,) + shape, lambda b, s: (b,) + (0,) * len(shape))
    return pl.pallas_call(
        front_kernel,
        grid_spec=pltpu.PrefetchScalarGridSpec(
            num_scalar_prefetch=1,
            grid=(n,),
            in_specs=[
                item(SEQ, D), item(SEQ, D), item(E, ROWS), whole((8, D)), whole((D, 3 * D)), whole((D, D)), whole((D, AUX)),
            ],
            out_specs=[
                item(ROWS, 3 * D), item(ROWS, D), item(ROWS, D), item(ROWS, AUX), item(HEADS, ROWS),
                whole((1, 128)), whole((E, SLOTS, WIDE)),
            ],
            scratch_shapes=[
                pltpu.VMEM((ROWS, D), F32), pltpu.VMEM((ROWS, WIDE), BF16), pltpu.VMEM((E * WIN, ROWS), BF16),
            ],
        ),
        out_shape=(
            jax.ShapeDtypeStruct((n, ROWS, 3 * D), BF16),
            jax.ShapeDtypeStruct((n, ROWS, D), BF16),
            jax.ShapeDtypeStruct((n, ROWS, D), F32),
            jax.ShapeDtypeStruct((n, ROWS, AUX), F32),
            jax.ShapeDtypeStruct((n, HEADS, ROWS), F32),
            jax.ShapeDtypeStruct((1, 128), F32),
            jax.ShapeDtypeStruct((E, SLOTS, WIDE), BF16),
        ),
        compiler_params=params("arbitrary"),
        name="front",
    )(starts, images, cot, slot_t, ln, qkvw, outw, rw)


def gelu_parts(pre):
    c = math.sqrt(2.0 / math.pi)
    sq = pre * pre
    t = jnp.tanh(c * pre * (1.0 + 0.044715 * sq))
    half = 0.5 * (1.0 + t)
    act = pre * half
    slope = half + 0.5 * pre * (1.0 - t * t) * (c * (1.0 + 3.0 * 0.044715 * sq))
    return act, slope


def expert_kernel(nb, adds, ids, slots_ref, win0_ref, wout0_ref, *refs):
    refs = list(refs)
    other_ref = refs.pop(0) if nb == 2 else None
    sums = [refs.pop(0) for _ in range(nb)] if adds else None
    out_ref = refs.pop(0)
    grads = [refs.pop(0) for _ in range(nb)]
    act_s, preg_s = refs
    e = ids[0]
    me = ids[1]
    hb = win0_ref.shape[1]
    spot = [me, 1 - me] if nb == 2 else [0]

    def at(ref, start, size):
        if isinstance(start, int):
            return ref[:, start : start + size]
        return ref[:, pl.ds(pl.multiple_of(start, 128), size)]

    def win(r, q):
        return win0_ref[0, :, 512 * q : 512 * q + 512] if r == 0 else other_ref[q]

    def win_cols(r, start):
        if isinstance(start, int):
            return win0_ref[0, :, start : start + hb]
        if r == 0:
            return win0_ref[0, :, pl.ds(pl.multiple_of(start, 128), hb)]
        return other_ref[start // 512, :, pl.ds(pl.multiple_of(start % 512, 128), hb)]

    def wout(r, q):
        return wout0_ref[0, hb * q : hb * q + hb, :] if r == 0 else other_ref[4 + q]

    view = slots_ref.at[0]
    hid = [at(view, spot[r] * hb, hb) for r in range(nb)]
    got = view[:, D : 2 * D].astype(F32)
    aux = view[:, 2 * D : WIDE].astype(F32)
    lane = lanes((SLOTS, AUX))
    gate = jnp.sum(jnp.where((lane == e) | (lane == e + E), aux, 0.0), axis=-1, keepdims=True)
    resg = (gate * got).astype(BF16)
    for r in range(nb):
        for q in range(4):
            start = spot[r] * (4 * hb) + q * hb
            pre = dot(hid[0], win_cols(0, start))
            for o in range(1, nb):
                pre = pre + dot(hid[o], win_cols(o, start))
            act, slope = gelu_parts(pre)
            actg = dot_nt(resg, wout(r, q))
            if isinstance(start, int):
                act_s[:, start : start + hb] = act.astype(BF16)
                preg_s[:, start : start + hb] = (actg * slope).astype(BF16)
            else:
                act_s[:, pl.ds(pl.multiple_of(start, 128), hb)] = act.astype(BF16)
                preg_s[:, pl.ds(pl.multiple_of(start, 128), hb)] = (actg * slope).astype(BF16)
    res = None
    for r in range(nb):
        for q in range(4):
            part = dot(at(act_s, spot[r] * (4 * hb) + q * hb, hb), wout(r, q))
            res = part if res is None else res + part
    out_ref[0, :, 0:D] = (gate * res).astype(BF16)
    gg = jnp.sum(got * res, axis=-1, keepdims=True)
    high = gg.astype(BF16).astype(F32)
    out_ref[0, :, 2 * D : WIDE] = jnp.where(lane == e, high, jnp.where(lane == e + E, gg - high, 0.0)).astype(BF16)
    for r in range(nb):
        back = None
        for q in range(4):
            part = dot_nt(preg_s[:, 512 * q : 512 * q + 512], win(r, q))
            back = part if back is None else back + part
        if nb == 1:
            out_ref[0, :, D : 2 * D] = back.astype(BF16)
        else:
            out_ref[0, :, pl.ds(pl.multiple_of(D + spot[r] * hb, 128), hb)] = back.astype(BF16)
    for r in range(nb):
        for q in range(4):
            gin = dot_tn(hid[r], preg_s[:, 512 * q : 512 * q + 512])
            gout = dot_tn(at(act_s, spot[r] * (4 * hb) + q * hb, hb), resg)
            if adds:
                gin = gin + sums[r][q].astype(F32)
                gout = gout + sums[r][4 + q].astype(F32)
            grads[r][q] = gin.astype(BF16)
            grads[r][4 + q] = gout.astype(BF16)


def expert_call(ids, slots, win0, wout0, other, sums):
    nb = 1 if other is None else 2
    hb = win0.shape[1]
    adds = sums is not None
    once = lambda shape: pl.BlockSpec(shape, lambda i, s: (0,) * len(shape))
    ins = [slots, win0, wout0] + ([other] if nb == 2 else []) + (list(sums) if adds else [])
    pick = lambda *shape: pl.BlockSpec((1,) + shape, lambda i, s: (s[0],) + (0,) * len(shape))
    specs = [pick(SLOTS, WIDE), pick(hb, FF), pick(4 * hb, D)]
    specs += [once((8, hb, 512))] * ((nb == 2) + (nb if adds else 0))
    return pl.pallas_call(
        functools.partial(expert_kernel, nb, adds),
        grid_spec=pltpu.PrefetchScalarGridSpec(
            num_scalar_prefetch=1,
            grid=(1,),
            in_specs=specs,
            out_specs=[pick(SLOTS, WIDE)] + [once((8, hb, 512))] * nb,
            scratch_shapes=[pltpu.VMEM((SLOTS, FF), BF16), pltpu.VMEM((SLOTS, FF), BF16)],
        ),
        out_shape=[jax.ShapeDtypeStruct((E, SLOTS, WIDE), BF16)] + [jax.ShapeDtypeStruct((8, hb, 512), BF16)] * nb,
        input_output_aliases={1: 0},
        compiler_params=params("arbitrary"),
        name="expert",
    )(ids, *ins)


def norm_back(grad, n, rs, gain):
    u = grad * gain
    return rs * (u - jnp.mean(u, axis=-1, keepdims=True) - n * jnp.mean(u * n, axis=-1, keepdims=True))


def back_kernel(
    starts, ys_ref, slot_ref, middle_ref, img_ref, cot_ref, rp_ref, mixed_ref, qkv_ref, lse_ref, ln_ref, qkvw_ref, outw_ref, rw_ref,
    layer_ref, ingrad_ref, gqkv_ref, gout_ref, gmisc_ref,
    xb, gb, rhs, oh, comb, qg, lnacc,
):
    b = pl.program_id(0)

    @pl.when(b == 0)
    def _():
        xb[...] = jnp.zeros_like(xb)
        gb[...] = jnp.zeros_like(gb)
        gqkv_ref[...] = jnp.zeros_like(gqkv_ref)
        gout_ref[...] = jnp.zeros_like(gout_ref)
        gmisc_ref[...] = jnp.zeros_like(gmisc_ref)
        lnacc[...] = jnp.zeros_like(lnacc)

    firsts, needs, passes = windows(starts, b)
    lane = lanes((ROWS, 128))
    comb[...] = jnp.zeros_like(comb)

    def one_pass(p, carry):
        for e in range(E):
            begin = firsts[e] + p * WIN
            off = pl.multiple_of(jnp.minimum(begin, SLOTS - WIN), 16)
            rhs[WIN * e : WIN * e + WIN, :] = ys_ref[e, pl.ds(off, WIN), :]
            named = slot_ref[0, :, e : e + 1]
            ok = (named >= begin) & (named < begin + WIN)
            hit = jnp.where(ok, named - off, -1) == lane
            oh[:, WIN * e : WIN * e + WIN] = hit.astype(F32).astype(BF16)
        comb[...] += dot(oh[...], rhs[...])
        return carry

    lax.fori_loop(0, passes, one_pass, 0)

    middle = middle_ref[0]
    layer_ref[0] = (middle + comb[:, 0:D])[0:SEQ, :].astype(BF16)
    pg = comb[:, 2 * D : WIDE]
    rp = rp_ref[0]
    pg = jnp.where(lane < E, pg + pltpu.roll(pg, 128 - E, 1), 0.0)
    lg = (rp * (pg - jnp.sum(rp * pg, axis=-1, keepdims=True))).astype(BF16)
    n2, rs2 = norm_stats(middle)
    g2 = ln_ref[2:3, :]
    hidden = (n2 * g2 + ln_ref[3:4, :]).astype(BF16)
    gmisc_ref[...] += dot_tn(hidden, lg)
    hg = comb[:, D : 2 * D] + dot_nt(lg, rw_ref[...])
    gb[0:SEQ, :] = cot_ref[0].astype(F32)
    lnacc[10:11, :] += jnp.sum(hg * n2, axis=0, keepdims=True)
    lnacc[11:12, :] += jnp.sum(hg, axis=0, keepdims=True)
    mid_grad = gb[...] + norm_back(hg, n2, rs2, g2)
    bg = mid_grad.astype(BF16)
    gout_ref[...] += dot_tn(mixed_ref[0], bg)
    mg = dot_nt(bg, outw_ref[...]).astype(BF16)
    zero = jnp.zeros((ROWS, 128), BF16)
    keys = subs((ROWS, ROWS))
    for pair in range(HEADS // 2):
        lo = 128 * pair
        q = qkv_ref[0, :, lo : lo + 128]
        k = qkv_ref[0, :, D + lo : D + lo + 128]
        v = qkv_ref[0, :, 2 * D + lo : 2 * D + lo + 128]
        m = mg[:, lo : lo + 128]
        dq = dk = dv = None
        for half in range(2):
            mine = head_lane(half)
            kh = jnp.where(mine, k, zero)
            h = 2 * pair + half
            st = dot_nt(kh, q) * SCALE
            pt = jnp.where(keys < SEQ, jnp.exp(st - lse_ref[0, h : h + 1, :]), 0.0)
            dp = dot_nt(jnp.where(mine, v, zero), m)
            delta = jnp.sum(pt * dp, axis=0, keepdims=True)
            ds = (pt * (dp - delta)).astype(BF16)
            a = dot(pt.astype(BF16), jnp.where(mine, m, zero))
            c = dot(ds, jnp.where(mine, q, zero))
            d = dot_tn(ds, kh)
            dv = a if dv is None else dv + a
            dk = c if dk is None else dk + c
            dq = d if dq is None else dq + d
        qg[:, lo : lo + 128] = (dq * SCALE).astype(BF16)
        qg[:, D + lo : D + lo + 128] = (dk * SCALE).astype(BF16)
        qg[:, 2 * D + lo : 2 * D + lo + 128] = dv.astype(BF16)
    xb[0:SEQ, :] = img_ref[0].astype(F32)
    n1, rs1 = norm_stats(xb[...])
    g1 = ln_ref[0:1, :]
    normed = (n1 * g1 + ln_ref[1:2, :]).astype(BF16)
    gqkv_ref[...] += dot_tn(normed, qg[...])
    ng = dot_nt(qg[...], qkvw_ref[...])
    lnacc[8:9, :] += jnp.sum(ng * n1, axis=0, keepdims=True)
    lnacc[9:10, :] += jnp.sum(ng, axis=0, keepdims=True)
    ingrad_ref[0] = (mid_grad + norm_back(ng, n1, rs1, g1))[0:SEQ, :].astype(BF16)

    @pl.when(b == pl.num_programs(0) - 1)
    def _():
        gmisc_ref[...] += jnp.transpose(lnacc[...])


def back(starts, ys, slot, middle, images, cot, rp, mixed, qkv, lse, ln, qkvw, outw, rw):
    n = images.shape[0]
    whole = lambda shape: pl.BlockSpec(shape, lambda b, s: (0,) * len(shape), pipeline_mode=pl.Buffered(1))
    item = lambda *shape: pl.BlockSpec((1,) + shape, lambda b, s: (b,) + (0,) * len(shape))
    return pl.pallas_call(
        back_kernel,
        grid_spec=pltpu.PrefetchScalarGridSpec(
            num_scalar_prefetch=1,
            grid=(n,),
            in_specs=[
                whole((E, SLOTS, WIDE)), item(ROWS, 128), item(ROWS, D), item(SEQ, D), item(SEQ, D), item(ROWS, AUX), item(ROWS, D),
                item(ROWS, 3 * D), item(HEADS, ROWS), whole((8, D)), whole((D, 3 * D)), whole((D, D)), whole((D, AUX)),
            ],
            out_specs=[item(SEQ, D), item(SEQ, D), whole((D, 3 * D)), whole((D, D)), whole((D, AUX))],
            scratch_shapes=[
                pltpu.VMEM((ROWS, D), F32), pltpu.VMEM((ROWS, D), F32), pltpu.VMEM((E * WIN, WIDE), BF16),
                pltpu.VMEM((ROWS, E * WIN), BF16), pltpu.VMEM((ROWS, WIDE), F32), pltpu.VMEM((ROWS, 3 * D), BF16),
                pltpu.VMEM((AUX, D), F32),
            ],
        ),
        out_shape=(
            jax.ShapeDtypeStruct(images.shape, BF16),
            jax.ShapeDtypeStruct(images.shape, BF16),
            jax.ShapeDtypeStruct((D, 3 * D), F32),
            jax.ShapeDtypeStruct((D, D), F32),
            jax.ShapeDtypeStruct((D, AUX), F32),
        ),
        compiler_params=params("arbitrary"),
        name="back",
    )(starts, ys, slot, middle, images, cot, rp, mixed, qkv, lse, ln, qkvw, outw, rw)


def place_kernel(ids, a_ref, b_ref, in_old, out_old, in_ref, out_ref):
    hb = in_ref.shape[1]

    def put(ref):
        for q in range(4):
            in_ref[0, :, 512 * q : 512 * q + 512] = ref[q].astype(F32)
            out_ref[0, hb * q : hb * q + hb, :] = ref[4 + q].astype(F32)

    @pl.when(pl.program_id(0) == 0)
    def _():
        put(a_ref)

    @pl.when(pl.program_id(0) == 1)
    def _():
        put(b_ref)


def place(ids, a, b, gin, gout):
    hb = a.shape[1]
    once = pl.BlockSpec((8, hb, 512), lambda i, s: (0, 0, 0))
    keep = pl.BlockSpec(memory_space=pl.ANY)
    fresh = gin is None
    args = (a, b) if fresh else (a, b, gin, gout)

    def kernel(*refs):
        if fresh:
            place_kernel(refs[0], refs[1], refs[2], None, None, *refs[3:])
        else:
            place_kernel(*refs)

    return pl.pallas_call(
        kernel,
        grid_spec=pltpu.PrefetchScalarGridSpec(
            num_scalar_prefetch=1,
            grid=(2,),
            in_specs=[once, once] + ([] if fresh else [keep, keep]),
            out_specs=[
                pl.BlockSpec((1, hb, FF), lambda i, s: (s[i], 0, 0)),
                pl.BlockSpec((1, 4 * hb, D), lambda i, s: (s[i], 0, 0)),
            ],
        ),
        out_shape=[jax.ShapeDtypeStruct((E, hb, FF), F32), jax.ShapeDtypeStruct((E, 4 * hb, D), F32)],
        input_output_aliases={} if fresh else {3: 0, 4: 1},
        compiler_params=params("arbitrary"),
        name="place",
    )(ids, *args)


def swap(value, axis, size, bit):
    return lax.ppermute(value, axis, [(i, i ^ (1 << bit)) for i in range(size)])


def halves(value, flag, axis):
    size = value.shape[axis] // 2
    mine = lax.dynamic_slice_in_dim(value, flag * size, size, axis)
    other = lax.dynamic_slice_in_dim(value, (1 - flag) * size, size, axis)
    return mine, other


def joined(mine, other, flag, axis):
    return jnp.where(flag == 0, jnp.concatenate([mine, other], axis), jnp.concatenate([other, mine], axis))


def add(a, b):
    return (a.astype(F32) + b.astype(F32)).astype(BF16)


def pack(win, wout):
    hb = win.shape[0]
    return jnp.concatenate([jnp.transpose(win.reshape(hb, 4, 512), (1, 0, 2)), wout.reshape(4, hb, 512)], axis=0)


def per_device(
    reps, groups, images, ln1_gain, ln1_bias, qkv_weight, out_weight, ln2_gain, ln2_bias, router_weight, expert_in, expert_out, routes, cotangent
):
    rep = lax.axis_index("rep")
    grp = lax.axis_index("grp")
    bits = reps.bit_length() - 1
    rbit = [(rep >> i) & 1 for i in range(bits)]
    core = rbit[0]
    rswap = lambda value, bit: swap(value, "rep", reps, bit)
    pairs = groups == 2
    hb = expert_in.shape[1]

    width = ln1_gain.shape[0]
    small = jnp.concatenate(
        [jnp.stack([ln1_gain, ln1_bias, ln2_gain, ln2_bias]), jnp.transpose(router_weight), jnp.zeros((4, width), BF16)], axis=0
    )
    dense = jnp.concatenate([qkv_weight, out_weight], axis=1)
    if pairs:
        small = joined(small, swap(small, "grp", 2, 0), grp, 1)
        dense = joined(dense, swap(dense, "grp", 2, 0), grp, 0)
    else:
        small = lax.all_gather(small, "grp", axis=1, tiled=True)
        dense = lax.all_gather(dense, "grp", axis=0, tiled=True)
    ln = jnp.concatenate([small[0:4].astype(F32), jnp.zeros((4, D), F32)], axis=0)
    rw = jnp.pad(jnp.transpose(small[4 : 4 + E]), ((0, 0), (0, AUX - E)))
    qkvw = dense[:, : 3 * D]
    outw = dense[:, 3 * D :]

    chunks = E // 2
    first_ids = [j + chunks * core for j in range(chunks)]
    other_ids = [j + chunks * (1 - core) for j in range(chunks)]
    spread = [bit for bit in (1, 2) if bit < bits]
    mine_w, sib_w = [], []
    if pairs:
        for j in range(chunks):
            win = lax.dynamic_slice_in_dim(expert_in, first_ids[j], 1, 0)[0]
            wout = lax.dynamic_slice_in_dim(expert_out, first_ids[j], 1, 0)[0].reshape(4, hb, D)
            order = spread if j % 2 == 0 else spread[::-1]
            at = 0
            size = hb
            for bit in order:
                size = size // 2
                at = at + rbit[bit] * size
            win = lax.dynamic_slice_in_dim(win, at, size, 0)
            wout = lax.dynamic_slice_in_dim(wout, at, size, 1)
            piece = jnp.concatenate([jnp.transpose(win.reshape(size, 4, 512), (1, 0, 2)), wout], axis=0)
            piece = swap(piece, "grp", 2, 0)
            for bit in order[::-1]:
                piece = joined(piece, rswap(piece, bit), rbit[bit], 1)
            mine_w.append(piece)
            sib_w.append(rswap(piece, 0))
        win0, wout0 = expert_in, expert_out
    else:
        win0 = lax.all_gather(expert_in, "grp", axis=1, tiled=True)
        wout0 = lax.all_gather(expert_out, "grp", axis=1, tiled=True)
        mine_w = sib_w = [None] * chunks

    slot, slot_t, starts = route_tables(routes)
    qkv, mixed, middle, rp, lse, hmax, slots = front(starts, images, cotangent, slot_t, ln, qkvw, outw, rw)

    head_max = hmax
    for bit in range(bits):
        head_max = jnp.maximum(head_max, rswap(head_max, bit))
    for bit in range(groups.bit_length() - 1):
        head_max = jnp.maximum(head_max, swap(head_max, "grp", groups, bit))
    clip = jnp.sqrt(CLIP_LIMIT / jnp.maximum(head_max[0, :HEADS], CLIP_LIMIT))
    column_scale = jnp.tile(jnp.repeat(clip, HEAD_DIM), 2)
    clipped = qkv_weight[:, : 2 * D].astype(F32) * column_scale[None, :]

    reduced = []
    sent = [None] * chunks
    order = []
    for j in range(chunks):
        order.append((0, j))
        if j > 0:
            order.append((1, j - 1))
    order.append((1, chunks - 1))
    for own, j in order:
        if own == 0:
            ids = jnp.stack([other_ids[j], grp]).astype(I32)
            slots, *grads = expert_call(ids, slots, win0, wout0, sib_w[j], None)
            sent[j] = [rswap(g, 0) for g in grads]
        else:
            ids = jnp.stack([first_ids[j], grp]).astype(I32)
            slots, *grads = expert_call(ids, slots, win0, wout0, mine_w[j], sent[j])
            if pairs:
                total = (grads[0], swap(grads[1], "grp", 2, 0))
            else:
                full = grads[0]
                gin = lax.psum_scatter(jnp.transpose(full[0:4], (1, 0, 2)).reshape(D, FF), "grp", scatter_dimension=0, tiled=True)
                gout = lax.psum_scatter(full[4:8].reshape(FF, D), "grp", scatter_dimension=0, tiled=True)
                part = pack(gin, gout)
                total = (part, jnp.zeros_like(part))
            reduced.append(total)
    layer_out, input_grad, gqkv, gout, gmisc = back(starts, slots, slot, middle, images, cotangent, rp, mixed, qkv, lse, ln, qkvw, outw, rw)

    steps = list(range(1, bits))
    gin_all = gout_all = None
    for j in range(chunks):
        keep, recv = reduced[j]
        for bit in steps:
            keep_mine, keep_other = halves(keep, rbit[bit], 1)
            recv_mine, recv_other = halves(recv, rbit[bit], 1)
            send = add(keep_other, recv_other)
            keep = add(keep_mine, recv_mine)
            recv = rswap(send, bit)
        done = add(keep, recv)
        for bit in steps[::-1]:
            done = joined(done, rswap(done, bit), rbit[bit], 1)
        twin = rswap(done, 0)
        ids = jnp.stack([first_ids[j], other_ids[j]]).astype(I32)
        gin_all, gout_all = place(ids, done, twin, gin_all, gout_all)

    acc = jnp.concatenate([gqkv, gout, gmisc], axis=1).astype(BF16)
    acc = acc.reshape(groups, D // groups, -1)
    keep, send = halves(acc, core, 1)
    acc = add(keep, rswap(send, 0))
    if pairs:
        keep = lax.dynamic_slice_in_dim(acc, grp, 1, 0)[0]
        send = lax.dynamic_slice_in_dim(acc, 1 - grp, 1, 0)[0]
        acc = add(keep, swap(send, "grp", 2, 0))
    else:
        acc = lax.psum_scatter(acc, "grp", scatter_dimension=0, tiled=True)[0]
    for bit in steps:
        keep, send = halves(acc, rbit[bit], 0)
        acc = add(keep, rswap(send, bit))
    for bit in steps[::-1] + [0]:
        acc = joined(acc, rswap(acc, bit), rbit[bit], 0)
    acc = acc.astype(F32)
    misc = acc[:, 4 * D :]
    return (
        layer_out, input_grad, clipped, misc[:, 8], misc[:, 9], acc[:, : 3 * D], acc[:, 3 * D : 4 * D], misc[:, 10], misc[:, 11],
        misc[:, :E], gin_all, gout_all,
    )


def solution(mesh):
    rows = P(("rep", "grp"), None, None)
    line = P("grp")
    table = P("grp", None)
    cube = P(None, "grp", None)
    in_specs = (rows, line, line, table, table, line, line, table, cube, cube, rows, rows)
    out_specs = (rows, rows, table, line, line, table, table, line, line, table, cube, cube)
    body = functools.partial(per_device, mesh.shape["rep"], mesh.shape["grp"])
    return jax.shard_map(body, mesh=mesh, in_specs=in_specs, out_specs=out_specs, check_vma=False)
```

```python
import functools
import math

import jax
import jax.numpy as jnp
from jax import lax
from jax.experimental import pallas as pl
from jax.experimental.pallas import tpu as pltpu
from jax.sharding import PartitionSpec as P

D = 512
HEADS = 8
HEAD_DIM = 64
FF = 2048
E = 8
TOP = 2
SEQ = 197
CAP = 591
ROWS = 208
SLOTS = 640
WIN = 128
AUX = 128
WIDE = 2 * D + AUX
NORM_EPS = 1e-06
CLIP_LIMIT = 3.0
SCALE = HEAD_DIM ** (-0.5)
LOW = -1e30
F32 = jnp.float32
BF16 = jnp.bfloat16
I32 = jnp.int32


def dot(a, b):
    return lax.dot_general(a, b, (((1,), (0,)), ((), ())), preferred_element_type=F32)


def dot_nt(a, b):
    return lax.dot_general(a, b, (((1,), (1,)), ((), ())), preferred_element_type=F32)


def dot_tn(a, b):
    return lax.dot_general(a, b, (((0,), (0,)), ((), ())), preferred_element_type=F32)


def params(*semantics):
    return pltpu.CompilerParams(dimension_semantics=semantics, vmem_limit_bytes=60 * 1024 * 1024)


def tiny():
    return pl.CostEstimate(flops=1, transcendentals=0, bytes_accessed=1)


def lanes(shape):
    return lax.broadcasted_iota(I32, shape, len(shape) - 1)


def subs(shape):
    return lax.broadcasted_iota(I32, shape, len(shape) - 2)


def route_kernel(routes_ref, slot_ref, slot_t_ref, starts_ref, work):
    images = routes_ref.shape[0]
    lane = lanes((ROWS, 128))
    strict = (lanes((ROWS, ROWS)) < subs((ROWS, ROWS))).astype(BF16)
    work[...] = jnp.full_like(work, -100)
    hots = []
    befores = []
    run = jnp.zeros((1, 128), F32)
    for b in range(images):
        work[0:SEQ, 0:TOP] = routes_ref[b]
        both = work[...]
        hot = ((both[:, 0:1] == lane) & (lane < E)) | (both[:, 1:2] + E == lane) & (lane >= E) & (lane < 2 * E)
        hot = hot.astype(F32)
        hots.append(hot)
        befores.append(dot(strict, hot.astype(BF16)) + run)
        run = run + jnp.sum(hot, axis=0, keepdims=True)
    first = jnp.where(lanes((1, 128)) < E, run, 0.0)
    shift = pltpu.roll(first, E, 1)
    base = jnp.zeros((1, 128), F32)
    starts = jnp.zeros((16, 128), F32)
    row = subs((16, 128))
    for b in range(images):
        kept = jnp.where(befores[b] + shift < CAP, hots[b], 0.0)
        kept = kept + pltpu.roll(kept, 128 - E, 1)
        kept = jnp.where(lane < E, kept, 0.0)
        place = dot(strict, kept.astype(BF16)) + base
        slot = jnp.where(kept > 0.0, place, -1000.0)
        slot_ref[b] = slot.astype(I32)
        slot_t_ref[b] = jnp.transpose(slot)[0:E, :].astype(I32)
        starts = jnp.where(row == b, base, starts)
        base = base + jnp.sum(kept, axis=0, keepdims=True)
    starts_ref[...] = jnp.where(row == images, base, starts).astype(I32)


def route_tables(routes):
    images = routes.shape[0]
    return pl.pallas_call(
        route_kernel,
        out_shape=(
            jax.ShapeDtypeStruct((images, ROWS, 128), I32),
            jax.ShapeDtypeStruct((images, E, ROWS), I32),
            jax.ShapeDtypeStruct((16, 128), I32),
        ),
        scratch_shapes=[pltpu.VMEM((ROWS, 128), I32)],
        compiler_params=params(),
        cost_estimate=tiny(),
        name="routing",
    )(routes)


def windows(starts, b):
    firsts, needs = [], []
    passes = jnp.int32(0)
    for e in range(E):
        start = starts[b, e]
        first = (start // 16) * 16
        need = starts[b + 1, e] - first
        firsts.append(first)
        needs.append(need)
        passes = jnp.maximum(passes, (need + WIN - 1) // WIN)
    return firsts, needs, passes


def norm_stats(rows):
    center = jnp.mean(rows, axis=-1, keepdims=True)
    spread = rows - center
    rs = lax.rsqrt(jnp.mean(spread * spread, axis=-1, keepdims=True) + NORM_EPS)
    return spread * rs, rs


def head_lane(half):
    lane = lanes((ROWS, 128))
    return (lane < HEAD_DIM) if half == 0 else (lane >= HEAD_DIM)


def front_kernel(
    starts, img_ref, cot_ref, slot_t_ref, ln_ref, qkvw_ref, outw_ref, rw_ref,
    qkv_ref, mixed_ref, middle_ref, rp_ref, lse_ref, hmax_ref, slots_ref,
    xb, rhs, oh,
):
    b = pl.program_id(0)

    @pl.when(b == 0)
    def _():
        xb[...] = jnp.zeros_like(xb)
        rhs[...] = jnp.zeros_like(rhs)
        slots_ref[...] = jnp.zeros_like(slots_ref)
        hmax_ref[...] = jnp.full_like(hmax_ref, LOW)

    xb[0:SEQ, :] = img_ref[0].astype(F32)
    x = xb[...]
    n1, _ = norm_stats(x)
    normed = (n1 * ln_ref[0:1, :] + ln_ref[1:2, :]).astype(BF16)
    qkv = dot(normed, qkvw_ref[...]).astype(BF16)
    qkv_ref[0] = qkv
    zero = jnp.zeros((ROWS, 128), BF16)
    cols = lanes((ROWS, ROWS))
    real = subs((ROWS, 1)) < SEQ
    lane = lanes((ROWS, 128))
    lse_all = jnp.zeros((ROWS, 128), F32)
    peaks = jnp.full((ROWS, 128), LOW, F32)
    parts = []
    for pair in range(HEADS // 2):
        q = qkv[:, 128 * pair : 128 * pair + 128]
        k = qkv[:, D + 128 * pair : D + 128 * pair + 128]
        v = qkv[:, 2 * D + 128 * pair : 2 * D + 128 * pair + 128]
        total = None
        for half in range(2):
            mine = head_lane(half)
            s = dot_nt(q, jnp.where(mine, k, zero)) * SCALE
            s = jnp.where(cols < SEQ, s, LOW)
            top = jnp.max(s, axis=-1, keepdims=True)
            powers = jnp.exp(s - top)
            norm = jnp.sum(powers, axis=-1, keepdims=True)
            probs = (powers / norm).astype(BF16)
            part = dot(probs, jnp.where(mine, v, zero))
            total = part if total is None else total + part
            h = 2 * pair + half
            lse_all = jnp.where(lane == h, top + jnp.log(norm), lse_all)
            peaks = jnp.where((lane == h) & real, top, peaks)
        parts.append(total.astype(BF16))
    mixed = jnp.concatenate(parts, axis=1)
    mixed_ref[0] = mixed
    lse_ref[0] = jnp.transpose(lse_all)[0:HEADS, :]
    hmax_ref[...] = jnp.maximum(hmax_ref[...], jnp.max(peaks, axis=0, keepdims=True))
    middle = x + dot(mixed, outw_ref[...])
    middle_ref[0] = middle
    n2, _ = norm_stats(middle)
    hidden = (n2 * ln_ref[2:3, :] + ln_ref[3:4, :]).astype(BF16)
    logits = jnp.where(lane < E, dot(hidden, rw_ref[...]), LOW)
    powers = jnp.exp(logits - jnp.max(logits, axis=-1, keepdims=True))
    rp = powers / jnp.sum(powers, axis=-1, keepdims=True)
    rp_ref[0] = rp
    high = rp.astype(BF16).astype(F32)
    rhs[:, 0:D] = hidden
    rhs[0:SEQ, D : 2 * D] = cot_ref[0]
    rhs[:, 2 * D : WIDE] = (high + pltpu.roll(rp - high, E, 1)).astype(BF16)

    firsts, needs, passes = windows(starts, b)
    place = subs((WIN, ROWS))

    def one_pass(p, carry):
        offs = []
        for e in range(E):
            begin = firsts[e] + p * WIN
            off = pl.multiple_of(jnp.minimum(begin, SLOTS - WIN), 16)
            offs.append(off)
            named = slot_t_ref[0, e : e + 1, :]
            ok = (named >= begin) & (named < begin + WIN)
            hit = jnp.where(ok, named - off, -1) == place
            oh[WIN * e : WIN * e + WIN, :] = hit.astype(F32).astype(BF16)
        picked = dot(oh[...], rhs[...]).astype(BF16)
        for e in range(E):

            @pl.when(p * WIN < needs[e])
            def _():
                slots_ref[e, pl.ds(offs[e], WIN), :] += picked[WIN * e : WIN * e + WIN, :]

        return carry

    lax.fori_loop(0, passes, one_pass, 0)


def front(starts, images, cot, slot_t, ln, qkvw, outw, rw):
    n = images.shape[0]
    whole = lambda shape: pl.BlockSpec(shape, lambda b, s: (0,) * len(shape), pipeline_mode=pl.Buffered(1))
    item = lambda *shape: pl.BlockSpec((1,) + shape, lambda b, s: (b,) + (0,) * len(shape))
    return pl.pallas_call(
        front_kernel,
        grid_spec=pltpu.PrefetchScalarGridSpec(
            num_scalar_prefetch=1,
            grid=(n,),
            in_specs=[
                item(SEQ, D), item(SEQ, D), item(E, ROWS), whole((8, D)), whole((D, 3 * D)), whole((D, D)), whole((D, AUX)),
            ],
            out_specs=[
                item(ROWS, 3 * D), item(ROWS, D), item(ROWS, D), item(ROWS, AUX), item(HEADS, ROWS),
                whole((1, 128)), whole((E, SLOTS, WIDE)),
            ],
            scratch_shapes=[
                pltpu.VMEM((ROWS, D), F32), pltpu.VMEM((ROWS, WIDE), BF16), pltpu.VMEM((E * WIN, ROWS), BF16),
            ],
        ),
        out_shape=(
            jax.ShapeDtypeStruct((n, ROWS, 3 * D), BF16),
            jax.ShapeDtypeStruct((n, ROWS, D), BF16),
            jax.ShapeDtypeStruct((n, ROWS, D), F32),
            jax.ShapeDtypeStruct((n, ROWS, AUX), F32),
            jax.ShapeDtypeStruct((n, HEADS, ROWS), F32),
            jax.ShapeDtypeStruct((1, 128), F32),
            jax.ShapeDtypeStruct((E, SLOTS, WIDE), BF16),
        ),
        compiler_params=params("arbitrary"),
        cost_estimate=tiny(),
        name="front",
    )(starts, images, cot, slot_t, ln, qkvw, outw, rw)


def gelu_parts(pre):
    c = math.sqrt(2.0 / math.pi)
    sq = pre * pre
    t = jnp.tanh(c * pre * (1.0 + 0.044715 * sq))
    half = 0.5 * (1.0 + t)
    act = pre * half
    slope = half + 0.5 * pre * (1.0 - t * t) * (c * (1.0 + 3.0 * 0.044715 * sq))
    return act, slope


def expert_kernel(nb, adds, ids, slots_ref, win0_ref, wout0_ref, *refs):
    refs = list(refs)
    other_ref = refs.pop(0) if nb == 2 else None
    sums = refs.pop(0) if adds else None
    out_ref = refs.pop(0)
    grads = [refs.pop(0) for _ in range(nb)] if adds else [refs[0].at[r] for r in range(nb)]
    if not adds:
        refs.pop(0)
    act_s, preg_s = refs
    e = ids[0]
    me = ids[1]
    hb = win0_ref.shape[1]
    spot = [me, 1 - me] if nb == 2 else [0]

    def at(ref, start, size):
        if isinstance(start, int):
            return ref[:, start : start + size]
        return ref[:, pl.ds(pl.multiple_of(start, 128), size)]

    def win(r, q):
        return win0_ref[0, :, 512 * q : 512 * q + 512] if r == 0 else other_ref[q]

    def win_cols(r, start):
        if isinstance(start, int):
            return win0_ref[0, :, start : start + hb]
        if r == 0:
            return win0_ref[0, :, pl.ds(pl.multiple_of(start, 128), hb)]
        return other_ref[start // 512, :, pl.ds(pl.multiple_of(start % 512, 128), hb)]

    def wout(r, q):
        return wout0_ref[0, hb * q : hb * q + hb, :] if r == 0 else other_ref[4 + q]

    view = slots_ref.at[0]
    hid = [at(view, spot[r] * hb, hb) for r in range(nb)]
    got = view[:, D : 2 * D].astype(F32)
    aux = view[:, 2 * D : WIDE].astype(F32)
    lane = lanes((SLOTS, AUX))
    gate = jnp.sum(jnp.where((lane == e) | (lane == e + E), aux, 0.0), axis=-1, keepdims=True)
    resg = (gate * got).astype(BF16)
    for r in range(nb):
        for q in range(4):
            start = spot[r] * (4 * hb) + q * hb
            pre = dot(hid[0], win_cols(0, start))
            for o in range(1, nb):
                pre = pre + dot(hid[o], win_cols(o, start))
            act, slope = gelu_parts(pre)
            actg = dot_nt(resg, wout(r, q))
            if isinstance(start, int):
                act_s[:, start : start + hb] = act.astype(BF16)
                preg_s[:, start : start + hb] = (actg * slope).astype(BF16)
            else:
                act_s[:, pl.ds(pl.multiple_of(start, 128), hb)] = act.astype(BF16)
                preg_s[:, pl.ds(pl.multiple_of(start, 128), hb)] = (actg * slope).astype(BF16)
    res = None
    for r in range(nb):
        for q in range(4):
            part = dot(at(act_s, spot[r] * (4 * hb) + q * hb, hb), wout(r, q))
            res = part if res is None else res + part
    out_ref[0, :, 0:D] = (gate * res).astype(BF16)
    gg = jnp.sum(got * res, axis=-1, keepdims=True)
    high = gg.astype(BF16).astype(F32)
    out_ref[0, :, 2 * D : WIDE] = jnp.where(lane == e, high, jnp.where(lane == e + E, gg - high, 0.0)).astype(BF16)
    for r in range(nb):
        back = None
        for q in range(4):
            part = dot_nt(preg_s[:, 512 * q : 512 * q + 512], win(r, q))
            back = part if back is None else back + part
        if nb == 1:
            out_ref[0, :, D : 2 * D] = back.astype(BF16)
        else:
            out_ref[0, :, pl.ds(pl.multiple_of(D + spot[r] * hb, 128), hb)] = back.astype(BF16)
    for r in range(nb):
        for q in range(4):
            gin = dot_tn(hid[r], preg_s[:, 512 * q : 512 * q + 512])
            gout = dot_tn(at(act_s, spot[r] * (4 * hb) + q * hb, hb), resg)
            if adds:
                gin = gin + sums[r, q].astype(F32)
                gout = gout + sums[r, 4 + q].astype(F32)
            grads[r][q] = gin.astype(BF16)
            grads[r][4 + q] = gout.astype(BF16)


def expert_call(ids, slots, win0, wout0, other, sums):
    nb = 1 if other is None else 2
    hb = win0.shape[1]
    adds = sums is not None
    once = lambda shape: pl.BlockSpec(shape, lambda i, s: (0,) * len(shape))
    ins = [slots, win0, wout0] + ([other] if nb == 2 else []) + ([sums] if adds else [])
    pick = lambda *shape: pl.BlockSpec((1,) + shape, lambda i, s: (s[0],) + (0,) * len(shape))
    specs = [pick(SLOTS, WIDE), pick(hb, FF), pick(4 * hb, D)]
    specs += [once((8, hb, 512))] * (nb == 2) + [once((nb, 8, hb, 512))] * adds
    return pl.pallas_call(
        functools.partial(expert_kernel, nb, adds),
        grid_spec=pltpu.PrefetchScalarGridSpec(
            num_scalar_prefetch=1,
            grid=(1,),
            in_specs=specs,
            out_specs=[pick(SLOTS, WIDE)] + ([once((8, hb, 512))] * nb if adds else [once((nb, 8, hb, 512))]),
            scratch_shapes=[pltpu.VMEM((SLOTS, FF), BF16), pltpu.VMEM((SLOTS, FF), BF16)],
        ),
        out_shape=[jax.ShapeDtypeStruct((E, SLOTS, WIDE), BF16)]
        + ([jax.ShapeDtypeStruct((8, hb, 512), BF16)] * nb if adds else [jax.ShapeDtypeStruct((nb, 8, hb, 512), BF16)]),
        input_output_aliases={1: 0},
        compiler_params=params("arbitrary"),
        cost_estimate=tiny(),
        name="expert",
    )(ids, *ins)


def norm_back(grad, n, rs, gain):
    u = grad * gain
    return rs * (u - jnp.mean(u, axis=-1, keepdims=True) - n * jnp.mean(u * n, axis=-1, keepdims=True))


def back_kernel(
    base, starts, ys_ref, slot_ref, middle_ref, img_ref, cot_ref, rp_ref, mixed_ref, qkv_ref, lse_ref, ln_ref, qkvw_ref, outw_ref, rw_ref,
    layer_ref, ingrad_ref, gqkv_ref, gout_ref, gmisc_ref,
    xb, gb, rhs, oh, comb, qg, lnacc,
):
    b = pl.program_id(0)

    @pl.when(b == 0)
    def _():
        xb[...] = jnp.zeros_like(xb)
        gb[...] = jnp.zeros_like(gb)
        gqkv_ref[...] = jnp.zeros_like(gqkv_ref)
        gout_ref[...] = jnp.zeros_like(gout_ref)
        gmisc_ref[...] = jnp.zeros_like(gmisc_ref)
        lnacc[...] = jnp.zeros_like(lnacc)

    firsts, needs, passes = windows(starts, base + b)
    lane = lanes((ROWS, 128))
    comb[...] = jnp.zeros_like(comb)

    def one_pass(p, carry):
        for e in range(E):
            begin = firsts[e] + p * WIN
            off = pl.multiple_of(jnp.minimum(begin, SLOTS - WIN), 16)
            rhs[WIN * e : WIN * e + WIN, :] = ys_ref[e, pl.ds(off, WIN), :]
            named = slot_ref[0, :, e : e + 1]
            ok = (named >= begin) & (named < begin + WIN)
            hit = jnp.where(ok, named - off, -1) == lane
            oh[:, WIN * e : WIN * e + WIN] = hit.astype(F32).astype(BF16)
        comb[...] += dot(oh[...], rhs[...])
        return carry

    lax.fori_loop(0, passes, one_pass, 0)

    middle = middle_ref[0]
    layer_ref[0] = (middle + comb[:, 0:D])[0:SEQ, :].astype(BF16)
    pg = comb[:, 2 * D : WIDE]
    rp = rp_ref[0]
    pg = jnp.where(lane < E, pg + pltpu.roll(pg, 128 - E, 1), 0.0)
    lg = (rp * (pg - jnp.sum(rp * pg, axis=-1, keepdims=True))).astype(BF16)
    n2, rs2 = norm_stats(middle)
    g2 = ln_ref[2:3, :]
    hidden = (n2 * g2 + ln_ref[3:4, :]).astype(BF16)
    gmisc_ref[...] += dot_tn(hidden, lg)
    hg = comb[:, D : 2 * D] + dot_nt(lg, rw_ref[...])
    gb[0:SEQ, :] = cot_ref[0].astype(F32)
    lnacc[10:11, :] += jnp.sum(hg * n2, axis=0, keepdims=True)
    lnacc[11:12, :] += jnp.sum(hg, axis=0, keepdims=True)
    mid_grad = gb[...] + norm_back(hg, n2, rs2, g2)
    bg = mid_grad.astype(BF16)
    gout_ref[...] += dot_tn(mixed_ref[0], bg)
    mg = dot_nt(bg, outw_ref[...]).astype(BF16)
    zero = jnp.zeros((ROWS, 128), BF16)
    keys = subs((ROWS, ROWS))
    for pair in range(HEADS // 2):
        lo = 128 * pair
        q = qkv_ref[0, :, lo : lo + 128]
        k = qkv_ref[0, :, D + lo : D + lo + 128]
        v = qkv_ref[0, :, 2 * D + lo : 2 * D + lo + 128]
        m = mg[:, lo : lo + 128]
        dq = dk = dv = None
        for half in range(2):
            mine = head_lane(half)
            kh = jnp.where(mine, k, zero)
            h = 2 * pair + half
            st = dot_nt(kh, q) * SCALE
            pt = jnp.where(keys < SEQ, jnp.exp(st - lse_ref[0, h : h + 1, :]), 0.0)
            dp = dot_nt(jnp.where(mine, v, zero), m)
            delta = jnp.sum(pt * dp, axis=0, keepdims=True)
            ds = (pt * (dp - delta)).astype(BF16)
            a = dot(pt.astype(BF16), jnp.where(mine, m, zero))
            c = dot(ds, jnp.where(mine, q, zero))
            d = dot_tn(ds, kh)
            dv = a if dv is None else dv + a
            dk = c if dk is None else dk + c
            dq = d if dq is None else dq + d
        qg[:, lo : lo + 128] = (dq * SCALE).astype(BF16)
        qg[:, D + lo : D + lo + 128] = (dk * SCALE).astype(BF16)
        qg[:, 2 * D + lo : 2 * D + lo + 128] = dv.astype(BF16)
    xb[0:SEQ, :] = img_ref[0].astype(F32)
    n1, rs1 = norm_stats(xb[...])
    g1 = ln_ref[0:1, :]
    normed = (n1 * g1 + ln_ref[1:2, :]).astype(BF16)
    gqkv_ref[...] += dot_tn(normed, qg[...])
    ng = dot_nt(qg[...], qkvw_ref[...])
    lnacc[8:9, :] += jnp.sum(ng * n1, axis=0, keepdims=True)
    lnacc[9:10, :] += jnp.sum(ng, axis=0, keepdims=True)
    ingrad_ref[0] = (mid_grad + norm_back(ng, n1, rs1, g1))[0:SEQ, :].astype(BF16)

    @pl.when(b == pl.num_programs(0) - 1)
    def _():
        gmisc_ref[...] += jnp.transpose(lnacc[...])


def back(base, count, starts, ys, slot, middle, images, cot, rp, mixed, qkv, lse, ln, qkvw, outw, rw, olds):
    whole = lambda shape: pl.BlockSpec(shape, lambda b, s: (0,) * len(shape), pipeline_mode=pl.Buffered(1))
    item = lambda *shape: pl.BlockSpec((1,) + shape, lambda b, s: (base + b,) + (0,) * len(shape))
    olds = list(olds or [])

    def kernel(*refs):
        back_kernel(base, *refs[:14], *refs[14 + len(olds) :])

    return pl.pallas_call(
        kernel,
        grid_spec=pltpu.PrefetchScalarGridSpec(
            num_scalar_prefetch=1,
            grid=(count,),
            in_specs=[
                whole((E, SLOTS, WIDE)), item(ROWS, 128), item(ROWS, D), item(SEQ, D), item(SEQ, D), item(ROWS, AUX), item(ROWS, D),
                item(ROWS, 3 * D), item(HEADS, ROWS), whole((8, D)), whole((D, 3 * D)), whole((D, D)), whole((D, AUX)),
            ] + [pl.BlockSpec(memory_space=pl.ANY)] * len(olds),
            out_specs=[item(SEQ, D), item(SEQ, D), whole((D, 3 * D)), whole((D, D)), whole((D, AUX))],
            scratch_shapes=[
                pltpu.VMEM((ROWS, D), F32), pltpu.VMEM((ROWS, D), F32), pltpu.VMEM((E * WIN, WIDE), BF16),
                pltpu.VMEM((ROWS, E * WIN), BF16), pltpu.VMEM((ROWS, WIDE), F32), pltpu.VMEM((ROWS, 3 * D), BF16),
                pltpu.VMEM((AUX, D), F32),
            ],
        ),
        out_shape=(
            jax.ShapeDtypeStruct(images.shape, BF16),
            jax.ShapeDtypeStruct(images.shape, BF16),
            jax.ShapeDtypeStruct((D, 3 * D), F32),
            jax.ShapeDtypeStruct((D, D), F32),
            jax.ShapeDtypeStruct((D, AUX), F32),
        ),
        input_output_aliases={14: 0, 15: 1} if olds else {},
        compiler_params=params("arbitrary"),
        cost_estimate=tiny(),
        name="back",
    )(starts, ys, slot, middle, images, cot, rp, mixed, qkv, lse, ln, qkvw, outw, rw, *olds)


def place_kernel(ids, a_ref, b_ref, in_old, out_old, in_ref, out_ref):
    hb = in_ref.shape[1]

    def put(ref):
        for q in range(4):
            in_ref[0, :, 512 * q : 512 * q + 512] = ref[q].astype(F32)
            out_ref[0, hb * q : hb * q + hb, :] = ref[4 + q].astype(F32)

    @pl.when(pl.program_id(0) == 0)
    def _():
        put(a_ref)

    @pl.when(pl.program_id(0) == 1)
    def _():
        put(b_ref)


def place(ids, a, b, gin, gout):
    hb = a.shape[1]
    once = pl.BlockSpec((8, hb, 512), lambda i, s: (0, 0, 0))
    keep = pl.BlockSpec(memory_space=pl.ANY)
    fresh = gin is None
    args = (a, b) if fresh else (a, b, gin, gout)

    def kernel(*refs):
        if fresh:
            place_kernel(refs[0], refs[1], refs[2], None, None, *refs[3:])
        else:
            place_kernel(*refs)

    return pl.pallas_call(
        kernel,
        grid_spec=pltpu.PrefetchScalarGridSpec(
            num_scalar_prefetch=1,
            grid=(2,),
            in_specs=[once, once] + ([] if fresh else [keep, keep]),
            out_specs=[
                pl.BlockSpec((1, hb, FF), lambda i, s: (s[i], 0, 0)),
                pl.BlockSpec((1, 4 * hb, D), lambda i, s: (s[i], 0, 0)),
            ],
        ),
        out_shape=[jax.ShapeDtypeStruct((E, hb, FF), F32), jax.ShapeDtypeStruct((E, 4 * hb, D), F32)],
        input_output_aliases={} if fresh else {3: 0, 4: 1},
        compiler_params=params("arbitrary"),
        cost_estimate=tiny(),
        name="place",
    )(ids, *args)


def swap(value, axis, size, bit, name):
    with jax.named_scope(name):
        return lax.ppermute(value, axis, [(i, i ^ (1 << bit)) for i in range(size)])


def halves(value, flag, axis):
    size = value.shape[axis] // 2
    mine = lax.dynamic_slice_in_dim(value, flag * size, size, axis)
    other = lax.dynamic_slice_in_dim(value, (1 - flag) * size, size, axis)
    return mine, other


def joined(mine, other, flag, axis):
    return jnp.where(flag == 0, jnp.concatenate([mine, other], axis), jnp.concatenate([other, mine], axis))


def add(a, b):
    return (a.astype(F32) + b.astype(F32)).astype(BF16)


def pack(win, wout):
    hb = win.shape[0]
    return jnp.concatenate([jnp.transpose(win.reshape(hb, 4, 512), (1, 0, 2)), wout.reshape(4, hb, 512)], axis=0)


class Order:
    def __init__(self):
        self.last = None

    def __call__(self, *values):
        if self.last is None:
            return values
        return lax.optimization_barrier((*values, self.last))[:-1]

    def done(self, value):
        self.last = value
        return value


def per_device(
    reps, groups, images, ln1_gain, ln1_bias, qkv_weight, out_weight, ln2_gain, ln2_bias, router_weight, expert_in, expert_out, routes, cotangent
):
    rep = lax.axis_index("rep")
    grp = lax.axis_index("grp")
    bits = reps.bit_length() - 1
    rbit = [(rep >> i) & 1 for i in range(bits)]
    core = rbit[0]
    rswap = lambda value, bit, name: swap(value, "rep", reps, bit, f"{name}_rep{bit}")
    gswap = lambda value, name: swap(value, "grp", 2, 0, f"{name}_grp")
    pairs = groups == 2
    hb = expert_in.shape[1]
    order = Order()
    chunks = E // 2
    near_ids = [j + chunks * core for j in range(chunks)]
    far_ids = [j + chunks * (1 - core) for j in range(chunks)]
    spread = [bit for bit in (2, 1) if bit < bits]
    ways = [spread if j % 2 == 0 else spread[::-1] for j in range(chunks)]

    def cut(j):
        win = lax.dynamic_slice_in_dim(expert_in, near_ids[j], 1, 0)[0]
        wout = lax.dynamic_slice_in_dim(expert_out, near_ids[j], 1, 0)[0].reshape(4, hb, D)
        at, size = 0, hb
        for bit in ways[j][::-1]:
            size = size // 2
            at = at + rbit[bit] * size
        win = lax.dynamic_slice_in_dim(win, at, size, 0)
        wout = lax.dynamic_slice_in_dim(wout, at, size, 1)
        return jnp.concatenate([jnp.transpose(win.reshape(size, 4, 512), (1, 0, 2)), wout], axis=0)

    weights = [None] * chunks
    step = [0] * chunks

    def weights_out(j):
        if not pairs:
            return
        if step[j] == 0:
            weights[j] = (gswap(order.done(cut(j)), f"weights{j}"), None)
        elif step[j] <= len(spread) + 1:
            mine, other = weights[j]
            if other is not None:
                mine, other = order(mine, other)
                mine = order.done(joined(mine, other, rbit[ways[j][step[j] - 2]], 1))
            if step[j] <= len(spread):
                weights[j] = (mine, rswap(mine, ways[j][step[j] - 1], f"weights{j}"))
            else:
                weights[j] = (mine, rswap(mine, 0, f"weights{j}"))
        step[j] += 1

    weights_out(0)

    width = ln1_gain.shape[0]
    small = jnp.concatenate(
        [jnp.stack([ln1_gain, ln1_bias, ln2_gain, ln2_bias]), jnp.transpose(router_weight), jnp.zeros((4, width), BF16)], axis=0
    )
    dense = jnp.concatenate([qkv_weight, out_weight], axis=1)
    if pairs:
        small_other = gswap(small, "small")
        part = gswap(lax.dynamic_slice_in_dim(dense, core * (hb // 2), hb // 2, 0), "dense")
        for j in range(1, chunks):
            weights_out(j)
        weights_out(0)
        slot, slot_t, starts = route_tables(*order(routes))
        order.done(starts)
        (part,) = order(part)
        other = joined(part, rswap(part, 0, "dense"), core, 0)
        weights_out(0)
        small = joined(small, small_other, grp, 1)
        dense = joined(dense, other, grp, 0)
    else:
        small = lax.all_gather(small, "grp", axis=1, tiled=True)
        dense = lax.all_gather(dense, "grp", axis=0, tiled=True)
        slot, slot_t, starts = route_tables(routes)
    ln = jnp.concatenate([small[0:4].astype(F32), jnp.zeros((4, D), F32)], axis=0)
    rw = jnp.pad(jnp.transpose(small[4 : 4 + E]), ((0, 0), (0, AUX - E)))
    qkvw = dense[:, : 3 * D]
    outw = dense[:, 3 * D :]
    win0, wout0 = expert_in, expert_out
    if not pairs:
        win0 = lax.all_gather(expert_in, "grp", axis=1, tiled=True)
        wout0 = lax.all_gather(expert_out, "grp", axis=1, tiled=True)
        weights = [(None, None)] * chunks

    (ln,) = order(ln)
    qkv, mixed, middle, rp, lse, hmax, slots = front(starts, images, cotangent, slot_t, ln, qkvw, outw, rw)
    order.done(hmax)

    sent = [None] * chunks
    state = [None] * chunks
    peak = [hmax, 0]

    def first(j):
        nonlocal slots
        mine, _ = weights[j]
        ids = jnp.stack([near_ids[j], grp]).astype(I32)
        (held,) = order(slots)
        slots, grads = expert_call(ids, held, win0, wout0, mine, None)
        sent[j] = rswap(order.done(grads), 0, f"grad{j}")

    def second(j):
        nonlocal slots
        _, other = weights[j]
        ids = jnp.stack([far_ids[j], grp]).astype(I32)
        (held,) = order(slots)
        slots, *grads = expert_call(ids, held, win0, wout0, other, sent[j])
        order.done(grads[0])
        if pairs:
            state[j] = (0, grads[0], gswap(grads[1], f"grad{j}"))
        else:
            full = grads[0]
            gin = lax.psum_scatter(jnp.transpose(full[0:4], (1, 0, 2)).reshape(D, FF), "grp", scatter_dimension=0, tiled=True)
            gout = lax.psum_scatter(full[4:8].reshape(FF, D), "grp", scatter_dimension=0, tiled=True)
            part = pack(gin, gout)
            state[j] = (0, part, jnp.zeros_like(part))

    down = list(range(1, bits))
    up = down[::-1] + [0]
    placed = [None, None]

    def more(j):
        at, keep, recv = state[j]
        keep, recv = order(keep, recv)
        n = len(down)
        if at < n:
            bit = down[at]
            keep_mine, keep_other = halves(keep, rbit[bit], 1)
            recv_mine, recv_other = halves(recv, rbit[bit], 1)
            send = order.done(add(keep_other, recv_other))
            state[j] = (at + 1, add(keep_mine, recv_mine), rswap(send, bit, f"grad{j}_down"))
        elif at < n + len(up):
            bit = up[at - n]
            total = add(keep, recv) if at == n else joined(keep, recv, rbit[up[at - n - 1]], 1)
            order.done(total)
            state[j] = (at + 1, total, rswap(total, bit, f"grad{j}_up"))
        else:
            ids = jnp.stack([far_ids[j], near_ids[j]]).astype(I32)
            placed[0], placed[1] = place(ids, keep, recv, placed[0], placed[1])
            order.done(placed[0])

    def peak_more():
        value, at = peak
        (value,) = order(value)
        if at > 0:
            value = order.done(jnp.maximum(*value))
        if at < bits:
            peak[:] = [(value, rswap(value, at, "peak")), at + 1]
        elif at < bits + groups.bit_length() - 1:
            peak[:] = [(value, swap(value, "grp", groups, at - bits, "peak_grp")), at + 1]
        else:
            peak[:] = [value, at]

    for j in range(1, chunks):
        weights_out(j)
    weights_out(0)
    first(0)
    for j in range(1, chunks):
        weights_out(j)
    second(0)
    weights_out(1)
    first(1)
    weights_out(2)
    first(2)
    weights_out(3)
    second(1)
    first(3)
    more(0)
    second(2)
    second(3)
    more(0)
    more(1)

    n = images.shape[0]
    parts = 2
    outs, accs = None, None
    for i in range(parts):
        (held,) = order(slots)
        *outs, gqkv, gout, gmisc = back(
            i * (n // parts), n // parts, starts, held, slot, middle, images, cotangent, rp, mixed, qkv, lse, ln, qkvw, outw, rw, outs
        )
        order.done(gmisc)
        accs = (gqkv, gout, gmisc) if accs is None else tuple(a + b for a, b in zip(accs, (gqkv, gout, gmisc)))
        if i == 0:
            more(0)
            more(1)
            more(2)

    acc = jnp.concatenate(accs, axis=1).astype(BF16)
    acc = acc.reshape(groups, D // groups, -1)
    keep, send = halves(acc, core, 1)
    acc = add(keep, rswap(send, 0, "dense_down"))
    if pairs:
        keep = lax.dynamic_slice_in_dim(acc, grp, 1, 0)[0]
        send = lax.dynamic_slice_in_dim(acc, 1 - grp, 1, 0)[0]
        acc = add(keep, gswap(send, "dense_down"))
    else:
        acc = lax.psum_scatter(acc, "grp", scatter_dimension=0, tiled=True)[0]
    for bit in down:
        keep, send = halves(acc, rbit[bit], 0)
        acc = add(keep, rswap(send, bit, "dense_down"))
    for bit in up:
        acc = joined(acc, rswap(acc, bit, "dense_up"), rbit[bit], 0)
    acc = acc.astype(F32)
    misc = acc[:, 4 * D :]

    while any(state[j][0] <= len(down) + len(up) and state[j] != "end" for j in range(chunks) if state[j] != "end"):
        for j in range(chunks):
            if state[j] == "end":
                continue
            at = state[j][0]
            more(j)
            if at == len(down) + len(up):
                state[j] = "end"

    for _ in range(bits + groups.bit_length()):
        peak_more()
    head_max = peak[0]
    clip = jnp.sqrt(CLIP_LIMIT / jnp.maximum(head_max[0, :HEADS], CLIP_LIMIT))
    column_scale = jnp.tile(jnp.repeat(clip, HEAD_DIM), 2)
    clipped = qkv_weight[:, : 2 * D].astype(F32) * column_scale[None, :]
    return (
        outs[0], outs[1], clipped, misc[:, 8], misc[:, 9], acc[:, : 3 * D], acc[:, 3 * D : 4 * D], misc[:, 10], misc[:, 11],
        misc[:, :E], placed[0], placed[1],
    )


def solution(mesh):
    rows = P(("rep", "grp"), None, None)
    line = P("grp")
    table = P("grp", None)
    cube = P(None, "grp", None)
    in_specs = (rows, line, line, table, table, line, line, table, cube, cube, rows, rows)
    out_specs = (rows, rows, table, line, line, table, table, line, line, table, cube, cube)
    body = functools.partial(per_device, mesh.shape["rep"], mesh.shape["grp"])
    return jax.shard_map(body, mesh=mesh, in_specs=in_specs, out_specs=out_specs, check_vma=False)
```

```python
import functools
import math

import jax
import jax.numpy as jnp
from jax import lax
from jax.experimental import pallas as pl
from jax.experimental.pallas import tpu as pltpu
from jax.sharding import PartitionSpec as P

D = 512
HEADS = 8
HEAD_DIM = 64
FF = 2048
E = 8
TOP = 2
SEQ = 197
CAP = 591
ROWS = 208
SLOTS = 640
WIN = 128
AUX = 128
WIDE = 2 * D + AUX
NORM_EPS = 1e-06
CLIP_LIMIT = 3.0
SCALE = HEAD_DIM ** (-0.5)
LOW = -1e30
F32 = jnp.float32
BF16 = jnp.bfloat16
I32 = jnp.int32


def dot(a, b):
    return lax.dot_general(a, b, (((1,), (0,)), ((), ())), preferred_element_type=F32)


def dot_nt(a, b):
    return lax.dot_general(a, b, (((1,), (1,)), ((), ())), preferred_element_type=F32)


def dot_tn(a, b):
    return lax.dot_general(a, b, (((0,), (0,)), ((), ())), preferred_element_type=F32)


def params(*semantics):
    return pltpu.CompilerParams(dimension_semantics=semantics, vmem_limit_bytes=60 * 1024 * 1024)


def cost(us):
    return pl.CostEstimate(flops=int(us * 5e+08), transcendentals=0, bytes_accessed=1)


def lanes(shape):
    return lax.broadcasted_iota(I32, shape, len(shape) - 1)


def subs(shape):
    return lax.broadcasted_iota(I32, shape, len(shape) - 2)


def route_kernel(routes_ref, slot_ref, slot_t_ref, starts_ref, work):
    images = routes_ref.shape[0]
    lane = lanes((ROWS, 128))
    strict = (lanes((ROWS, ROWS)) < subs((ROWS, ROWS))).astype(BF16)
    work[...] = jnp.full_like(work, -100)
    hots = []
    befores = []
    run = jnp.zeros((1, 128), F32)
    for b in range(images):
        work[0:SEQ, 0:TOP] = routes_ref[b]
        both = work[...]
        hot = ((both[:, 0:1] == lane) & (lane < E)) | (both[:, 1:2] + E == lane) & (lane >= E) & (lane < 2 * E)
        hot = hot.astype(F32)
        hots.append(hot)
        befores.append(dot(strict, hot.astype(BF16)) + run)
        run = run + jnp.sum(hot, axis=0, keepdims=True)
    first = jnp.where(lanes((1, 128)) < E, run, 0.0)
    shift = pltpu.roll(first, E, 1)
    base = jnp.zeros((1, 128), F32)
    starts = jnp.zeros((16, 128), F32)
    row = subs((16, 128))
    for b in range(images):
        kept = jnp.where(befores[b] + shift < CAP, hots[b], 0.0)
        kept = kept + pltpu.roll(kept, 128 - E, 1)
        kept = jnp.where(lane < E, kept, 0.0)
        place = dot(strict, kept.astype(BF16)) + base
        slot = jnp.where(kept > 0.0, place, -1000.0)
        slot_ref[b] = slot.astype(I32)
        slot_t_ref[b] = jnp.transpose(slot)[0:E, :].astype(I32)
        starts = jnp.where(row == b, base, starts)
        base = base + jnp.sum(kept, axis=0, keepdims=True)
    starts_ref[...] = jnp.where(row == images, base, starts).astype(I32)


def route_tables(routes):
    images = routes.shape[0]
    return pl.pallas_call(
        route_kernel,
        out_shape=(
            jax.ShapeDtypeStruct((images, ROWS, 128), I32),
            jax.ShapeDtypeStruct((images, E, ROWS), I32),
            jax.ShapeDtypeStruct((16, 128), I32),
        ),
        scratch_shapes=[pltpu.VMEM((ROWS, 128), I32)],
        compiler_params=params(),
        cost_estimate=cost(4),
        name="routing",
    )(routes)


def windows(starts, b):
    firsts, needs = [], []
    passes = jnp.int32(0)
    for e in range(E):
        start = starts[b, e]
        first = (start // 16) * 16
        need = starts[b + 1, e] - first
        firsts.append(first)
        needs.append(need)
        passes = jnp.maximum(passes, (need + WIN - 1) // WIN)
    return firsts, needs, passes


def norm_stats(rows):
    center = jnp.mean(rows, axis=-1, keepdims=True)
    spread = rows - center
    rs = lax.rsqrt(jnp.mean(spread * spread, axis=-1, keepdims=True) + NORM_EPS)
    return spread * rs, rs


def head_lane(half):
    lane = lanes((ROWS, 128))
    return (lane < HEAD_DIM) if half == 0 else (lane >= HEAD_DIM)


def front_kernel(
    starts, img_ref, cot_ref, slot_t_ref, ln_ref, qkvw_ref, outw_ref, rw_ref,
    qkv_ref, mixed_ref, middle_ref, rp_ref, lse_ref, hmax_ref, slots_ref,
    xb, rhs, oh,
):
    b = pl.program_id(0)

    @pl.when(b == 0)
    def _():
        xb[...] = jnp.zeros_like(xb)
        rhs[...] = jnp.zeros_like(rhs)
        slots_ref[...] = jnp.zeros_like(slots_ref)
        hmax_ref[...] = jnp.full_like(hmax_ref, LOW)

    xb[0:SEQ, :] = img_ref[0].astype(F32)
    x = xb[...]
    n1, _ = norm_stats(x)
    normed = (n1 * ln_ref[0:1, :] + ln_ref[1:2, :]).astype(BF16)
    qkv = dot(normed, qkvw_ref[...]).astype(BF16)
    qkv_ref[0] = qkv
    zero = jnp.zeros((ROWS, 128), BF16)
    cols = lanes((ROWS, ROWS))
    real = subs((ROWS, 1)) < SEQ
    lane = lanes((ROWS, 128))
    lse_all = jnp.zeros((ROWS, 128), F32)
    peaks = jnp.full((ROWS, 128), LOW, F32)
    parts = []
    for pair in range(HEADS // 2):
        q = qkv[:, 128 * pair : 128 * pair + 128]
        k = qkv[:, D + 128 * pair : D + 128 * pair + 128]
        v = qkv[:, 2 * D + 128 * pair : 2 * D + 128 * pair + 128]
        total = None
        for half in range(2):
            mine = head_lane(half)
            s = dot_nt(q, jnp.where(mine, k, zero)) * SCALE
            s = jnp.where(cols < SEQ, s, LOW)
            top = jnp.max(s, axis=-1, keepdims=True)
            powers = jnp.exp(s - top)
            norm = jnp.sum(powers, axis=-1, keepdims=True)
            probs = (powers / norm).astype(BF16)
            part = dot(probs, jnp.where(mine, v, zero))
            total = part if total is None else total + part
            h = 2 * pair + half
            lse_all = jnp.where(lane == h, top + jnp.log(norm), lse_all)
            peaks = jnp.where((lane == h) & real, top, peaks)
        parts.append(total.astype(BF16))
    mixed = jnp.concatenate(parts, axis=1)
    mixed_ref[0] = mixed
    lse_ref[0] = jnp.transpose(lse_all)[0:HEADS, :]
    hmax_ref[...] = jnp.maximum(hmax_ref[...], jnp.max(peaks, axis=0, keepdims=True))
    middle = x + dot(mixed, outw_ref[...])
    middle_ref[0] = middle
    n2, _ = norm_stats(middle)
    hidden = (n2 * ln_ref[2:3, :] + ln_ref[3:4, :]).astype(BF16)
    logits = jnp.where(lane < E, dot(hidden, rw_ref[...]), LOW)
    powers = jnp.exp(logits - jnp.max(logits, axis=-1, keepdims=True))
    rp = powers / jnp.sum(powers, axis=-1, keepdims=True)
    rp_ref[0] = rp
    high = rp.astype(BF16).astype(F32)
    rhs[:, 0:D] = hidden
    rhs[0:SEQ, D : 2 * D] = cot_ref[0]
    rhs[:, 2 * D : WIDE] = (high + pltpu.roll(rp - high, E, 1)).astype(BF16)

    firsts, needs, passes = windows(starts, b)
    place = subs((WIN, ROWS))

    def one_pass(p, carry):
        offs = []
        for e in range(E):
            begin = firsts[e] + p * WIN
            off = pl.multiple_of(jnp.minimum(begin, SLOTS - WIN), 16)
            offs.append(off)
            named = slot_t_ref[0, e : e + 1, :]
            ok = (named >= begin) & (named < begin + WIN)
            hit = jnp.where(ok, named - off, -1) == place
            oh[WIN * e : WIN * e + WIN, :] = hit.astype(F32).astype(BF16)
        picked = dot(oh[...], rhs[...]).astype(BF16)
        for e in range(E):

            @pl.when(p * WIN < needs[e])
            def _():
                slots_ref[e, pl.ds(offs[e], WIN), :] += picked[WIN * e : WIN * e + WIN, :]

        return carry

    lax.fori_loop(0, passes, one_pass, 0)


def front(starts, images, cot, slot_t, ln, qkvw, outw, rw):
    n = images.shape[0]
    whole = lambda shape: pl.BlockSpec(shape, lambda b, s: (0,) * len(shape), pipeline_mode=pl.Buffered(1))
    item = lambda *shape: pl.BlockSpec((1,) + shape, lambda b, s: (b,) + (0,) * len(shape))
    return pl.pallas_call(
        front_kernel,
        grid_spec=pltpu.PrefetchScalarGridSpec(
            num_scalar_prefetch=1,
            grid=(n,),
            in_specs=[
                item(SEQ, D), item(SEQ, D), item(E, ROWS), whole((8, D)), whole((D, 3 * D)), whole((D, D)), whole((D, AUX)),
            ],
            out_specs=[
                item(ROWS, 3 * D), item(ROWS, D), item(ROWS, D), item(ROWS, AUX), item(HEADS, ROWS),
                whole((1, 128)), whole((E, SLOTS, WIDE)),
            ],
            scratch_shapes=[
                pltpu.VMEM((ROWS, D), F32), pltpu.VMEM((ROWS, WIDE), BF16), pltpu.VMEM((E * WIN, ROWS), BF16),
            ],
        ),
        out_shape=(
            jax.ShapeDtypeStruct((n, ROWS, 3 * D), BF16),
            jax.ShapeDtypeStruct((n, ROWS, D), BF16),
            jax.ShapeDtypeStruct((n, ROWS, D), F32),
            jax.ShapeDtypeStruct((n, ROWS, AUX), F32),
            jax.ShapeDtypeStruct((n, HEADS, ROWS), F32),
            jax.ShapeDtypeStruct((1, 128), F32),
            jax.ShapeDtypeStruct((E, SLOTS, WIDE), BF16),
        ),
        compiler_params=params("arbitrary"),
        cost_estimate=cost(40),
        name="front",
    )(starts, images, cot, slot_t, ln, qkvw, outw, rw)


def gelu_parts(pre):
    c = math.sqrt(2.0 / math.pi)
    sq = pre * pre
    t = jnp.tanh(c * pre * (1.0 + 0.044715 * sq))
    half = 0.5 * (1.0 + t)
    act = pre * half
    slope = half + 0.5 * pre * (1.0 - t * t) * (c * (1.0 + 3.0 * 0.044715 * sq))
    return act, slope


def expert_kernel(nb, adds, ids, slots_ref, win0_ref, wout0_ref, *refs):
    refs = list(refs)
    other_ref = refs.pop(0).at[0] if nb == 2 else None
    sums = refs.pop(0).at[0] if adds else None
    out_ref = refs.pop(0)
    grads = [refs.pop(0) for _ in range(nb)] if adds else [refs[0].at[0, r] for r in range(nb)]
    if not adds:
        refs.pop(0)
    act_s, preg_s = refs
    e = ids[0]
    me = ids[1]
    hb = win0_ref.shape[1]
    spot = [me, 1 - me] if nb == 2 else [0]

    def at(ref, start, size):
        if isinstance(start, int):
            return ref[:, start : start + size]
        return ref[:, pl.ds(pl.multiple_of(start, 128), size)]

    def win(r, q):
        return win0_ref[0, :, 512 * q : 512 * q + 512] if r == 0 else other_ref[q]

    def win_cols(r, start):
        if isinstance(start, int):
            return win0_ref[0, :, start : start + hb]
        if r == 0:
            return win0_ref[0, :, pl.ds(pl.multiple_of(start, 128), hb)]
        return other_ref[start // 512, :, pl.ds(pl.multiple_of(start % 512, 128), hb)]

    def wout(r, q):
        return wout0_ref[0, hb * q : hb * q + hb, :] if r == 0 else other_ref[4 + q]

    view = slots_ref.at[0]
    hid = [at(view, spot[r] * hb, hb) for r in range(nb)]
    got = view[:, D : 2 * D].astype(F32)
    aux = view[:, 2 * D : WIDE].astype(F32)
    lane = lanes((SLOTS, AUX))
    gate = jnp.sum(jnp.where((lane == e) | (lane == e + E), aux, 0.0), axis=-1, keepdims=True)
    resg = (gate * got).astype(BF16)
    for r in range(nb):
        for q in range(4):
            start = spot[r] * (4 * hb) + q * hb
            pre = dot(hid[0], win_cols(0, start))
            for o in range(1, nb):
                pre = pre + dot(hid[o], win_cols(o, start))
            act, slope = gelu_parts(pre)
            actg = dot_nt(resg, wout(r, q))
            if isinstance(start, int):
                act_s[:, start : start + hb] = act.astype(BF16)
                preg_s[:, start : start + hb] = (actg * slope).astype(BF16)
            else:
                act_s[:, pl.ds(pl.multiple_of(start, 128), hb)] = act.astype(BF16)
                preg_s[:, pl.ds(pl.multiple_of(start, 128), hb)] = (actg * slope).astype(BF16)
    res = None
    for r in range(nb):
        for q in range(4):
            part = dot(at(act_s, spot[r] * (4 * hb) + q * hb, hb), wout(r, q))
            res = part if res is None else res + part
    out_ref[0, :, 0:D] = (gate * res).astype(BF16)
    gg = jnp.sum(got * res, axis=-1, keepdims=True)
    high = gg.astype(BF16).astype(F32)
    out_ref[0, :, 2 * D : WIDE] = jnp.where(lane == e, high, jnp.where(lane == e + E, gg - high, 0.0)).astype(BF16)
    for r in range(nb):
        back = None
        for q in range(4):
            part = dot_nt(preg_s[:, 512 * q : 512 * q + 512], win(r, q))
            back = part if back is None else back + part
        if nb == 1:
            out_ref[0, :, D : 2 * D] = back.astype(BF16)
        else:
            out_ref[0, :, pl.ds(pl.multiple_of(D + spot[r] * hb, 128), hb)] = back.astype(BF16)
    for r in range(nb):
        for q in range(4):
            gin = dot_tn(hid[r], preg_s[:, 512 * q : 512 * q + 512])
            gout = dot_tn(at(act_s, spot[r] * (4 * hb) + q * hb, hb), resg)
            if adds:
                gin = gin + sums[r, q].astype(F32)
                gout = gout + sums[r, 4 + q].astype(F32)
            grads[r][q] = gin.astype(BF16)
            grads[r][4 + q] = gout.astype(BF16)


def expert_call(ids, slots, win0, wout0, other, sums):
    nb = 1 if other is None else 2
    hb = win0.shape[1]
    adds = sums is not None
    ins = [slots, win0, wout0] + ([other] if nb == 2 else []) + ([sums] if adds else [])
    pick = lambda at, *shape: pl.BlockSpec((1,) + shape, lambda i, s: (s[at],) + (0,) * len(shape))
    specs = [pick(0, SLOTS, WIDE), pick(0, hb, FF), pick(0, 4 * hb, D)]
    specs += [pick(4, 8, hb, 512)] * (nb == 2) + [pick(3, nb, 8, hb, 512)] * adds
    once = pl.BlockSpec((8, hb, 512), lambda i, s: (0, 0, 0))
    return pl.pallas_call(
        functools.partial(expert_kernel, nb, adds),
        grid_spec=pltpu.PrefetchScalarGridSpec(
            num_scalar_prefetch=1,
            grid=(1,),
            in_specs=specs,
            out_specs=[pick(0, SLOTS, WIDE)] + ([once] * nb if adds else [pick(2, nb, 8, hb, 512)]),
            scratch_shapes=[pltpu.VMEM((SLOTS, FF), BF16), pltpu.VMEM((SLOTS, FF), BF16)],
        ),
        out_shape=[jax.ShapeDtypeStruct((E, SLOTS, WIDE), BF16)]
        + ([jax.ShapeDtypeStruct((8, hb, 512), BF16)] * nb if adds else [jax.ShapeDtypeStruct((2, nb, 8, hb, 512), BF16)]),
        input_output_aliases={1: 0},
        compiler_params=params("arbitrary"),
        cost_estimate=cost(17),
        name="expert",
    )(ids, *ins)


def norm_back(grad, n, rs, gain):
    u = grad * gain
    return rs * (u - jnp.mean(u, axis=-1, keepdims=True) - n * jnp.mean(u * n, axis=-1, keepdims=True))


def back_kernel(
    base, starts, ys_ref, slot_ref, middle_ref, img_ref, cot_ref, rp_ref, mixed_ref, qkv_ref, lse_ref, ln_ref, qkvw_ref, outw_ref, rw_ref,
    layer_ref, ingrad_ref, gqkv_ref, gout_ref, gmisc_ref,
    xb, gb, rhs, oh, comb, qg, lnacc,
):
    b = pl.program_id(0)

    @pl.when(b == 0)
    def _():
        xb[...] = jnp.zeros_like(xb)
        gb[...] = jnp.zeros_like(gb)
        gqkv_ref[...] = jnp.zeros_like(gqkv_ref)
        gout_ref[...] = jnp.zeros_like(gout_ref)
        gmisc_ref[...] = jnp.zeros_like(gmisc_ref)
        lnacc[...] = jnp.zeros_like(lnacc)

    firsts, needs, passes = windows(starts, base + b)
    lane = lanes((ROWS, 128))
    comb[...] = jnp.zeros_like(comb)

    def one_pass(p, carry):
        for e in range(E):
            begin = firsts[e] + p * WIN
            off = pl.multiple_of(jnp.minimum(begin, SLOTS - WIN), 16)
            rhs[WIN * e : WIN * e + WIN, :] = ys_ref[e, pl.ds(off, WIN), :]
            named = slot_ref[0, :, e : e + 1]
            ok = (named >= begin) & (named < begin + WIN)
            hit = jnp.where(ok, named - off, -1) == lane
            oh[:, WIN * e : WIN * e + WIN] = hit.astype(F32).astype(BF16)
        comb[...] += dot(oh[...], rhs[...])
        return carry

    lax.fori_loop(0, passes, one_pass, 0)

    middle = middle_ref[0]
    layer_ref[0] = (middle + comb[:, 0:D])[0:SEQ, :].astype(BF16)
    pg = comb[:, 2 * D : WIDE]
    rp = rp_ref[0]
    pg = jnp.where(lane < E, pg + pltpu.roll(pg, 128 - E, 1), 0.0)
    lg = (rp * (pg - jnp.sum(rp * pg, axis=-1, keepdims=True))).astype(BF16)
    n2, rs2 = norm_stats(middle)
    g2 = ln_ref[2:3, :]
    hidden = (n2 * g2 + ln_ref[3:4, :]).astype(BF16)
    gmisc_ref[...] += dot_tn(hidden, lg)
    hg = comb[:, D : 2 * D] + dot_nt(lg, rw_ref[...])
    gb[0:SEQ, :] = cot_ref[0].astype(F32)
    lnacc[10:11, :] += jnp.sum(hg * n2, axis=0, keepdims=True)
    lnacc[11:12, :] += jnp.sum(hg, axis=0, keepdims=True)
    mid_grad = gb[...] + norm_back(hg, n2, rs2, g2)
    bg = mid_grad.astype(BF16)
    gout_ref[...] += dot_tn(mixed_ref[0], bg)
    mg = dot_nt(bg, outw_ref[...]).astype(BF16)
    zero = jnp.zeros((ROWS, 128), BF16)
    keys = subs((ROWS, ROWS))
    for pair in range(HEADS // 2):
        lo = 128 * pair
        q = qkv_ref[0, :, lo : lo + 128]
        k = qkv_ref[0, :, D + lo : D + lo + 128]
        v = qkv_ref[0, :, 2 * D + lo : 2 * D + lo + 128]
        m = mg[:, lo : lo + 128]
        dq = dk = dv = None
        for half in range(2):
            mine = head_lane(half)
            kh = jnp.where(mine, k, zero)
            h = 2 * pair + half
            st = dot_nt(kh, q) * SCALE
            pt = jnp.where(keys < SEQ, jnp.exp(st - lse_ref[0, h : h + 1, :]), 0.0)
            dp = dot_nt(jnp.where(mine, v, zero), m)
            delta = jnp.sum(pt * dp, axis=0, keepdims=True)
            ds = (pt * (dp - delta)).astype(BF16)
            a = dot(pt.astype(BF16), jnp.where(mine, m, zero))
            c = dot(ds, jnp.where(mine, q, zero))
            d = dot_tn(ds, kh)
            dv = a if dv is None else dv + a
            dk = c if dk is None else dk + c
            dq = d if dq is None else dq + d
        qg[:, lo : lo + 128] = (dq * SCALE).astype(BF16)
        qg[:, D + lo : D + lo + 128] = (dk * SCALE).astype(BF16)
        qg[:, 2 * D + lo : 2 * D + lo + 128] = dv.astype(BF16)
    xb[0:SEQ, :] = img_ref[0].astype(F32)
    n1, rs1 = norm_stats(xb[...])
    g1 = ln_ref[0:1, :]
    normed = (n1 * g1 + ln_ref[1:2, :]).astype(BF16)
    gqkv_ref[...] += dot_tn(normed, qg[...])
    ng = dot_nt(qg[...], qkvw_ref[...])
    lnacc[8:9, :] += jnp.sum(ng * n1, axis=0, keepdims=True)
    lnacc[9:10, :] += jnp.sum(ng, axis=0, keepdims=True)
    ingrad_ref[0] = (mid_grad + norm_back(ng, n1, rs1, g1))[0:SEQ, :].astype(BF16)

    @pl.when(b == pl.num_programs(0) - 1)
    def _():
        gmisc_ref[...] += jnp.transpose(lnacc[...])


def back(base, count, starts, ys, slot, middle, images, cot, rp, mixed, qkv, lse, ln, qkvw, outw, rw, olds):
    whole = lambda shape: pl.BlockSpec(shape, lambda b, s: (0,) * len(shape), pipeline_mode=pl.Buffered(1))
    item = lambda *shape: pl.BlockSpec((1,) + shape, lambda b, s: (base + b,) + (0,) * len(shape))
    olds = list(olds or [])

    def kernel(*refs):
        back_kernel(base, *refs[:14], *refs[14 + len(olds) :])

    return pl.pallas_call(
        kernel,
        grid_spec=pltpu.PrefetchScalarGridSpec(
            num_scalar_prefetch=1,
            grid=(count,),
            in_specs=[
                whole((E, SLOTS, WIDE)), item(ROWS, 128), item(ROWS, D), item(SEQ, D), item(SEQ, D), item(ROWS, AUX), item(ROWS, D),
                item(ROWS, 3 * D), item(HEADS, ROWS), whole((8, D)), whole((D, 3 * D)), whole((D, D)), whole((D, AUX)),
            ] + [pl.BlockSpec(memory_space=pl.ANY)] * len(olds),
            out_specs=[item(SEQ, D), item(SEQ, D), whole((D, 3 * D)), whole((D, D)), whole((D, AUX))],
            scratch_shapes=[
                pltpu.VMEM((ROWS, D), F32), pltpu.VMEM((ROWS, D), F32), pltpu.VMEM((E * WIN, WIDE), BF16),
                pltpu.VMEM((ROWS, E * WIN), BF16), pltpu.VMEM((ROWS, WIDE), F32), pltpu.VMEM((ROWS, 3 * D), BF16),
                pltpu.VMEM((AUX, D), F32),
            ],
        ),
        out_shape=(
            jax.ShapeDtypeStruct(images.shape, BF16),
            jax.ShapeDtypeStruct(images.shape, BF16),
            jax.ShapeDtypeStruct((D, 3 * D), F32),
            jax.ShapeDtypeStruct((D, D), F32),
            jax.ShapeDtypeStruct((D, AUX), F32),
        ),
        input_output_aliases={14: 0, 15: 1} if olds else {},
        compiler_params=params("arbitrary"),
        cost_estimate=cost(30),
        name="back",
    )(starts, ys, slot, middle, images, cot, rp, mixed, qkv, lse, ln, qkvw, outw, rw, *olds)


def place_kernel(ids, a_ref, b_ref, in_old, out_old, in_ref, out_ref):
    hb = in_ref.shape[1]

    def put(ref):
        for q in range(4):
            in_ref[0, :, 512 * q : 512 * q + 512] = ref[q].astype(F32)
            out_ref[0, hb * q : hb * q + hb, :] = ref[4 + q].astype(F32)

    @pl.when(pl.program_id(0) == 0)
    def _():
        put(a_ref)

    @pl.when(pl.program_id(0) == 1)
    def _():
        put(b_ref)


def place(ids, a, b, gin, gout):
    hb = a.shape[1]
    once = pl.BlockSpec((8, hb, 512), lambda i, s: (0, 0, 0))
    keep = pl.BlockSpec(memory_space=pl.ANY)
    fresh = gin is None
    args = (a, b) if fresh else (a, b, gin, gout)

    def kernel(*refs):
        if fresh:
            place_kernel(refs[0], refs[1], refs[2], None, None, *refs[3:])
        else:
            place_kernel(*refs)

    return pl.pallas_call(
        kernel,
        grid_spec=pltpu.PrefetchScalarGridSpec(
            num_scalar_prefetch=1,
            grid=(2,),
            in_specs=[once, once] + ([] if fresh else [keep, keep]),
            out_specs=[
                pl.BlockSpec((1, hb, FF), lambda i, s: (s[i], 0, 0)),
                pl.BlockSpec((1, 4 * hb, D), lambda i, s: (s[i], 0, 0)),
            ],
        ),
        out_shape=[jax.ShapeDtypeStruct((E, hb, FF), F32), jax.ShapeDtypeStruct((E, 4 * hb, D), F32)],
        input_output_aliases={} if fresh else {3: 0, 4: 1},
        compiler_params=params("arbitrary"),
        cost_estimate=cost(7),
        name="place",
    )(ids, *args)


def swap(value, axis, size, bit, name):
    with jax.named_scope(name):
        return lax.ppermute(value, axis, [(i, i ^ (1 << bit)) for i in range(size)])


def halves(value, flag, axis):
    size = value.shape[axis] // 2
    mine = lax.dynamic_slice_in_dim(value, flag * size, size, axis)
    other = lax.dynamic_slice_in_dim(value, (1 - flag) * size, size, axis)
    return mine, other


def joined(mine, other, flag, axis):
    return jnp.where(flag == 0, jnp.concatenate([mine, other], axis), jnp.concatenate([other, mine], axis))


def add(a, b):
    return (a.astype(F32) + b.astype(F32)).astype(BF16)


def pack(win, wout):
    hb = win.shape[0]
    return jnp.concatenate([jnp.transpose(win.reshape(hb, 4, 512), (1, 0, 2)), wout.reshape(4, hb, 512)], axis=0)


def cut_kernel(ids, win_ref, wout_ref, out_ref):
    for q in range(4):
        out_ref[q] = win_ref[0, :, 512 * q : 512 * q + 512]
        out_ref[4 + q] = wout_ref[0, q]


def cut(expert, piece, size, win, wout):
    hb = win.shape[1]
    return pl.pallas_call(
        cut_kernel,
        grid_spec=pltpu.PrefetchScalarGridSpec(
            num_scalar_prefetch=1,
            grid=(1,),
            in_specs=[
                pl.BlockSpec((1, size, FF), lambda i, s: (s[0], s[1], 0)),
                pl.BlockSpec((1, 4, size, D), lambda i, s: (s[0], 0, s[1], 0)),
            ],
            out_specs=pl.BlockSpec((8, size, 512), lambda i, s: (0, 0, 0)),
        ),
        out_shape=jax.ShapeDtypeStruct((8, size, 512), BF16),
        compiler_params=params("arbitrary"),
        cost_estimate=cost(2),
        name="cut",
    )(jnp.stack([expert, piece]).astype(I32), win, wout.reshape(E, 4, hb, D))


def gather_kernel(ids, qkv_ref, out_ref, near_ref, far_ref, small_ref, qkvw_ref, outw_ref, ln_ref, rw_ref, work):
    grp = ids[0]
    core = ids[1]
    hb = qkv_ref.shape[0]
    part = hb // 2
    rows = lambda start, size: pl.ds(pl.multiple_of(start, 128), size)
    mine = grp * hb
    other = (1 - grp) * hb
    qkvw_ref[rows(mine, hb), :] = qkv_ref[...]
    outw_ref[rows(mine, hb), :] = out_ref[...]
    for ref, at in ((near_ref, other + core * part), (far_ref, other + (1 - core) * part)):
        qkvw_ref[rows(at, part), :] = ref[:, 0 : 3 * D]
        outw_ref[rows(at, part), :] = ref[:, 3 * D : 4 * D]
    ln_ref[...] = jnp.zeros_like(ln_ref)
    work[...] = jnp.zeros_like(work)
    lane = lanes((hb, AUX))
    for these, at in ((small_ref[...], mine), (near_ref[0:16, 4 * D :], other)):
        work[0:16, :] = these.astype(F32)
        ln_ref[0:4, rows(at, hb)] = work[0:4, :]
        router = pltpu.roll(jnp.transpose(work[...]), AUX - 4, 1)
        rw_ref[rows(at, hb), :] = jnp.where(lane < E, router, 0.0).astype(BF16)


def gathered(ids, qkv_weight, out_weight, near, far, small):
    return pl.pallas_call(
        gather_kernel,
        grid_spec=pltpu.PrefetchScalarGridSpec(
            num_scalar_prefetch=1,
            grid=(1,),
            in_specs=[pl.BlockSpec(a.shape, lambda i, s: (0, 0)) for a in (qkv_weight, out_weight, near, far, small)],
            out_specs=[pl.BlockSpec(shape, lambda i, s: (0, 0)) for shape in ((D, 3 * D), (D, D), (8, D), (D, AUX))],
            scratch_shapes=[pltpu.VMEM((AUX, qkv_weight.shape[0]), F32)],
        ),
        out_shape=[
            jax.ShapeDtypeStruct((D, 3 * D), BF16),
            jax.ShapeDtypeStruct((D, D), BF16),
            jax.ShapeDtypeStruct((8, D), F32),
            jax.ShapeDtypeStruct((D, AUX), BF16),
        ],
        compiler_params=params("arbitrary"),
        cost_estimate=cost(3),
        name="gathered",
    )(ids, qkv_weight, out_weight, near, far, small)


class Order:
    def __init__(self):
        self.last = None

    def __call__(self, *values):
        if self.last is None:
            return values
        return lax.optimization_barrier((*values, self.last))[:-1]

    def done(self, value):
        self.last = value
        return value

    def pass_on(self, value):
        (value,) = self(value)
        return self.done(value)


def per_device(
    reps, groups, images, ln1_gain, ln1_bias, qkv_weight, out_weight, ln2_gain, ln2_bias, router_weight, expert_in, expert_out, routes, cotangent
):
    rep = lax.axis_index("rep")
    grp = lax.axis_index("grp")
    bits = reps.bit_length() - 1
    rbit = [(rep >> i) & 1 for i in range(bits)]
    core = rbit[0]
    rswap = lambda value, bit, name: swap(value, "rep", reps, bit, f"{name}_rep{bit}")
    couples = [[i, i + 1] for i in range(0, reps, 2)]

    def between(value, name):
        with jax.named_scope(f"{name}_cores"):
            return lax.all_to_all(value, "rep", 0, 0, axis_index_groups=couples, tiled=True)

    gswap = lambda value, name: swap(value, "grp", 2, 0, f"{name}_grp")
    pairs = groups == 2
    hb = expert_in.shape[1]
    order = Order()
    chunks = E // 2
    near_ids = [j + chunks * core for j in range(chunks)]
    far_ids = [j + chunks * (1 - core) for j in range(chunks)]
    spread = [bit for bit in (2, 1) if bit < bits]
    ways = [spread if j % 2 == 0 else spread[::-1] for j in range(chunks)]

    def first_cut(j):
        piece, size = 0, hb
        for bit in ways[j][::-1]:
            size = size // 2
            piece = piece * 2 + rbit[bit]
        win, wout = order(expert_in, expert_out)
        return order.done(cut(near_ids[j], piece, size, win, wout))

    weights = [None] * chunks
    step = [0] * chunks

    def weights_out(j):
        if not pairs:
            return
        at = step[j]
        step[j] += 1
        if at == 0:
            weights[j] = (None, gswap(first_cut(j), f"weights{j}"))
            return
        mine, other = weights[j]
        if at == 1:
            mine = order.pass_on(other)
        elif at <= len(spread):
            mine, other = order(mine, other)
            mine = order.done(joined(mine, other, rbit[ways[j][at - 2]], 1))
        if at <= len(spread):
            weights[j] = (mine, rswap(mine, ways[j][at - 1], f"weights{j}"))
        else:
            mine, other = order(mine, other)
            mine = joined(mine, other, rbit[ways[j][at - 2]], 1)
            weights[j] = order.done(between(jnp.stack([mine, mine]), f"weights{j}"))

    peak = [None, 0]
    last_peak = bits + groups.bit_length() - 1
    clipped = None

    def peak_more():
        nonlocal clipped
        value, at = peak
        if at > last_peak + 1:
            return
        if at > 0:
            value = order(*value)
            value = order.done(jnp.maximum(*value))
        if at < bits:
            peak[0] = (value, rswap(value, at, "peak"))
        elif at < last_peak:
            peak[0] = (value, swap(value, "grp", groups, at - bits, "peak_grp"))
        else:
            clip = jnp.sqrt(CLIP_LIMIT / jnp.maximum(value[0, :HEADS], CLIP_LIMIT))
            column_scale = jnp.tile(jnp.repeat(clip, HEAD_DIM), 2)
            clipped = order.done(qkv_weight[:, : 2 * D].astype(F32) * column_scale[None, :])
            peak[1] = last_peak + 2
            return
        peak[1] += 1

    width = ln1_gain.shape[0]
    small = jnp.concatenate(
        [jnp.stack([ln1_gain, ln1_bias, ln2_gain, ln2_bias]), jnp.transpose(router_weight), jnp.zeros((4, width), BF16)], axis=0
    )
    win0, wout0 = expert_in, expert_out
    if pairs:
        weights_out(0)
        dense = [lax.dynamic_slice_in_dim(w, core * (hb // 2), hb // 2, 0) for w in order(qkv_weight, out_weight)]
        dense = jnp.concatenate([*dense, jnp.pad(small, ((0, hb // 2 - 16), (0, 0)))], axis=1)
        near = gswap(order.done(dense), "dense")
        for j in range(1, chunks):
            weights_out(j)
        slot, slot_t, starts = route_tables(*order(routes))
        order.done(starts)
        weights_out(0)
        near = order.pass_on(near)
        far = rswap(near, 0, "dense")
        weights_out(0)
        ids = jnp.stack([grp, core]).astype(I32)
        qkvw, outw, ln, rw = gathered(ids, qkv_weight, out_weight, *order(near, far, small))
        order.done(ln)
    else:
        dense = jnp.concatenate([qkv_weight, out_weight], axis=1)
        small = lax.all_gather(small, "grp", axis=1, tiled=True)
        dense = lax.all_gather(dense, "grp", axis=0, tiled=True)
        slot, slot_t, starts = route_tables(routes)
        ln = jnp.concatenate([small[0:4].astype(F32), jnp.zeros((4, D), F32)], axis=0)
        rw = jnp.pad(jnp.transpose(small[4 : 4 + E]), ((0, 0), (0, AUX - E)))
        qkvw = dense[:, : 3 * D]
        outw = dense[:, 3 * D :]
        win0 = lax.all_gather(expert_in, "grp", axis=1, tiled=True)
        wout0 = lax.all_gather(expert_out, "grp", axis=1, tiled=True)
        weights = [None] * chunks

    (ln,) = order(ln)
    qkv, mixed, middle, rp, lse, hmax, slots = front(starts, images, cotangent, slot_t, ln, qkvw, outw, rw)
    peak[0] = order.done(hmax)

    sent = [None] * chunks
    state = [None] * chunks

    def first(j):
        nonlocal slots
        ids = jnp.stack([near_ids[j], grp, 1 - core, 1 - core, core]).astype(I32)
        (held,) = order(slots)
        slots, grads = expert_call(ids, held, win0, wout0, weights[j], None)
        sent[j] = order.done(between(grads, f"grad{j}"))

    def second(j):
        nonlocal slots
        ids = jnp.stack([far_ids[j], grp, core, 1 - core, 1 - core]).astype(I32)
        (held,) = order(slots)
        slots, *grads = expert_call(ids, held, win0, wout0, weights[j], sent[j])
        order.done(grads[0])
        if pairs:
            state[j] = (0, grads[0], gswap(grads[1], f"grad{j}"))
        else:
            full = grads[0]
            gin = lax.psum_scatter(jnp.transpose(full[0:4], (1, 0, 2)).reshape(D, FF), "grp", scatter_dimension=0, tiled=True)
            gout = lax.psum_scatter(full[4:8].reshape(FF, D), "grp", scatter_dimension=0, tiled=True)
            part = pack(gin, gout)
            state[j] = (0, part, jnp.zeros_like(part))

    down = list(range(1, bits))
    up = down[::-1] + [0]
    placed = [None, None]
    ends = len(down) + len(up)

    def more(j):
        at, keep, recv = state[j]
        if at > ends:
            return
        keep, recv = order(keep, recv)
        n = len(down)
        if at < n:
            bit = down[at]
            keep_mine, keep_other = halves(keep, rbit[bit], 1)
            recv_mine, recv_other = halves(recv, rbit[bit], 1)
            send = add(keep_other, recv_other)
            keep = order.done(add(keep_mine, recv_mine))
            state[j] = (at + 1, keep, rswap(send, bit, f"grad{j}_down"))
        elif at < ends:
            bit = up[at - n]
            total = add(keep, recv) if at == n else joined(keep, recv, rbit[up[at - n - 1]], 1)
            order.done(total)
            state[j] = (at + 1, total, rswap(total, bit, f"grad{j}_up"))
        else:
            ids = jnp.stack([far_ids[j], near_ids[j]]).astype(I32)
            placed[0], placed[1] = place(ids, keep, recv, placed[0], placed[1])
            order.done(placed[0])
            state[j] = (at + 1, None, None)

    weights_out(0)
    for j in range(1, chunks):
        weights_out(j)
    first(0)
    for j in range(1, chunks):
        weights_out(j)
    second(0)
    weights_out(1)
    first(1)
    second(1)
    weights_out(2)
    more(0)
    first(2)
    weights_out(3)
    second(2)
    more(0)
    first(3)
    more(0)
    more(1)
    second(3)
    more(0)
    more(1)

    n = images.shape[0]
    parts = 2
    outs, accs = None, None
    for i in range(parts):
        (held,) = order(slots)
        *outs, gqkv, gout, gmisc = back(
            i * (n // parts), n // parts, starts, held, slot, middle, images, cotangent, rp, mixed, qkv, lse, ln, qkvw, outw, rw, outs
        )
        order.done(gmisc)
        accs = (gqkv, gout, gmisc) if accs is None else tuple(a + b for a, b in zip(accs, (gqkv, gout, gmisc)))
        if i == 0:
            more(0)
            more(1)
            more(2)

    dense_at = [0]
    acc = jnp.concatenate(order(*accs), axis=1).astype(BF16)
    dense_state = [acc.reshape(groups, D // groups, -1), None]
    final = None

    def dense_more():
        nonlocal final
        at = dense_at[0]
        dense_at[0] += 1
        keep, recv = dense_state
        n = len(down)
        if at == 0:
            (keep,) = order(keep)
            mine, send = halves(keep, core, 1)
            order.done(send)
            dense_state[:] = [mine, rswap(send, 0, "dense_down")]
        elif at == 1:
            total = order.done(add(*order(keep, recv)))
            if pairs:
                mine = lax.dynamic_slice_in_dim(total, grp, 1, 0)[0]
                send = lax.dynamic_slice_in_dim(total, 1 - grp, 1, 0)[0]
                dense_state[:] = [mine, gswap(send, "dense_down")]
            else:
                total = lax.psum_scatter(total, "grp", scatter_dimension=0, tiled=True)[0]
                dense_state[:] = [total, jnp.zeros_like(total)]
        elif at < 2 + n:
            total = order.done(add(*order(keep, recv)))
            bit = down[at - 2]
            mine, send = halves(total, rbit[bit], 0)
            dense_state[:] = [mine, rswap(send, bit, "dense_down")]
        elif at < 2 + n + len(up):
            bit = up[at - 2 - n]
            keep, recv = order(keep, recv)
            total = add(keep, recv) if at == 2 + n else joined(keep, recv, rbit[up[at - 3 - n]], 0)
            dense_state[:] = [order.done(total), rswap(total, bit, "dense_up")]
        elif at == 2 + n + len(up):
            total = joined(*order(keep, recv), core, 0).astype(F32)
            misc = total[:, 4 * D :]
            final = (
                misc[:, 8], misc[:, 9], total[:, : 3 * D], total[:, 3 * D : 4 * D], misc[:, 10], misc[:, 11], misc[:, :E],
            )
            order.done(final[2])

    peak_more()
    while any(state[j][0] <= ends for j in range(chunks)) or final is None or clipped is None:
        for j in range(chunks):
            more(j)
        if final is None:
            dense_more()
        peak_more()
    return (outs[0], outs[1], clipped, *final, placed[0], placed[1])


def solution(mesh):
    rows = P(("rep", "grp"), None, None)
    line = P("grp")
    table = P("grp", None)
    cube = P(None, "grp", None)
    in_specs = (rows, line, line, table, table, line, line, table, cube, cube, rows, rows)
    out_specs = (rows, rows, table, line, line, table, table, line, line, table, cube, cube)
    body = functools.partial(per_device, mesh.shape["rep"], mesh.shape["grp"])
    return jax.shard_map(body, mesh=mesh, in_specs=in_specs, out_specs=out_specs, check_vma=False)
```

```python
import functools
import math

import jax
import jax.numpy as jnp
from jax import lax
from jax.experimental import pallas as pl
from jax.experimental.pallas import tpu as pltpu
from jax.sharding import PartitionSpec as P

D = 512
HEADS = 8
HEAD_DIM = 64
FF = 2048
E = 8
TOP = 2
SEQ = 197
CAP = 591
ROWS = 208
SLOTS = 640
WIN = 128
AUX = 128
WIDE = 2 * D + AUX
NORM_EPS = 1e-06
CLIP_LIMIT = 3.0
SCALE = HEAD_DIM ** (-0.5)
LOW = -1e30
F32 = jnp.float32
BF16 = jnp.bfloat16
I32 = jnp.int32


def dot(a, b):
    return lax.dot_general(a, b, (((1,), (0,)), ((), ())), preferred_element_type=F32)


def dot_nt(a, b):
    return lax.dot_general(a, b, (((1,), (1,)), ((), ())), preferred_element_type=F32)


def dot_tn(a, b):
    return lax.dot_general(a, b, (((0,), (0,)), ((), ())), preferred_element_type=F32)


def params(*semantics):
    return pltpu.CompilerParams(dimension_semantics=semantics, vmem_limit_bytes=60 * 1024 * 1024)


def cost(us):
    return pl.CostEstimate(flops=int(us * 6e+08), transcendentals=0, bytes_accessed=1)


def lanes(shape):
    return lax.broadcasted_iota(I32, shape, len(shape) - 1)


def subs(shape):
    return lax.broadcasted_iota(I32, shape, len(shape) - 2)


def route_kernel(routes_ref, slot_ref, slot_t_ref, starts_ref, work):
    images = routes_ref.shape[0]
    lane = lanes((ROWS, 128))
    strict = (lanes((ROWS, ROWS)) < subs((ROWS, ROWS))).astype(BF16)
    work[...] = jnp.full_like(work, -100)
    hots = []
    befores = []
    run = jnp.zeros((1, 128), F32)
    for b in range(images):
        work[0:SEQ, 0:TOP] = routes_ref[b]
        both = work[...]
        hot = ((both[:, 0:1] == lane) & (lane < E)) | (both[:, 1:2] + E == lane) & (lane >= E) & (lane < 2 * E)
        hot = hot.astype(F32)
        hots.append(hot)
        befores.append(dot(strict, hot.astype(BF16)) + run)
        run = run + jnp.sum(hot, axis=0, keepdims=True)
    first = jnp.where(lanes((1, 128)) < E, run, 0.0)
    shift = pltpu.roll(first, E, 1)
    base = jnp.zeros((1, 128), F32)
    starts = jnp.zeros((16, 128), F32)
    row = subs((16, 128))
    for b in range(images):
        kept = jnp.where(befores[b] + shift < CAP, hots[b], 0.0)
        kept = kept + pltpu.roll(kept, 128 - E, 1)
        kept = jnp.where(lane < E, kept, 0.0)
        place = dot(strict, kept.astype(BF16)) + base
        slot = jnp.where(kept > 0.0, place, -1000.0)
        slot_ref[b] = slot.astype(I32)
        slot_t_ref[b] = jnp.transpose(slot)[0:E, :].astype(I32)
        starts = jnp.where(row == b, base, starts)
        base = base + jnp.sum(kept, axis=0, keepdims=True)
    starts_ref[...] = jnp.where(row == images, base, starts).astype(I32)


def route_tables(routes):
    images = routes.shape[0]
    return pl.pallas_call(
        route_kernel,
        out_shape=(
            jax.ShapeDtypeStruct((images, ROWS, 128), I32),
            jax.ShapeDtypeStruct((images, E, ROWS), I32),
            jax.ShapeDtypeStruct((16, 128), I32),
        ),
        scratch_shapes=[pltpu.VMEM((ROWS, 128), I32)],
        compiler_params=params(),
        cost_estimate=cost(4),
        name="routing",
    )(routes)


def windows(starts, b):
    firsts, needs = [], []
    passes = jnp.int32(0)
    for e in range(E):
        start = starts[b, e]
        first = (start // 16) * 16
        need = starts[b + 1, e] - first
        firsts.append(first)
        needs.append(need)
        passes = jnp.maximum(passes, (need + WIN - 1) // WIN)
    return firsts, needs, passes


def norm_stats(rows):
    center = jnp.mean(rows, axis=-1, keepdims=True)
    spread = rows - center
    rs = lax.rsqrt(jnp.mean(spread * spread, axis=-1, keepdims=True) + NORM_EPS)
    return spread * rs, rs


def head_lane(half):
    lane = lanes((ROWS, 128))
    return (lane < HEAD_DIM) if half == 0 else (lane >= HEAD_DIM)


def front_kernel(
    starts, img_ref, cot_ref, slot_t_ref, ln_ref, qkvw_ref, outw_ref, rw_ref,
    qkv_ref, mixed_ref, middle_ref, rp_ref, lse_ref, hmax_ref, slots_ref,
    xb, rhs, oh,
):
    b = pl.program_id(0)

    @pl.when(b == 0)
    def _():
        xb[...] = jnp.zeros_like(xb)
        rhs[...] = jnp.zeros_like(rhs)
        slots_ref[...] = jnp.zeros_like(slots_ref)
        hmax_ref[...] = jnp.full_like(hmax_ref, LOW)

    xb[0:SEQ, :] = img_ref[0].astype(F32)
    x = xb[...]
    n1, _ = norm_stats(x)
    normed = (n1 * ln_ref[0:1, :] + ln_ref[1:2, :]).astype(BF16)
    qkv = dot(normed, qkvw_ref[...]).astype(BF16)
    qkv_ref[0] = qkv
    zero = jnp.zeros((ROWS, 128), BF16)
    cols = lanes((ROWS, ROWS))
    real = subs((ROWS, 1)) < SEQ
    lane = lanes((ROWS, 128))
    lse_all = jnp.zeros((ROWS, 128), F32)
    peaks = jnp.full((ROWS, 128), LOW, F32)
    parts = []
    for pair in range(HEADS // 2):
        q = qkv[:, 128 * pair : 128 * pair + 128]
        k = qkv[:, D + 128 * pair : D + 128 * pair + 128]
        v = qkv[:, 2 * D + 128 * pair : 2 * D + 128 * pair + 128]
        total = None
        for half in range(2):
            mine = head_lane(half)
            s = dot_nt(q, jnp.where(mine, k, zero)) * SCALE
            s = jnp.where(cols < SEQ, s, LOW)
            top = jnp.max(s, axis=-1, keepdims=True)
            powers = jnp.exp(s - top)
            norm = jnp.sum(powers, axis=-1, keepdims=True)
            probs = (powers / norm).astype(BF16)
            part = dot(probs, jnp.where(mine, v, zero))
            total = part if total is None else total + part
            h = 2 * pair + half
            lse_all = jnp.where(lane == h, top + jnp.log(norm), lse_all)
            peaks = jnp.where((lane == h) & real, top, peaks)
        parts.append(total.astype(BF16))
    mixed = jnp.concatenate(parts, axis=1)
    mixed_ref[0] = mixed
    lse_ref[0] = jnp.transpose(lse_all)[0:HEADS, :]
    hmax_ref[...] = jnp.maximum(hmax_ref[...], jnp.max(peaks, axis=0, keepdims=True))
    middle = x + dot(mixed, outw_ref[...])
    middle_ref[0] = middle
    n2, _ = norm_stats(middle)
    hidden = (n2 * ln_ref[2:3, :] + ln_ref[3:4, :]).astype(BF16)
    logits = jnp.where(lane < E, dot(hidden, rw_ref[...]), LOW)
    powers = jnp.exp(logits - jnp.max(logits, axis=-1, keepdims=True))
    rp = powers / jnp.sum(powers, axis=-1, keepdims=True)
    rp_ref[0] = rp
    high = rp.astype(BF16).astype(F32)
    rhs[:, 0:D] = hidden
    rhs[0:SEQ, D : 2 * D] = cot_ref[0]
    rhs[:, 2 * D : WIDE] = (high + pltpu.roll(rp - high, E, 1)).astype(BF16)

    firsts, needs, passes = windows(starts, b)
    place = subs((WIN, ROWS))

    def one_pass(p, carry):
        offs = []
        for e in range(E):
            begin = firsts[e] + p * WIN
            off = pl.multiple_of(jnp.minimum(begin, SLOTS - WIN), 16)
            offs.append(off)
            named = slot_t_ref[0, e : e + 1, :]
            ok = (named >= begin) & (named < begin + WIN)
            hit = jnp.where(ok, named - off, -1) == place
            oh[WIN * e : WIN * e + WIN, :] = hit.astype(F32).astype(BF16)
        picked = dot(oh[...], rhs[...]).astype(BF16)
        for e in range(E):

            @pl.when(p * WIN < needs[e])
            def _():
                slots_ref[e, pl.ds(offs[e], WIN), :] += picked[WIN * e : WIN * e + WIN, :]

        return carry

    lax.fori_loop(0, passes, one_pass, 0)


def front(starts, images, cot, slot_t, ln, qkvw, outw, rw):
    n = images.shape[0]
    whole = lambda shape: pl.BlockSpec(shape, lambda b, s: (0,) * len(shape), pipeline_mode=pl.Buffered(1))
    item = lambda *shape: pl.BlockSpec((1,) + shape, lambda b, s: (b,) + (0,) * len(shape))
    return pl.pallas_call(
        front_kernel,
        grid_spec=pltpu.PrefetchScalarGridSpec(
            num_scalar_prefetch=1,
            grid=(n,),
            in_specs=[
                item(SEQ, D), item(SEQ, D), item(E, ROWS), whole((8, D)), whole((D, 3 * D)), whole((D, D)), whole((D, AUX)),
            ],
            out_specs=[
                item(ROWS, 3 * D), item(ROWS, D), item(ROWS, D), item(ROWS, AUX), item(HEADS, ROWS),
                whole((1, 128)), whole((E, SLOTS, WIDE)),
            ],
            scratch_shapes=[
                pltpu.VMEM((ROWS, D), F32), pltpu.VMEM((ROWS, WIDE), BF16), pltpu.VMEM((E * WIN, ROWS), BF16),
            ],
        ),
        out_shape=(
            jax.ShapeDtypeStruct((n, ROWS, 3 * D), BF16),
            jax.ShapeDtypeStruct((n, ROWS, D), BF16),
            jax.ShapeDtypeStruct((n, ROWS, D), F32),
            jax.ShapeDtypeStruct((n, ROWS, AUX), F32),
            jax.ShapeDtypeStruct((n, HEADS, ROWS), F32),
            jax.ShapeDtypeStruct((1, 128), F32),
            jax.ShapeDtypeStruct((E, SLOTS, WIDE), BF16),
        ),
        compiler_params=params("arbitrary"),
        cost_estimate=cost(40),
        name="front",
    )(starts, images, cot, slot_t, ln, qkvw, outw, rw)


def gelu_parts(pre):
    c = math.sqrt(2.0 / math.pi)
    sq = pre * pre
    t = jnp.tanh(c * pre * (1.0 + 0.044715 * sq))
    half = 0.5 * (1.0 + t)
    act = pre * half
    slope = half + 0.5 * pre * (1.0 - t * t) * (c * (1.0 + 3.0 * 0.044715 * sq))
    return act, slope


def expert_kernel(nb, ids, slots_ref, win0_ref, wout0_ref, *refs):
    refs = list(refs)
    other_ref = refs.pop(0) if nb == 2 else None
    out_ref = refs.pop(0)
    act_s, preg_s, view = refs[-3:]
    grads = refs[:-3]
    for c in range(2):
        view[SLOTS * c : SLOTS * c + SLOTS, :] = slots_ref[c, 0]
    e = ids[0]
    me = ids[1]
    hb = win0_ref.shape[1]
    spot = [me, 1 - me] if nb == 2 else [0]

    def at(ref, start, size):
        if isinstance(start, int):
            return ref[:, start : start + size]
        return ref[:, pl.ds(pl.multiple_of(start, 128), size)]

    def win(r, q):
        return win0_ref[0, :, 512 * q : 512 * q + 512] if r == 0 else other_ref[q]

    def win_cols(r, start):
        if isinstance(start, int):
            return win0_ref[0, :, start : start + hb]
        if r == 0:
            return win0_ref[0, :, pl.ds(pl.multiple_of(start, 128), hb)]
        return other_ref[start // 512, :, pl.ds(pl.multiple_of(start % 512, 128), hb)]

    def wout(r, q):
        return wout0_ref[0, hb * q : hb * q + hb, :] if r == 0 else other_ref[4 + q]

    hid = [at(view, spot[r] * hb, hb) for r in range(nb)]
    got = view[:, D : 2 * D].astype(F32)
    aux = view[:, 2 * D : WIDE].astype(F32)
    lane = lanes((2 * SLOTS, AUX))
    gate = jnp.sum(jnp.where((lane == e) | (lane == e + E), aux, 0.0), axis=-1, keepdims=True)
    resg = (gate * got).astype(BF16)
    for r in range(nb):
        for q in range(4):
            start = spot[r] * (4 * hb) + q * hb
            pre = dot(hid[0], win_cols(0, start))
            for o in range(1, nb):
                pre = pre + dot(hid[o], win_cols(o, start))
            act, slope = gelu_parts(pre)
            actg = dot_nt(resg, wout(r, q))
            if isinstance(start, int):
                act_s[:, start : start + hb] = act.astype(BF16)
                preg_s[:, start : start + hb] = (actg * slope).astype(BF16)
            else:
                act_s[:, pl.ds(pl.multiple_of(start, 128), hb)] = act.astype(BF16)
                preg_s[:, pl.ds(pl.multiple_of(start, 128), hb)] = (actg * slope).astype(BF16)
    res = None
    for r in range(nb):
        for q in range(4):
            part = dot(at(act_s, spot[r] * (4 * hb) + q * hb, hb), wout(r, q))
            res = part if res is None else res + part
    gg = jnp.sum(got * res, axis=-1, keepdims=True)
    high = gg.astype(BF16).astype(F32)
    gg = jnp.where(lane == e, high, jnp.where(lane == e + E, gg - high, 0.0)).astype(BF16)
    res = (gate * res).astype(BF16)
    for c in range(2):
        out_ref[c, 0, :, 0:D] = res[SLOTS * c : SLOTS * c + SLOTS]
        out_ref[c, 0, :, 2 * D : WIDE] = gg[SLOTS * c : SLOTS * c + SLOTS]
    for r in range(nb):
        back = None
        for q in range(4):
            part = dot_nt(preg_s[:, 512 * q : 512 * q + 512], win(r, q))
            back = part if back is None else back + part
        back = back.astype(BF16)
        for c in range(2):
            if nb == 1:
                out_ref[c, 0, :, D : 2 * D] = back[SLOTS * c : SLOTS * c + SLOTS]
            else:
                out_ref[c, 0, :, pl.ds(pl.multiple_of(D + spot[r] * hb, 128), hb)] = back[SLOTS * c : SLOTS * c + SLOTS]
    for r in range(nb):
        for q in range(4):
            gin = dot_tn(hid[r], preg_s[:, 512 * q : 512 * q + 512])
            gout = dot_tn(at(act_s, spot[r] * (4 * hb) + q * hb, hb), resg)
            grads[r][q] = gin.astype(BF16)
            grads[r][4 + q] = gout.astype(BF16)


def expert_call(ids, slots, win0, wout0, other):
    nb = 1 if other is None else 2
    hb = win0.shape[1]
    once = pl.BlockSpec((8, hb, 512), lambda i, s: (0, 0, 0))
    both = pl.BlockSpec((2, 1, SLOTS, WIDE), lambda i, s: (0, s[2], 0, 0))
    pick = lambda *shape: pl.BlockSpec((1,) + shape, lambda i, s: (s[0],) + (0,) * len(shape))
    return pl.pallas_call(
        functools.partial(expert_kernel, nb),
        grid_spec=pltpu.PrefetchScalarGridSpec(
            num_scalar_prefetch=1,
            grid=(1,),
            in_specs=[both, pick(hb, FF), pick(4 * hb, D)] + [once] * (nb == 2),
            out_specs=[both] + [once] * nb,
            scratch_shapes=[
                pltpu.VMEM((2 * SLOTS, FF), BF16), pltpu.VMEM((2 * SLOTS, FF), BF16), pltpu.VMEM((2 * SLOTS, WIDE), BF16),
            ],
        ),
        out_shape=[jax.ShapeDtypeStruct(slots.shape, BF16)] + [jax.ShapeDtypeStruct((8, hb, 512), BF16)] * nb,
        input_output_aliases={1: 0},
        compiler_params=params("arbitrary"),
        cost_estimate=cost(31),
        name="expert",
    )(ids, slots, win0, wout0, *([other] if nb == 2 else []))


def norm_back(grad, n, rs, gain):
    u = grad * gain
    return rs * (u - jnp.mean(u, axis=-1, keepdims=True) - n * jnp.mean(u * n, axis=-1, keepdims=True))


def back_kernel(
    base, starts, ys_ref, slot_ref, middle_ref, img_ref, cot_ref, rp_ref, mixed_ref, qkv_ref, lse_ref, ln_ref, qkvw_ref, outw_ref, rw_ref,
    layer_ref, ingrad_ref, gqkv_ref, gout_ref, gmisc_ref,
    xb, gb, rhs, oh, comb, qg, lnacc,
):
    b = pl.program_id(0)

    @pl.when(b == 0)
    def _():
        xb[...] = jnp.zeros_like(xb)
        gb[...] = jnp.zeros_like(gb)
        gqkv_ref[...] = jnp.zeros_like(gqkv_ref)
        gout_ref[...] = jnp.zeros_like(gout_ref)
        gmisc_ref[...] = jnp.zeros_like(gmisc_ref)
        lnacc[...] = jnp.zeros_like(lnacc)

    firsts, needs, passes = windows(starts, base + b)
    lane = lanes((ROWS, 128))
    comb[...] = jnp.zeros_like(comb)

    def one_pass(p, carry):
        for e in range(E):
            begin = firsts[e] + p * WIN
            off = pl.multiple_of(jnp.minimum(begin, SLOTS - WIN), 16)
            rhs[WIN * e : WIN * e + WIN, :] = ys_ref[e, pl.ds(off, WIN), :]
            named = slot_ref[0, :, e : e + 1]
            ok = (named >= begin) & (named < begin + WIN)
            hit = jnp.where(ok, named - off, -1) == lane
            oh[:, WIN * e : WIN * e + WIN] = hit.astype(F32).astype(BF16)
        comb[...] += dot(oh[...], rhs[...])
        return carry

    lax.fori_loop(0, passes, one_pass, 0)

    middle = middle_ref[0]
    layer_ref[0] = (middle + comb[:, 0:D])[0:SEQ, :].astype(BF16)
    pg = comb[:, 2 * D : WIDE]
    rp = rp_ref[0]
    pg = jnp.where(lane < E, pg + pltpu.roll(pg, 128 - E, 1), 0.0)
    lg = (rp * (pg - jnp.sum(rp * pg, axis=-1, keepdims=True))).astype(BF16)
    n2, rs2 = norm_stats(middle)
    g2 = ln_ref[2:3, :]
    hidden = (n2 * g2 + ln_ref[3:4, :]).astype(BF16)
    gmisc_ref[...] += dot_tn(hidden, lg)
    hg = comb[:, D : 2 * D] + dot_nt(lg, rw_ref[...])
    gb[0:SEQ, :] = cot_ref[0].astype(F32)
    lnacc[10:11, :] += jnp.sum(hg * n2, axis=0, keepdims=True)
    lnacc[11:12, :] += jnp.sum(hg, axis=0, keepdims=True)
    mid_grad = gb[...] + norm_back(hg, n2, rs2, g2)
    bg = mid_grad.astype(BF16)
    gout_ref[...] += dot_tn(mixed_ref[0], bg)
    mg = dot_nt(bg, outw_ref[...]).astype(BF16)
    zero = jnp.zeros((ROWS, 128), BF16)
    keys = subs((ROWS, ROWS))
    for pair in range(HEADS // 2):
        lo = 128 * pair
        q = qkv_ref[0, :, lo : lo + 128]
        k = qkv_ref[0, :, D + lo : D + lo + 128]
        v = qkv_ref[0, :, 2 * D + lo : 2 * D + lo + 128]
        m = mg[:, lo : lo + 128]
        dq = dk = dv = None
        for half in range(2):
            mine = head_lane(half)
            kh = jnp.where(mine, k, zero)
            h = 2 * pair + half
            st = dot_nt(kh, q) * SCALE
            pt = jnp.where(keys < SEQ, jnp.exp(st - lse_ref[0, h : h + 1, :]), 0.0)
            dp = dot_nt(jnp.where(mine, v, zero), m)
            delta = jnp.sum(pt * dp, axis=0, keepdims=True)
            ds = (pt * (dp - delta)).astype(BF16)
            a = dot(pt.astype(BF16), jnp.where(mine, m, zero))
            c = dot(ds, jnp.where(mine, q, zero))
            d = dot_tn(ds, kh)
            dv = a if dv is None else dv + a
            dk = c if dk is None else dk + c
            dq = d if dq is None else dq + d
        qg[:, lo : lo + 128] = (dq * SCALE).astype(BF16)
        qg[:, D + lo : D + lo + 128] = (dk * SCALE).astype(BF16)
        qg[:, 2 * D + lo : 2 * D + lo + 128] = dv.astype(BF16)
    xb[0:SEQ, :] = img_ref[0].astype(F32)
    n1, rs1 = norm_stats(xb[...])
    g1 = ln_ref[0:1, :]
    normed = (n1 * g1 + ln_ref[1:2, :]).astype(BF16)
    gqkv_ref[...] += dot_tn(normed, qg[...])
    ng = dot_nt(qg[...], qkvw_ref[...])
    lnacc[8:9, :] += jnp.sum(ng * n1, axis=0, keepdims=True)
    lnacc[9:10, :] += jnp.sum(ng, axis=0, keepdims=True)
    ingrad_ref[0] = (mid_grad + norm_back(ng, n1, rs1, g1))[0:SEQ, :].astype(BF16)

    @pl.when(b == pl.num_programs(0) - 1)
    def _():
        gmisc_ref[...] += jnp.transpose(lnacc[...])


def back(base, count, starts, ys, slot, middle, images, cot, rp, mixed, qkv, lse, ln, qkvw, outw, rw, olds):
    whole = lambda shape: pl.BlockSpec(shape, lambda b, s: (0,) * len(shape), pipeline_mode=pl.Buffered(1))
    item = lambda *shape: pl.BlockSpec((1,) + shape, lambda b, s: (base + b,) + (0,) * len(shape))
    olds = list(olds or [])

    def kernel(*refs):
        back_kernel(base, *refs[:14], *refs[14 + len(olds) :])

    return pl.pallas_call(
        kernel,
        grid_spec=pltpu.PrefetchScalarGridSpec(
            num_scalar_prefetch=1,
            grid=(count,),
            in_specs=[
                whole((E, SLOTS, WIDE)), item(ROWS, 128), item(ROWS, D), item(SEQ, D), item(SEQ, D), item(ROWS, AUX), item(ROWS, D),
                item(ROWS, 3 * D), item(HEADS, ROWS), whole((8, D)), whole((D, 3 * D)), whole((D, D)), whole((D, AUX)),
            ] + [pl.BlockSpec(memory_space=pl.ANY)] * len(olds),
            out_specs=[item(SEQ, D), item(SEQ, D), whole((D, 3 * D)), whole((D, D)), whole((D, AUX))],
            scratch_shapes=[
                pltpu.VMEM((ROWS, D), F32), pltpu.VMEM((ROWS, D), F32), pltpu.VMEM((E * WIN, WIDE), BF16),
                pltpu.VMEM((ROWS, E * WIN), BF16), pltpu.VMEM((ROWS, WIDE), F32), pltpu.VMEM((ROWS, 3 * D), BF16),
                pltpu.VMEM((AUX, D), F32),
            ],
        ),
        out_shape=(
            jax.ShapeDtypeStruct(images.shape, BF16),
            jax.ShapeDtypeStruct(images.shape, BF16),
            jax.ShapeDtypeStruct((D, 3 * D), F32),
            jax.ShapeDtypeStruct((D, D), F32),
            jax.ShapeDtypeStruct((D, AUX), F32),
        ),
        input_output_aliases={14: 0, 15: 1} if olds else {},
        compiler_params=params("arbitrary"),
        cost_estimate=cost(17),
        name="back",
    )(starts, ys, slot, middle, images, cot, rp, mixed, qkv, lse, ln, qkvw, outw, rw, *olds)


def place_kernel(ids, *refs):
    in_ref, out_ref = refs[-2:]
    hb = in_ref.shape[1]

    def put(win_ref, wout_ref):
        for q in range(4):
            in_ref[0, :, 512 * q : 512 * q + 512] = win_ref[q].astype(F32)
            out_ref[0, hb * q : hb * q + hb, :] = wout_ref[q].astype(F32)

    for i in range(2):
        pl.when(pl.program_id(0) == i)(functools.partial(put, *refs[2 * i : 2 * i + 2]))


def place(ids, a, b, gin, gout):
    hb = a[0].shape[1]
    quad = lambda at: pl.BlockSpec((4, hb, 512), lambda i, s: (at, 0, 0))
    keep = pl.BlockSpec(memory_space=pl.ANY)
    fresh = gin is None
    olds = () if fresh else (gin, gout)
    args = (a[0], a[-1], b[0], b[-1], *olds)
    last = 1 if len(a) == 1 else 0
    return pl.pallas_call(
        place_kernel,
        grid_spec=pltpu.PrefetchScalarGridSpec(
            num_scalar_prefetch=1,
            grid=(2,),
            in_specs=[quad(0), quad(last), quad(0), quad(last)] + [keep] * len(olds),
            out_specs=[
                pl.BlockSpec((1, hb, FF), lambda i, s: (s[i], 0, 0)),
                pl.BlockSpec((1, 4 * hb, D), lambda i, s: (s[i], 0, 0)),
            ],
        ),
        out_shape=[jax.ShapeDtypeStruct((E, hb, FF), F32), jax.ShapeDtypeStruct((E, 4 * hb, D), F32)],
        input_output_aliases={} if fresh else {5: 0, 6: 1},
        compiler_params=params("arbitrary"),
        cost_estimate=cost(7),
        name="place",
    )(ids, *args)


def swap(value, axis, size, bit, name):
    with jax.named_scope(name):
        return lax.ppermute(value, axis, [(i, i ^ (1 << bit)) for i in range(size)])


def halves(value, flag, axis):
    size = value.shape[axis] // 2
    mine = lax.dynamic_slice_in_dim(value, flag * size, size, axis)
    other = lax.dynamic_slice_in_dim(value, (1 - flag) * size, size, axis)
    return mine, other


def joined(mine, other, flag, axis):
    return jnp.where(flag == 0, jnp.concatenate([mine, other], axis), jnp.concatenate([other, mine], axis))


def add(a, b):
    return (a.astype(F32) + b.astype(F32)).astype(BF16)


def pack(win, wout):
    hb = win.shape[0]
    return jnp.concatenate([jnp.transpose(win.reshape(hb, 4, 512), (1, 0, 2)), wout.reshape(4, hb, 512)], axis=0)


def cut_kernel(ids, win_ref, wout_ref, out_ref):
    for q in range(4):
        out_ref[q] = win_ref[0, :, 512 * q : 512 * q + 512]
        out_ref[4 + q] = wout_ref[0, q]


def cut(expert, piece, size, win, wout):
    hb = win.shape[1]
    return pl.pallas_call(
        cut_kernel,
        grid_spec=pltpu.PrefetchScalarGridSpec(
            num_scalar_prefetch=1,
            grid=(1,),
            in_specs=[
                pl.BlockSpec((1, size, FF), lambda i, s: (s[0], s[1], 0)),
                pl.BlockSpec((1, 4, size, D), lambda i, s: (s[0], 0, s[1], 0)),
            ],
            out_specs=pl.BlockSpec((8, size, 512), lambda i, s: (0, 0, 0)),
        ),
        out_shape=jax.ShapeDtypeStruct((8, size, 512), BF16),
        compiler_params=params("arbitrary"),
        cost_estimate=cost(2),
        name="cut",
    )(jnp.stack([expert, piece]).astype(I32), win, wout.reshape(E, 4, hb, D))


def gather_kernel(ids, qkv_ref, out_ref, near_ref, far_ref, small_ref, qkvw_ref, outw_ref, ln_ref, rw_ref, work):
    grp = ids[0]
    core = ids[1]
    hb = qkv_ref.shape[0]
    part = hb // 2
    rows = lambda start, size: pl.ds(pl.multiple_of(start, 128), size)
    mine = grp * hb
    other = (1 - grp) * hb
    qkvw_ref[rows(mine, hb), :] = qkv_ref[...]
    outw_ref[rows(mine, hb), :] = out_ref[...]
    for ref, at in ((near_ref, other + core * part), (far_ref, other + (1 - core) * part)):
        qkvw_ref[rows(at, part), :] = ref[:, 0 : 3 * D]
        outw_ref[rows(at, part), :] = ref[:, 3 * D : 4 * D]
    ln_ref[...] = jnp.zeros_like(ln_ref)
    work[...] = jnp.zeros_like(work)
    lane = lanes((hb, AUX))
    for these, at in ((small_ref[...], mine), (near_ref[0:16, 4 * D :], other)):
        work[0:16, :] = these.astype(F32)
        ln_ref[0:4, rows(at, hb)] = work[0:4, :]
        router = pltpu.roll(jnp.transpose(work[...]), AUX - 4, 1)
        rw_ref[rows(at, hb), :] = jnp.where(lane < E, router, 0.0).astype(BF16)


def gathered(ids, qkv_weight, out_weight, near, far, small):
    return pl.pallas_call(
        gather_kernel,
        grid_spec=pltpu.PrefetchScalarGridSpec(
            num_scalar_prefetch=1,
            grid=(1,),
            in_specs=[pl.BlockSpec(a.shape, lambda i, s: (0, 0)) for a in (qkv_weight, out_weight, near, far, small)],
            out_specs=[pl.BlockSpec(shape, lambda i, s: (0, 0)) for shape in ((D, 3 * D), (D, D), (8, D), (D, AUX))],
            scratch_shapes=[pltpu.VMEM((AUX, qkv_weight.shape[0]), F32)],
        ),
        out_shape=[
            jax.ShapeDtypeStruct((D, 3 * D), BF16),
            jax.ShapeDtypeStruct((D, D), BF16),
            jax.ShapeDtypeStruct((8, D), F32),
            jax.ShapeDtypeStruct((D, AUX), BF16),
        ],
        compiler_params=params("arbitrary"),
        cost_estimate=cost(3),
        name="gathered",
    )(ids, qkv_weight, out_weight, near, far, small)


class Order:
    def __init__(self):
        self.last = None

    def __call__(self, *values):
        if self.last is None:
            return values
        return lax.optimization_barrier((*values, self.last))[:-1]

    def done(self, value):
        self.last = value
        return value

    def pass_on(self, value):
        (value,) = self(value)
        return self.done(value)


def per_device(
    reps, groups, images, ln1_gain, ln1_bias, qkv_weight, out_weight, ln2_gain, ln2_bias, router_weight, expert_in, expert_out, routes, cotangent
):
    rep = lax.axis_index("rep")
    grp = lax.axis_index("grp")
    bits = reps.bit_length() - 1
    rbit = [(rep >> i) & 1 for i in range(bits)]
    core = rbit[0]
    rswap = lambda value, bit, name: swap(value, "rep", reps, bit, f"{name}_rep{bit}")
    gswap = lambda value, name: swap(value, "grp", 2, 0, f"{name}_grp")
    pairs = groups == 2
    hb = expert_in.shape[1]
    order = Order()
    chunks = E // 2
    near_ids = [j + chunks * core for j in range(chunks)]
    far_ids = [j + chunks * (1 - core) for j in range(chunks)]
    spread = [bit for bit in (2, 1) if bit < bits]
    ways = [spread if j % 2 == 0 else spread[::-1] for j in range(chunks)]

    def first_cut(j):
        piece, size = 0, hb
        for bit in ways[j][::-1]:
            size = size // 2
            piece = piece * 2 + rbit[bit]
        win, wout = order(expert_in, expert_out)
        return order.done(cut(near_ids[j], piece, size, win, wout))

    weights = [None] * chunks
    step = [0] * chunks

    def weights_out(j):
        if not pairs:
            return
        at = step[j]
        step[j] += 1
        if at == 0:
            weights[j] = (None, gswap(first_cut(j), f"weights{j}"))
            return
        mine, other = weights[j]
        if at == 1:
            mine = order.pass_on(other)
        else:
            mine, other = order(mine, other)
            mine = order.done(joined(mine, other, rbit[ways[j][at - 2]], 1))
        weights[j] = (mine, rswap(mine, ways[j][at - 1], f"weights{j}") if at <= len(spread) else None)

    peak = [None, 0]
    last_peak = bits + groups.bit_length() - 1
    clipped = None

    def peak_more():
        nonlocal clipped
        value, at = peak
        if at > last_peak + 1:
            return
        if at > 0:
            value = order(*value)
            value = order.done(jnp.maximum(*value))
        if at < last_peak - bits:
            peak[0] = (value, swap(value, "grp", groups, at, "peak_grp"))
        elif at < last_peak:
            peak[0] = (value, rswap(value, at - (last_peak - bits), "peak"))
        else:
            clip = jnp.sqrt(CLIP_LIMIT / jnp.maximum(value[0, :HEADS], CLIP_LIMIT))
            column_scale = jnp.tile(jnp.repeat(clip, HEAD_DIM), 2)
            clipped = order.done(qkv_weight[:, : 2 * D].astype(F32) * column_scale[None, :])
            peak[1] = last_peak + 2
            return
        peak[1] += 1

    width = ln1_gain.shape[0]
    small = jnp.concatenate(
        [jnp.stack([ln1_gain, ln1_bias, ln2_gain, ln2_bias]), jnp.transpose(router_weight), jnp.zeros((4, width), BF16)], axis=0
    )
    win0, wout0 = expert_in, expert_out
    if pairs:
        weights_out(0)
        dense = [lax.dynamic_slice_in_dim(w, core * (hb // 2), hb // 2, 0) for w in order(qkv_weight, out_weight)]
        dense = jnp.concatenate([*dense, jnp.pad(small, ((0, hb // 2 - 16), (0, 0)))], axis=1)
        near = gswap(order.done(dense), "dense")
        for j in range(1, chunks):
            weights_out(j)
        slot, slot_t, starts = route_tables(*order(routes))
        order.done(starts)
        weights_out(0)
        near = order.pass_on(near)
        far = rswap(near, 0, "dense")
        weights_out(0)
        ids = jnp.stack([grp, core]).astype(I32)
        qkvw, outw, ln, rw = gathered(ids, qkv_weight, out_weight, *order(near, far, small))
        order.done(ln)
    else:
        dense = jnp.concatenate([qkv_weight, out_weight], axis=1)
        small = lax.all_gather(small, "grp", axis=1, tiled=True)
        dense = lax.all_gather(dense, "grp", axis=0, tiled=True)
        slot, slot_t, starts = route_tables(routes)
        ln = jnp.concatenate([small[0:4].astype(F32), jnp.zeros((4, D), F32)], axis=0)
        rw = jnp.pad(jnp.transpose(small[4 : 4 + E]), ((0, 0), (0, AUX - E)))
        qkvw = dense[:, : 3 * D]
        outw = dense[:, 3 * D :]
        win0 = lax.all_gather(expert_in, "grp", axis=1, tiled=True)
        wout0 = lax.all_gather(expert_out, "grp", axis=1, tiled=True)
        weights = [(None, None)] * chunks

    (ln,) = order(ln)
    qkv, mixed, middle, rp, lse, hmax, slots = front(starts, images, cotangent, slot_t, ln, qkvw, outw, rw)
    peak[0] = order.done(hmax)

    couples = [[i, i + 1] for i in range(0, reps, 2)]

    def between_cores(value, name):
        (value,) = order(value)
        with jax.named_scope(name):
            return order.done(lax.all_to_all(value, "rep", 0, 0, axis_index_groups=couples, tiled=True))

    state = {}

    def expert(j):
        nonlocal slots
        ids = jnp.stack([near_ids[j], grp, j]).astype(I32)
        (held,) = order(slots)
        slots, *grads = expert_call(ids, held, win0, wout0, weights[j][0])
        order.done(grads[0])
        if pairs:
            state[j] = (0, grads[0], gswap(grads[1], f"grad{j}"))
        else:
            full = grads[0]
            gin = lax.psum_scatter(jnp.transpose(full[0:4], (1, 0, 2)).reshape(D, FF), "grp", scatter_dimension=0, tiled=True)
            gout = lax.psum_scatter(full[4:8].reshape(FF, D), "grp", scatter_dimension=0, tiled=True)
            part = pack(gin, gout)
            state[j] = (0, part, jnp.zeros_like(part))

    down = list(range(1, bits))
    up = down[::-1] + [0]
    placed = [None, None]
    ends = len(down) + len(up)

    def more(j):
        at, keep, recv = state[j]
        if at > ends:
            return
        keep, recv = order(keep, recv)
        n = len(down)
        if at < n:
            bit = down[at]
            keep_mine, keep_other = halves(keep, rbit[bit], 1)
            recv_mine, recv_other = halves(recv, rbit[bit], 1)
            send = add(keep_other, recv_other)
            keep = order.done(add(keep_mine, recv_mine))
            state[j] = (at + 1, keep, rswap(send, bit, f"grad{j}_down"))
        elif at < ends:
            bit = up[at - n]
            total = add(keep, recv) if at == n else joined(keep, recv, rbit[up[at - n - 1]], 1)
            order.done(total)
            state[j] = (at + 1, total, rswap(total, bit, f"grad{j}_up"))
        else:
            ids = jnp.stack([near_ids[j], far_ids[j]]).astype(I32)
            placed[0], placed[1] = place(ids, [keep], [recv], placed[0], placed[1])
            order.done(placed[0])
            state[j] = (at + 1, None, None)

    peak_more()
    weights_out(1)
    weights_out(2)
    weights_out(3)
    slots = between_cores(slots.reshape(2, chunks, SLOTS, WIDE), "slots")
    weights_out(0)
    weights_out(1)
    weights_out(2)
    peak_more()
    expert(0)
    weights_out(1)
    weights_out(3)
    peak_more()
    expert(1)
    weights_out(2)
    peak_more()
    expert(2)
    weights_out(3)
    more(0)
    peak_more()
    expert(3)
    more(0)
    peak_more()
    peak_more()
    slots = between_cores(slots, "results").reshape(E, SLOTS, WIDE)
    while clipped is None:
        peak_more()

    n = images.shape[0]
    parts = 4
    outs, accs = None, None
    between = [
        [lambda: more(1), lambda: more(0)],
        [lambda: more(0), lambda: more(1)],
        [lambda: more(2), lambda: more(0), lambda: more(1)],
        [],
    ]
    for i in range(parts):
        (held,) = order(slots)
        *outs, gqkv, gout, gmisc = back(
            i * (n // parts), n // parts, starts, held, slot, middle, images, cotangent, rp, mixed, qkv, lse, ln, qkvw, outw, rw, outs
        )
        order.done(gmisc)
        accs = (gqkv, gout, gmisc) if accs is None else tuple(a + b for a, b in zip(accs, (gqkv, gout, gmisc)))
        for step in between[i]:
            step()

    dense_at = [0]
    acc = jnp.concatenate(order(*accs), axis=1).astype(BF16)
    dense_state = [acc.reshape(groups, D // groups, -1), None]
    final = None

    def dense_more():
        nonlocal final
        at = dense_at[0]
        dense_at[0] += 1
        keep, recv = dense_state
        n = len(down)
        if at == 0:
            (keep,) = order(keep)
            mine, send = halves(keep, core, 1)
            order.done(send)
            dense_state[:] = [mine, rswap(send, 0, "dense_down")]
        elif at == 1:
            total = order.done(add(*order(keep, recv)))
            if pairs:
                mine = lax.dynamic_slice_in_dim(total, grp, 1, 0)[0]
                send = lax.dynamic_slice_in_dim(total, 1 - grp, 1, 0)[0]
                dense_state[:] = [mine, gswap(send, "dense_down")]
            else:
                total = lax.psum_scatter(total, "grp", scatter_dimension=0, tiled=True)[0]
                dense_state[:] = [total, jnp.zeros_like(total)]
        elif at < 2 + n:
            total = order.done(add(*order(keep, recv)))
            bit = down[at - 2]
            mine, send = halves(total, rbit[bit], 0)
            dense_state[:] = [mine, rswap(send, bit, "dense_down")]
        elif at < 2 + n + len(up):
            bit = up[at - 2 - n]
            keep, recv = order(keep, recv)
            total = add(keep, recv) if at == 2 + n else joined(keep, recv, rbit[up[at - 3 - n]], 0)
            dense_state[:] = [order.done(total), rswap(total, bit, "dense_up")]
        elif at == 2 + n + len(up):
            total = joined(*order(keep, recv), core, 0).astype(F32)
            misc = total[:, 4 * D :]
            final = (
                misc[:, 8], misc[:, 9], total[:, : 3 * D], total[:, 3 * D : 4 * D], misc[:, 10], misc[:, 11], misc[:, :E],
            )
            order.done(final[2])

    more(3)
    sizes = {key: 2.1 for key in state}
    links = {bit: ("core", "y", "z", "z")[min(bit, 3)] for bit in range(bits)}
    wire = lambda bit, size: (links[bit], (2.5 if bit == 0 else 45.0 if bit == 3 else 22.5) * size + 4)
    legs = {}
    for key, size in sizes.items():
        legs[key] = [("x", 22.5 * size + 4)] + [wire(bit, size / 2 ** (i + 1)) for i, bit in enumerate(down)]
        legs[key] += [wire(bit, size / 2 ** (len(down) - i)) for i, bit in enumerate(up)]
        legs[key] = legs[key][state[key][0] :]
    legs["dense"] = [("none", 0), wire(0, 1.1), ("x", 16)] + [wire(bit, 0.28 / 2**i) for i, bit in enumerate(down)]
    legs["dense"] += [wire(bit, 0.28 / 2 ** max(0, len(down) - 1 - i)) for i, bit in enumerate(up)]
    clear, due, now = {}, {}, 0.0

    def sail(key):
        link, size = legs[key].pop(0)
        begin = now if link == "none" else max(now, clear.get(link, 0.0))
        clear[link] = due[key] = begin + size

    for key in list(legs):
        if legs[key]:
            sail(key)
    while due:
        key = min(due, key=lambda k: (due[k], str(k)))
        now = max(now, due.pop(key)) + 2
        if key == "dense":
            dense_more()
        else:
            more(key)
            if state[key][0] > ends:
                now = now + 7
        if legs[key]:
            sail(key)
    while clipped is None:
        peak_more()
    while final is None:
        dense_more()
    return (outs[0], outs[1], clipped, *final, placed[0], placed[1])


def solution(mesh):
    rows = P(("rep", "grp"), None, None)
    line = P("grp")
    table = P("grp", None)
    cube = P(None, "grp", None)
    in_specs = (rows, line, line, table, table, line, line, table, cube, cube, rows, rows)
    out_specs = (rows, rows, table, line, line, table, table, line, line, table, cube, cube)
    body = functools.partial(per_device, mesh.shape["rep"], mesh.shape["grp"])
    return jax.shard_map(body, mesh=mesh, in_specs=in_specs, out_specs=out_specs, check_vma=False)
```

```python
import functools
import math

import jax
import jax.numpy as jnp
from jax import lax
from jax.experimental import pallas as pl
from jax.experimental.pallas import tpu as pltpu
from jax.sharding import PartitionSpec as P

D = 512
HEADS = 8
HEAD_DIM = 64
FF = 2048
E = 8
TOP = 2
SEQ = 197
CAP = 591
ROWS = 208
SLOTS = 640
WIN = 128
AUX = 128
WIDE = 2 * D + AUX
NORM_EPS = 1e-06
CLIP_LIMIT = 3.0
SCALE = HEAD_DIM ** (-0.5)
LOW = -1e30
F32 = jnp.float32
BF16 = jnp.bfloat16
I32 = jnp.int32


def dot(a, b):
    return lax.dot_general(a, b, (((1,), (0,)), ((), ())), preferred_element_type=F32)


def dot_nt(a, b):
    return lax.dot_general(a, b, (((1,), (1,)), ((), ())), preferred_element_type=F32)


def dot_tn(a, b):
    return lax.dot_general(a, b, (((0,), (0,)), ((), ())), preferred_element_type=F32)


def params(*semantics):
    return pltpu.CompilerParams(dimension_semantics=semantics, vmem_limit_bytes=60 * 1024 * 1024)


def cost(us):
    return pl.CostEstimate(flops=int(us * 3e+08), transcendentals=0, bytes_accessed=1)


def lanes(shape):
    return lax.broadcasted_iota(I32, shape, len(shape) - 1)


def subs(shape):
    return lax.broadcasted_iota(I32, shape, len(shape) - 2)


def route_kernel(routes_ref, slot_ref, slot_t_ref, starts_ref, work):
    images = routes_ref.shape[0]
    lane = lanes((ROWS, 128))
    strict = (lanes((ROWS, ROWS)) < subs((ROWS, ROWS))).astype(BF16)
    work[...] = jnp.full_like(work, -100)
    hots = []
    befores = []
    run = jnp.zeros((1, 128), F32)
    for b in range(images):
        work[0:SEQ, 0:TOP] = routes_ref[b]
        both = work[...]
        hot = ((both[:, 0:1] == lane) & (lane < E)) | (both[:, 1:2] + E == lane) & (lane >= E) & (lane < 2 * E)
        hot = hot.astype(F32)
        hots.append(hot)
        befores.append(dot(strict, hot.astype(BF16)) + run)
        run = run + jnp.sum(hot, axis=0, keepdims=True)
    first = jnp.where(lanes((1, 128)) < E, run, 0.0)
    shift = pltpu.roll(first, E, 1)
    base = jnp.zeros((1, 128), F32)
    starts = jnp.zeros((16, 128), F32)
    row = subs((16, 128))
    for b in range(images):
        kept = jnp.where(befores[b] + shift < CAP, hots[b], 0.0)
        kept = kept + pltpu.roll(kept, 128 - E, 1)
        kept = jnp.where(lane < E, kept, 0.0)
        place = dot(strict, kept.astype(BF16)) + base
        slot = jnp.where(kept > 0.0, place, -1000.0)
        slot_ref[b] = slot.astype(I32)
        slot_t_ref[b] = jnp.transpose(slot)[0:E, :].astype(I32)
        starts = jnp.where(row == b, base, starts)
        base = base + jnp.sum(kept, axis=0, keepdims=True)
    starts_ref[...] = jnp.where(row == images, base, starts).astype(I32)


def route_tables(routes):
    images = routes.shape[0]
    return pl.pallas_call(
        route_kernel,
        out_shape=(
            jax.ShapeDtypeStruct((images, ROWS, 128), I32),
            jax.ShapeDtypeStruct((images, E, ROWS), I32),
            jax.ShapeDtypeStruct((16, 128), I32),
        ),
        scratch_shapes=[pltpu.VMEM((ROWS, 128), I32)],
        compiler_params=params(),
        cost_estimate=cost(4),
        name="routing",
    )(routes)


def windows(starts, b):
    firsts, needs = [], []
    passes = jnp.int32(0)
    for e in range(E):
        start = starts[b, e]
        first = (start // 16) * 16
        need = starts[b + 1, e] - first
        firsts.append(first)
        needs.append(need)
        passes = jnp.maximum(passes, (need + WIN - 1) // WIN)
    return firsts, needs, passes


def norm_stats(rows):
    center = jnp.mean(rows, axis=-1, keepdims=True)
    spread = rows - center
    rs = lax.rsqrt(jnp.mean(spread * spread, axis=-1, keepdims=True) + NORM_EPS)
    return spread * rs, rs


def head_lane(half):
    lane = lanes((ROWS, 128))
    return (lane < HEAD_DIM) if half == 0 else (lane >= HEAD_DIM)


def front_kernel(
    starts, img_ref, cot_ref, slot_t_ref, ln_ref, qkvw_ref, outw_ref, rw_ref,
    qkv_ref, mixed_ref, middle_ref, rp_ref, lse_ref, hmax_ref, slots_ref,
    xb, rhs, oh,
):
    b = pl.program_id(0)

    @pl.when(b == 0)
    def _():
        xb[...] = jnp.zeros_like(xb)
        rhs[...] = jnp.zeros_like(rhs)
        slots_ref[...] = jnp.zeros_like(slots_ref)
        hmax_ref[...] = jnp.full_like(hmax_ref, LOW)

    xb[0:SEQ, :] = img_ref[0].astype(F32)
    x = xb[...]
    n1, _ = norm_stats(x)
    normed = (n1 * ln_ref[0:1, :] + ln_ref[1:2, :]).astype(BF16)
    qkv = dot(normed, qkvw_ref[...]).astype(BF16)
    qkv_ref[0] = qkv
    zero = jnp.zeros((ROWS, 128), BF16)
    cols = lanes((ROWS, ROWS))
    real = subs((ROWS, 1)) < SEQ
    lane = lanes((ROWS, 128))
    lse_all = jnp.zeros((ROWS, 128), F32)
    peaks = jnp.full((ROWS, 128), LOW, F32)
    parts = []
    for pair in range(HEADS // 2):
        q = qkv[:, 128 * pair : 128 * pair + 128]
        k = qkv[:, D + 128 * pair : D + 128 * pair + 128]
        v = qkv[:, 2 * D + 128 * pair : 2 * D + 128 * pair + 128]
        total = None
        for half in range(2):
            mine = head_lane(half)
            s = dot_nt(q, jnp.where(mine, k, zero)) * SCALE
            s = jnp.where(cols < SEQ, s, LOW)
            top = jnp.max(s, axis=-1, keepdims=True)
            powers = jnp.exp(s - top)
            norm = jnp.sum(powers, axis=-1, keepdims=True)
            probs = (powers / norm).astype(BF16)
            part = dot(probs, jnp.where(mine, v, zero))
            total = part if total is None else total + part
            h = 2 * pair + half
            lse_all = jnp.where(lane == h, top + jnp.log(norm), lse_all)
            peaks = jnp.where((lane == h) & real, top, peaks)
        parts.append(total.astype(BF16))
    mixed = jnp.concatenate(parts, axis=1)
    mixed_ref[0] = mixed
    lse_ref[0] = jnp.transpose(lse_all)[0:HEADS, :]
    hmax_ref[...] = jnp.maximum(hmax_ref[...], jnp.max(peaks, axis=0, keepdims=True))
    middle = x + dot(mixed, outw_ref[...])
    middle_ref[0] = middle
    n2, _ = norm_stats(middle)
    hidden = (n2 * ln_ref[2:3, :] + ln_ref[3:4, :]).astype(BF16)
    logits = jnp.where(lane < E, dot(hidden, rw_ref[...]), LOW)
    powers = jnp.exp(logits - jnp.max(logits, axis=-1, keepdims=True))
    rp = powers / jnp.sum(powers, axis=-1, keepdims=True)
    rp_ref[0] = rp
    high = rp.astype(BF16).astype(F32)
    rhs[:, 0:D] = hidden
    rhs[0:SEQ, D : 2 * D] = cot_ref[0]
    rhs[:, 2 * D : WIDE] = (high + pltpu.roll(rp - high, E, 1)).astype(BF16)

    firsts, needs, passes = windows(starts, b)
    place = subs((WIN, ROWS))

    def one_pass(p, carry):
        offs = []
        for e in range(E):
            begin = firsts[e] + p * WIN
            off = pl.multiple_of(jnp.minimum(begin, SLOTS - WIN), 16)
            offs.append(off)
            named = slot_t_ref[0, e : e + 1, :]
            ok = (named >= begin) & (named < begin + WIN)
            hit = jnp.where(ok, named - off, -1) == place
            oh[WIN * e : WIN * e + WIN, :] = hit.astype(F32).astype(BF16)
        picked = dot(oh[...], rhs[...]).astype(BF16)
        for e in range(E):

            @pl.when(p * WIN < needs[e])
            def _():
                slots_ref[e, pl.ds(offs[e], WIN), :] += picked[WIN * e : WIN * e + WIN, :]

        return carry

    lax.fori_loop(0, passes, one_pass, 0)


def front(starts, images, cot, slot_t, ln, qkvw, outw, rw):
    n = images.shape[0]
    whole = lambda shape: pl.BlockSpec(shape, lambda b, s: (0,) * len(shape), pipeline_mode=pl.Buffered(1))
    item = lambda *shape: pl.BlockSpec((1,) + shape, lambda b, s: (b,) + (0,) * len(shape))
    return pl.pallas_call(
        front_kernel,
        grid_spec=pltpu.PrefetchScalarGridSpec(
            num_scalar_prefetch=1,
            grid=(n,),
            in_specs=[
                item(SEQ, D), item(SEQ, D), item(E, ROWS), whole((8, D)), whole((D, 3 * D)), whole((D, D)), whole((D, AUX)),
            ],
            out_specs=[
                item(ROWS, 3 * D), item(ROWS, D), item(ROWS, D), item(ROWS, AUX), item(HEADS, ROWS),
                whole((1, 128)), whole((E, SLOTS, WIDE)),
            ],
            scratch_shapes=[
                pltpu.VMEM((ROWS, D), F32), pltpu.VMEM((ROWS, WIDE), BF16), pltpu.VMEM((E * WIN, ROWS), BF16),
            ],
        ),
        out_shape=(
            jax.ShapeDtypeStruct((n, ROWS, 3 * D), BF16),
            jax.ShapeDtypeStruct((n, ROWS, D), BF16),
            jax.ShapeDtypeStruct((n, ROWS, D), F32),
            jax.ShapeDtypeStruct((n, ROWS, AUX), F32),
            jax.ShapeDtypeStruct((n, HEADS, ROWS), F32),
            jax.ShapeDtypeStruct((1, 128), F32),
            jax.ShapeDtypeStruct((E, SLOTS, WIDE), BF16),
        ),
        compiler_params=params("arbitrary"),
        cost_estimate=cost(40),
        name="front",
    )(starts, images, cot, slot_t, ln, qkvw, outw, rw)


def gelu_parts(pre):
    c = math.sqrt(2.0 / math.pi)
    sq = pre * pre
    t = jnp.tanh(c * pre * (1.0 + 0.044715 * sq))
    half = 0.5 * (1.0 + t)
    act = pre * half
    slope = half + 0.5 * pre * (1.0 - t * t) * (c * (1.0 + 3.0 * 0.044715 * sq))
    return act, slope


def expert_kernel(nb, ids, slots_ref, win0_ref, wout0_ref, *refs):
    refs = list(refs)
    other_ref = refs.pop(0) if nb == 2 else None
    out_ref = refs.pop(0)
    act_s, preg_s, view = refs[-3:]
    grads = refs[:-3]
    for c in range(2):
        view[SLOTS * c : SLOTS * c + SLOTS, :] = slots_ref[c, 0]
    e = ids[0]
    me = ids[1]
    hb = win0_ref.shape[1]
    spot = [me, 1 - me] if nb == 2 else [0]

    def at(ref, start, size):
        if isinstance(start, int):
            return ref[:, start : start + size]
        return ref[:, pl.ds(pl.multiple_of(start, 128), size)]

    def win(r, q):
        return win0_ref[0, :, 512 * q : 512 * q + 512] if r == 0 else other_ref[q]

    def win_cols(r, start):
        if isinstance(start, int):
            return win0_ref[0, :, start : start + hb]
        if r == 0:
            return win0_ref[0, :, pl.ds(pl.multiple_of(start, 128), hb)]
        return other_ref[start // 512, :, pl.ds(pl.multiple_of(start % 512, 128), hb)]

    def wout(r, q):
        return wout0_ref[0, hb * q : hb * q + hb, :] if r == 0 else other_ref[4 + q]

    hid = [at(view, spot[r] * hb, hb) for r in range(nb)]
    got = view[:, D : 2 * D].astype(F32)
    aux = view[:, 2 * D : WIDE].astype(F32)
    lane = lanes((2 * SLOTS, AUX))
    gate = jnp.sum(jnp.where((lane == e) | (lane == e + E), aux, 0.0), axis=-1, keepdims=True)
    resg = (gate * got).astype(BF16)
    for r in range(nb):
        for q in range(4):
            start = spot[r] * (4 * hb) + q * hb
            pre = dot(hid[0], win_cols(0, start))
            for o in range(1, nb):
                pre = pre + dot(hid[o], win_cols(o, start))
            act, slope = gelu_parts(pre)
            actg = dot_nt(resg, wout(r, q))
            if isinstance(start, int):
                act_s[:, start : start + hb] = act.astype(BF16)
                preg_s[:, start : start + hb] = (actg * slope).astype(BF16)
            else:
                act_s[:, pl.ds(pl.multiple_of(start, 128), hb)] = act.astype(BF16)
                preg_s[:, pl.ds(pl.multiple_of(start, 128), hb)] = (actg * slope).astype(BF16)
    res = None
    for r in range(nb):
        for q in range(4):
            part = dot(at(act_s, spot[r] * (4 * hb) + q * hb, hb), wout(r, q))
            res = part if res is None else res + part
    gg = jnp.sum(got * res, axis=-1, keepdims=True)
    high = gg.astype(BF16).astype(F32)
    gg = jnp.where(lane == e, high, jnp.where(lane == e + E, gg - high, 0.0)).astype(BF16)
    res = (gate * res).astype(BF16)
    for c in range(2):
        out_ref[c, 0, :, 0:D] = res[SLOTS * c : SLOTS * c + SLOTS]
        out_ref[c, 0, :, 2 * D : WIDE] = gg[SLOTS * c : SLOTS * c + SLOTS]
    for r in range(nb):
        back = None
        for q in range(4):
            part = dot_nt(preg_s[:, 512 * q : 512 * q + 512], win(r, q))
            back = part if back is None else back + part
        back = back.astype(BF16)
        for c in range(2):
            if nb == 1:
                out_ref[c, 0, :, D : 2 * D] = back[SLOTS * c : SLOTS * c + SLOTS]
            else:
                out_ref[c, 0, :, pl.ds(pl.multiple_of(D + spot[r] * hb, 128), hb)] = back[SLOTS * c : SLOTS * c + SLOTS]
    for r in range(nb):
        for q in range(4):
            gin = dot_tn(hid[r], preg_s[:, 512 * q : 512 * q + 512])
            gout = dot_tn(at(act_s, spot[r] * (4 * hb) + q * hb, hb), resg)
            grads[r][q] = gin.astype(BF16)
            grads[r][4 + q] = gout.astype(BF16)


def expert_call(ids, slots, win0, wout0, other):
    nb = 1 if other is None else 2
    hb = win0.shape[1]
    once = pl.BlockSpec((8, hb, 512), lambda i, s: (0, 0, 0))
    both = pl.BlockSpec((2, 1, SLOTS, WIDE), lambda i, s: (0, s[2], 0, 0))
    pick = lambda *shape: pl.BlockSpec((1,) + shape, lambda i, s: (s[0],) + (0,) * len(shape))
    return pl.pallas_call(
        functools.partial(expert_kernel, nb),
        grid_spec=pltpu.PrefetchScalarGridSpec(
            num_scalar_prefetch=1,
            grid=(1,),
            in_specs=[both, pick(hb, FF), pick(4 * hb, D)] + [once] * (nb == 2),
            out_specs=[both] + [once] * nb,
            scratch_shapes=[
                pltpu.VMEM((2 * SLOTS, FF), BF16), pltpu.VMEM((2 * SLOTS, FF), BF16), pltpu.VMEM((2 * SLOTS, WIDE), BF16),
            ],
        ),
        out_shape=[jax.ShapeDtypeStruct(slots.shape, BF16)] + [jax.ShapeDtypeStruct((8, hb, 512), BF16)] * nb,
        input_output_aliases={1: 0},
        compiler_params=params("arbitrary"),
        cost_estimate=cost(31),
        name="expert",
    )(ids, slots, win0, wout0, *([other] if nb == 2 else []))


def norm_back(grad, n, rs, gain):
    u = grad * gain
    return rs * (u - jnp.mean(u, axis=-1, keepdims=True) - n * jnp.mean(u * n, axis=-1, keepdims=True))


def back_kernel(
    base, sums, starts, ys_ref, slot_ref, middle_ref, img_ref, cot_ref, rp_ref, mixed_ref, qkv_ref, lse_ref, ln_ref, qkvw_ref, outw_ref, rw_ref,
    layer_ref, ingrad_ref, gqkv_ref, gout_ref, gmisc_ref,
    xb, gb, rhs, oh, comb, qg, lnacc,
):
    b = pl.program_id(0)

    @pl.when(b == 0)
    def _():
        xb[...] = jnp.zeros_like(xb)
        gb[...] = jnp.zeros_like(gb)
        for i, ref in enumerate((gqkv_ref, gout_ref, gmisc_ref)):
            ref[...] = sums[i][...] if sums else jnp.zeros_like(ref)
        lnacc[...] = jnp.zeros_like(lnacc)

    firsts, needs, passes = windows(starts, base + b)
    lane = lanes((ROWS, 128))
    comb[...] = jnp.zeros_like(comb)

    def one_pass(p, carry):
        for e in range(E):
            begin = firsts[e] + p * WIN
            off = pl.multiple_of(jnp.minimum(begin, SLOTS - WIN), 16)
            rhs[WIN * e : WIN * e + WIN, :] = ys_ref[e, pl.ds(off, WIN), :]
            named = slot_ref[0, :, e : e + 1]
            ok = (named >= begin) & (named < begin + WIN)
            hit = jnp.where(ok, named - off, -1) == lane
            oh[:, WIN * e : WIN * e + WIN] = hit.astype(F32).astype(BF16)
        comb[...] += dot(oh[...], rhs[...])
        return carry

    lax.fori_loop(0, passes, one_pass, 0)

    middle = middle_ref[0]
    layer_ref[0] = (middle + comb[:, 0:D])[0:SEQ, :].astype(BF16)
    pg = comb[:, 2 * D : WIDE]
    rp = rp_ref[0]
    pg = jnp.where(lane < E, pg + pltpu.roll(pg, 128 - E, 1), 0.0)
    lg = (rp * (pg - jnp.sum(rp * pg, axis=-1, keepdims=True))).astype(BF16)
    n2, rs2 = norm_stats(middle)
    g2 = ln_ref[2:3, :]
    hidden = (n2 * g2 + ln_ref[3:4, :]).astype(BF16)
    gmisc_ref[...] += dot_tn(hidden, lg)
    hg = comb[:, D : 2 * D] + dot_nt(lg, rw_ref[...])
    gb[0:SEQ, :] = cot_ref[0].astype(F32)
    lnacc[10:11, :] += jnp.sum(hg * n2, axis=0, keepdims=True)
    lnacc[11:12, :] += jnp.sum(hg, axis=0, keepdims=True)
    mid_grad = gb[...] + norm_back(hg, n2, rs2, g2)
    bg = mid_grad.astype(BF16)
    gout_ref[...] += dot_tn(mixed_ref[0], bg)
    mg = dot_nt(bg, outw_ref[...]).astype(BF16)
    zero = jnp.zeros((ROWS, 128), BF16)
    keys = subs((ROWS, ROWS))
    for pair in range(HEADS // 2):
        lo = 128 * pair
        q = qkv_ref[0, :, lo : lo + 128]
        k = qkv_ref[0, :, D + lo : D + lo + 128]
        v = qkv_ref[0, :, 2 * D + lo : 2 * D + lo + 128]
        m = mg[:, lo : lo + 128]
        dq = dk = dv = None
        for half in range(2):
            mine = head_lane(half)
            kh = jnp.where(mine, k, zero)
            h = 2 * pair + half
            st = dot_nt(kh, q) * SCALE
            pt = jnp.where(keys < SEQ, jnp.exp(st - lse_ref[0, h : h + 1, :]), 0.0)
            dp = dot_nt(jnp.where(mine, v, zero), m)
            delta = jnp.sum(pt * dp, axis=0, keepdims=True)
            ds = (pt * (dp - delta)).astype(BF16)
            a = dot(pt.astype(BF16), jnp.where(mine, m, zero))
            c = dot(ds, jnp.where(mine, q, zero))
            d = dot_tn(ds, kh)
            dv = a if dv is None else dv + a
            dk = c if dk is None else dk + c
            dq = d if dq is None else dq + d
        qg[:, lo : lo + 128] = (dq * SCALE).astype(BF16)
        qg[:, D + lo : D + lo + 128] = (dk * SCALE).astype(BF16)
        qg[:, 2 * D + lo : 2 * D + lo + 128] = dv.astype(BF16)
    xb[0:SEQ, :] = img_ref[0].astype(F32)
    n1, rs1 = norm_stats(xb[...])
    g1 = ln_ref[0:1, :]
    normed = (n1 * g1 + ln_ref[1:2, :]).astype(BF16)
    gqkv_ref[...] += dot_tn(normed, qg[...])
    ng = dot_nt(qg[...], qkvw_ref[...])
    lnacc[8:9, :] += jnp.sum(ng * n1, axis=0, keepdims=True)
    lnacc[9:10, :] += jnp.sum(ng, axis=0, keepdims=True)
    ingrad_ref[0] = (mid_grad + norm_back(ng, n1, rs1, g1))[0:SEQ, :].astype(BF16)

    @pl.when(b == pl.num_programs(0) - 1)
    def _():
        gmisc_ref[...] += jnp.transpose(lnacc[...])


def back(base, count, starts, ys, slot, middle, images, cot, rp, mixed, qkv, lse, ln, qkvw, outw, rw, olds):
    whole = lambda shape: pl.BlockSpec(shape, lambda b, s: (0,) * len(shape), pipeline_mode=pl.Buffered(1))
    item = lambda *shape: pl.BlockSpec((1,) + shape, lambda b, s: (base + b,) + (0,) * len(shape))
    keep = pl.BlockSpec(memory_space=pl.ANY)

    def kernel(*refs):
        back_kernel(base, refs[16 : 14 + len(olds)], *refs[:14], *refs[14 + len(olds) :])

    return pl.pallas_call(
        kernel,
        grid_spec=pltpu.PrefetchScalarGridSpec(
            num_scalar_prefetch=1,
            grid=(count,),
            in_specs=[
                whole((E, SLOTS, WIDE)), item(ROWS, 128), item(ROWS, D), item(SEQ, D), item(SEQ, D), item(ROWS, AUX), item(ROWS, D),
                item(ROWS, 3 * D), item(HEADS, ROWS), whole((8, D)), whole((D, 3 * D)), whole((D, D)), whole((D, AUX)),
            ] + ([keep, keep, whole((D, 3 * D)), whole((D, D)), whole((D, AUX))] if olds else []),
            out_specs=[item(SEQ, D), item(SEQ, D), whole((D, 3 * D)), whole((D, D)), whole((D, AUX))],
            scratch_shapes=[
                pltpu.VMEM((ROWS, D), F32), pltpu.VMEM((ROWS, D), F32), pltpu.VMEM((E * WIN, WIDE), BF16),
                pltpu.VMEM((ROWS, E * WIN), BF16), pltpu.VMEM((ROWS, WIDE), F32), pltpu.VMEM((ROWS, 3 * D), BF16),
                pltpu.VMEM((AUX, D), F32),
            ],
        ),
        out_shape=(
            jax.ShapeDtypeStruct(images.shape, BF16),
            jax.ShapeDtypeStruct(images.shape, BF16),
            jax.ShapeDtypeStruct((D, 3 * D), F32),
            jax.ShapeDtypeStruct((D, D), F32),
            jax.ShapeDtypeStruct((D, AUX), F32),
        ),
        input_output_aliases={14 + i: i for i in range(len(olds))},
        compiler_params=params("arbitrary"),
        cost_estimate=cost(17),
        name="back",
    )(starts, ys, slot, middle, images, cot, rp, mixed, qkv, lse, ln, qkvw, outw, rw, *olds)


def place_kernel(ids, *refs):
    in_ref, out_ref = refs[-2:]
    hb = in_ref.shape[1]

    def put(win_ref, wout_ref):
        for q in range(4):
            in_ref[0, :, 512 * q : 512 * q + 512] = win_ref[q].astype(F32)
            out_ref[0, hb * q : hb * q + hb, :] = wout_ref[q].astype(F32)

    for i in range(2):
        pl.when(pl.program_id(0) == i)(functools.partial(put, *refs[2 * i : 2 * i + 2]))


def place(ids, a, b, gin, gout):
    hb = a[0].shape[1]
    quad = lambda at: pl.BlockSpec((4, hb, 512), lambda i, s: (at, 0, 0))
    keep = pl.BlockSpec(memory_space=pl.ANY)
    fresh = gin is None
    olds = () if fresh else (gin, gout)
    args = (a[0], a[-1], b[0], b[-1], *olds)
    last = 1 if len(a) == 1 else 0
    return pl.pallas_call(
        place_kernel,
        grid_spec=pltpu.PrefetchScalarGridSpec(
            num_scalar_prefetch=1,
            grid=(2,),
            in_specs=[quad(0), quad(last), quad(0), quad(last)] + [keep] * len(olds),
            out_specs=[
                pl.BlockSpec((1, hb, FF), lambda i, s: (s[i], 0, 0)),
                pl.BlockSpec((1, 4 * hb, D), lambda i, s: (s[i], 0, 0)),
            ],
        ),
        out_shape=[jax.ShapeDtypeStruct((E, hb, FF), F32), jax.ShapeDtypeStruct((E, 4 * hb, D), F32)],
        input_output_aliases={} if fresh else {5: 0, 6: 1},
        compiler_params=params("arbitrary"),
        cost_estimate=cost(7),
        name="place",
    )(ids, *args)


def swap(value, axis, size, bit, name):
    with jax.named_scope(name):
        return lax.ppermute(value, axis, [(i, i ^ (1 << bit)) for i in range(size)])


def halves(value, flag, axis):
    size = value.shape[axis] // 2
    mine = lax.dynamic_slice_in_dim(value, flag * size, size, axis)
    other = lax.dynamic_slice_in_dim(value, (1 - flag) * size, size, axis)
    return mine, other


def joined(mine, other, flag, axis):
    return jnp.where(flag == 0, jnp.concatenate([mine, other], axis), jnp.concatenate([other, mine], axis))


def add(a, b):
    return (a.astype(F32) + b.astype(F32)).astype(BF16)


def pack(win, wout):
    hb = win.shape[0]
    return jnp.concatenate([jnp.transpose(win.reshape(hb, 4, 512), (1, 0, 2)), wout.reshape(4, hb, 512)], axis=0)


def cut_kernel(ids, win_ref, wout_ref, out_ref):
    for q in range(4):
        out_ref[q] = win_ref[0, :, 512 * q : 512 * q + 512]
        out_ref[4 + q] = wout_ref[0, q]


def cut(expert, piece, size, win, wout):
    hb = win.shape[1]
    return pl.pallas_call(
        cut_kernel,
        grid_spec=pltpu.PrefetchScalarGridSpec(
            num_scalar_prefetch=1,
            grid=(1,),
            in_specs=[
                pl.BlockSpec((1, size, FF), lambda i, s: (s[0], s[1], 0)),
                pl.BlockSpec((1, 4, size, D), lambda i, s: (s[0], 0, s[1], 0)),
            ],
            out_specs=pl.BlockSpec((8, size, 512), lambda i, s: (0, 0, 0)),
        ),
        out_shape=jax.ShapeDtypeStruct((8, size, 512), BF16),
        compiler_params=params("arbitrary"),
        cost_estimate=cost(2),
        name="cut",
    )(jnp.stack([expert, piece]).astype(I32), win, wout.reshape(E, 4, hb, D))


def gather_kernel(ids, qkv_ref, out_ref, near_ref, far_ref, small_ref, qkvw_ref, outw_ref, ln_ref, rw_ref, work):
    grp = ids[0]
    core = ids[1]
    hb = qkv_ref.shape[0]
    part = hb // 2
    rows = lambda start, size: pl.ds(pl.multiple_of(start, 128), size)
    mine = grp * hb
    other = (1 - grp) * hb
    qkvw_ref[rows(mine, hb), :] = qkv_ref[...]
    outw_ref[rows(mine, hb), :] = out_ref[...]
    for ref, at in ((near_ref, other + core * part), (far_ref, other + (1 - core) * part)):
        qkvw_ref[rows(at, part), :] = ref[:, 0 : 3 * D]
        outw_ref[rows(at, part), :] = ref[:, 3 * D : 4 * D]
    ln_ref[...] = jnp.zeros_like(ln_ref)
    work[...] = jnp.zeros_like(work)
    lane = lanes((hb, AUX))
    for these, at in ((small_ref[...], mine), (near_ref[0:16, 4 * D :], other)):
        work[0:16, :] = these.astype(F32)
        ln_ref[0:4, rows(at, hb)] = work[0:4, :]
        router = pltpu.roll(jnp.transpose(work[...]), AUX - 4, 1)
        rw_ref[rows(at, hb), :] = jnp.where(lane < E, router, 0.0).astype(BF16)


def gathered(ids, qkv_weight, out_weight, near, far, small):
    return pl.pallas_call(
        gather_kernel,
        grid_spec=pltpu.PrefetchScalarGridSpec(
            num_scalar_prefetch=1,
            grid=(1,),
            in_specs=[pl.BlockSpec(a.shape, lambda i, s: (0, 0)) for a in (qkv_weight, out_weight, near, far, small)],
            out_specs=[pl.BlockSpec(shape, lambda i, s: (0, 0)) for shape in ((D, 3 * D), (D, D), (8, D), (D, AUX))],
            scratch_shapes=[pltpu.VMEM((AUX, qkv_weight.shape[0]), F32)],
        ),
        out_shape=[
            jax.ShapeDtypeStruct((D, 3 * D), BF16),
            jax.ShapeDtypeStruct((D, D), BF16),
            jax.ShapeDtypeStruct((8, D), F32),
            jax.ShapeDtypeStruct((D, AUX), BF16),
        ],
        compiler_params=params("arbitrary"),
        cost_estimate=cost(3),
        name="gathered",
    )(ids, qkv_weight, out_weight, near, far, small)


class Order:
    def __init__(self):
        self.last = None

    def __call__(self, *values):
        if self.last is None:
            return values
        return lax.optimization_barrier((*values, self.last))[:-1]

    def done(self, value):
        self.last = value
        return value

    def pass_on(self, value):
        (value,) = self(value)
        return self.done(value)


def per_device(
    reps, groups, images, ln1_gain, ln1_bias, qkv_weight, out_weight, ln2_gain, ln2_bias, router_weight, expert_in, expert_out, routes, cotangent
):
    rep = lax.axis_index("rep")
    grp = lax.axis_index("grp")
    bits = reps.bit_length() - 1
    rbit = [(rep >> i) & 1 for i in range(bits)]
    core = rbit[0]
    rswap = lambda value, bit, name: swap(value, "rep", reps, bit, f"{name}_rep{bit}")
    gswap = lambda value, name: swap(value, "grp", 2, 0, f"{name}_grp")
    pairs = groups == 2
    hb = expert_in.shape[1]
    order = Order()
    chunks = E // 2
    near_ids = [j + chunks * core for j in range(chunks)]
    far_ids = [j + chunks * (1 - core) for j in range(chunks)]
    spread = [bit for bit in (2, 1) if bit < bits]
    ways = [spread if j % 2 == 0 else spread[::-1] for j in range(chunks)]

    def first_cut(j):
        piece, size = 0, hb
        for bit in ways[j][::-1]:
            size = size // 2
            piece = piece * 2 + rbit[bit]
        win, wout = order(expert_in, expert_out)
        return order.done(cut(near_ids[j], piece, size, win, wout))

    weights = [None] * chunks
    step = [0] * chunks

    def weights_out(j):
        if not pairs:
            return
        at = step[j]
        step[j] += 1
        if at == 0:
            weights[j] = (None, gswap(first_cut(j), f"weights{j}"))
            return
        mine, other = weights[j]
        if at == 1:
            mine = order.pass_on(other)
        else:
            mine, other = order(mine, other)
            mine = order.done(joined(mine, other, rbit[ways[j][at - 2]], 1))
        weights[j] = (mine, rswap(mine, ways[j][at - 1], f"weights{j}") if at <= len(spread) else None)

    peak = [None, 0]
    last_peak = bits + groups.bit_length() - 1
    clipped = None

    def peak_more():
        nonlocal clipped
        value, at = peak
        if at > last_peak + 1:
            return
        if at > 0:
            value = order(*value)
            value = order.done(jnp.maximum(*value))
        if at < last_peak - bits:
            peak[0] = (value, swap(value, "grp", groups, at, "peak_grp"))
        elif at < last_peak:
            peak[0] = (value, rswap(value, at - (last_peak - bits), "peak"))
        else:
            clip = jnp.sqrt(CLIP_LIMIT / jnp.maximum(value[0, :HEADS], CLIP_LIMIT))
            column_scale = jnp.tile(jnp.repeat(clip, HEAD_DIM), 2)
            clipped = order.done(qkv_weight[:, : 2 * D].astype(F32) * column_scale[None, :])
            peak[1] = last_peak + 2
            return
        peak[1] += 1

    width = ln1_gain.shape[0]
    small = jnp.concatenate(
        [jnp.stack([ln1_gain, ln1_bias, ln2_gain, ln2_bias]), jnp.transpose(router_weight), jnp.zeros((4, width), BF16)], axis=0
    )
    win0, wout0 = expert_in, expert_out
    if pairs:
        weights_out(0)
        dense = [lax.dynamic_slice_in_dim(w, core * (hb // 2), hb // 2, 0) for w in order(qkv_weight, out_weight)]
        dense = jnp.concatenate([*dense, jnp.pad(small, ((0, hb // 2 - 16), (0, 0)))], axis=1)
        near = gswap(order.done(dense), "dense")
        for j in range(1, chunks):
            weights_out(j)
        slot, slot_t, starts = route_tables(*order(routes))
        order.done(starts)
        weights_out(0)
        near = order.pass_on(near)
        far = rswap(near, 0, "dense")
        weights_out(0)
        ids = jnp.stack([grp, core]).astype(I32)
        qkvw, outw, ln, rw = gathered(ids, qkv_weight, out_weight, *order(near, far, small))
        order.done(ln)
    else:
        dense = jnp.concatenate([qkv_weight, out_weight], axis=1)
        small = lax.all_gather(small, "grp", axis=1, tiled=True)
        dense = lax.all_gather(dense, "grp", axis=0, tiled=True)
        slot, slot_t, starts = route_tables(routes)
        ln = jnp.concatenate([small[0:4].astype(F32), jnp.zeros((4, D), F32)], axis=0)
        rw = jnp.pad(jnp.transpose(small[4 : 4 + E]), ((0, 0), (0, AUX - E)))
        qkvw = dense[:, : 3 * D]
        outw = dense[:, 3 * D :]
        win0 = lax.all_gather(expert_in, "grp", axis=1, tiled=True)
        wout0 = lax.all_gather(expert_out, "grp", axis=1, tiled=True)
        weights = [(None, None)] * chunks

    (ln,) = order(ln)
    qkv, mixed, middle, rp, lse, hmax, slots = front(starts, images, cotangent, slot_t, ln, qkvw, outw, rw)
    peak[0] = order.done(hmax)

    couples = [[i, i + 1] for i in range(0, reps, 2)]

    def between_cores(value, name):
        (value,) = order(value)
        with jax.named_scope(name):
            return order.done(lax.all_to_all(value, "rep", 0, 0, axis_index_groups=couples, tiled=True))

    state = {}

    def expert(j):
        nonlocal slots
        ids = jnp.stack([near_ids[j], grp, j]).astype(I32)
        (held,) = order(slots)
        slots, *grads = expert_call(ids, held, win0, wout0, weights[j][0])
        order.done(grads[0])
        if pairs:
            state[j] = (0, grads[0], gswap(grads[1], f"grad{j}"))
        else:
            full = grads[0]
            gin = lax.psum_scatter(jnp.transpose(full[0:4], (1, 0, 2)).reshape(D, FF), "grp", scatter_dimension=0, tiled=True)
            gout = lax.psum_scatter(full[4:8].reshape(FF, D), "grp", scatter_dimension=0, tiled=True)
            part = pack(gin, gout)
            state[j] = (0, part, jnp.zeros_like(part))

    down = list(range(1, bits))
    up = down[::-1] + [0]
    placed = [None, None]
    ends = len(down) + len(up)

    def more(j):
        at, keep, recv = state[j]
        if at > ends:
            return
        keep, recv = order(keep, recv)
        n = len(down)
        if at < n:
            bit = down[at]
            keep_mine, keep_other = halves(keep, rbit[bit], 1)
            recv_mine, recv_other = halves(recv, rbit[bit], 1)
            send = add(keep_other, recv_other)
            keep = order.done(add(keep_mine, recv_mine))
            state[j] = (at + 1, keep, rswap(send, bit, f"grad{j}_down"))
        elif at < ends:
            bit = up[at - n]
            total = add(keep, recv) if at == n else joined(keep, recv, rbit[up[at - n - 1]], 1)
            order.done(total)
            state[j] = (at + 1, total, rswap(total, bit, f"grad{j}_up"))
        else:
            ids = jnp.stack([near_ids[j], far_ids[j]]).astype(I32)
            placed[0], placed[1] = place(ids, [keep], [recv], placed[0], placed[1])
            order.done(placed[0])
            state[j] = (at + 1, None, None)

    peak_more()
    weights_out(1)
    weights_out(2)
    weights_out(3)
    slots = between_cores(slots.reshape(2, chunks, SLOTS, WIDE), "slots")
    weights_out(0)
    weights_out(1)
    weights_out(2)
    peak_more()
    expert(0)
    weights_out(1)
    weights_out(3)
    peak_more()
    expert(1)
    weights_out(2)
    peak_more()
    expert(2)
    weights_out(3)
    more(0)
    peak_more()
    expert(3)
    more(0)
    more(1)
    peak_more()
    slots = between_cores(slots, "results").reshape(E, SLOTS, WIDE)
    while clipped is None:
        peak_more()
    more(2)
    more(1)
    more(0)

    n = images.shape[0]
    parts = 4
    outs, accs = [], []
    between = [
        [lambda: more(0), lambda: more(1)],
        [lambda: more(3), lambda: more(2), lambda: more(0), lambda: more(1)],
        [lambda: more(0), lambda: more(3), lambda: more(2)],
        [],
    ]
    for i in range(parts):
        (held,) = order(slots)
        *outs, gqkv, gout, gmisc = back(
            i * (n // parts), n // parts, starts, held, slot, middle, images, cotangent, rp, mixed, qkv, lse, ln, qkvw, outw, rw, [*outs, *accs]
        )
        order.done(gmisc)
        accs = [gqkv, gout, gmisc]
        for step in between[i]:
            step()

    dense_at = [0]
    acc = jnp.concatenate(order(*accs), axis=1).astype(BF16)
    dense_state = [acc.reshape(groups, D // groups, -1), None]
    final = None

    def dense_more():
        nonlocal final
        at = dense_at[0]
        dense_at[0] += 1
        keep, recv = dense_state
        n = len(down)
        if at == 0:
            (keep,) = order(keep)
            mine, send = halves(keep, core, 1)
            order.done(send)
            dense_state[:] = [mine, rswap(send, 0, "dense_down")]
        elif at == 1:
            total = order.done(add(*order(keep, recv)))
            if pairs:
                mine = lax.dynamic_slice_in_dim(total, grp, 1, 0)[0]
                send = lax.dynamic_slice_in_dim(total, 1 - grp, 1, 0)[0]
                dense_state[:] = [mine, gswap(send, "dense_down")]
            else:
                total = lax.psum_scatter(total, "grp", scatter_dimension=0, tiled=True)[0]
                dense_state[:] = [total, jnp.zeros_like(total)]
        elif at < 2 + n:
            total = order.done(add(*order(keep, recv)))
            bit = down[at - 2]
            mine, send = halves(total, rbit[bit], 0)
            dense_state[:] = [mine, rswap(send, bit, "dense_down")]
        elif at < 2 + n + len(up):
            bit = up[at - 2 - n]
            keep, recv = order(keep, recv)
            total = add(keep, recv) if at == 2 + n else joined(keep, recv, rbit[up[at - 3 - n]], 0)
            dense_state[:] = [order.done(total), rswap(total, bit, "dense_up")]
        elif at == 2 + n + len(up):
            total = joined(*order(keep, recv), core, 0).astype(F32)
            misc = total[:, 4 * D :]
            final = (
                misc[:, 8], misc[:, 9], total[:, : 3 * D], total[:, 3 * D : 4 * D], misc[:, 10], misc[:, 11], misc[:, :E],
            )
            order.done(final[2])

    for key in (3, 1, 0, 2, -1, -1, 3, 0, -1, 1, -1, 2, 3, -1, 1, 2, -1, 1, 3, -1, 2, -1, 3, -1, 2, -1, 3, -1, 3):
        if key >= 0:
            more(key)
        elif final is None:
            dense_more()
    while any(state[key][0] <= ends for key in state):
        for key in state:
            more(key)
    while final is None:
        dense_more()
    return (outs[0], outs[1], clipped, *final, placed[0], placed[1])


def solution(mesh):
    rows = P(("rep", "grp"), None, None)
    line = P("grp")
    table = P("grp", None)
    cube = P(None, "grp", None)
    in_specs = (rows, line, line, table, table, line, line, table, cube, cube, rows, rows)
    out_specs = (rows, rows, table, line, line, table, table, line, line, table, cube, cube)
    body = functools.partial(per_device, mesh.shape["rep"], mesh.shape["grp"])
    return jax.shard_map(body, mesh=mesh, in_specs=in_specs, out_specs=out_specs, check_vma=False)
```

```python
import functools
import math

import jax
import jax.numpy as jnp
from jax import lax
from jax.experimental import pallas as pl
from jax.experimental.pallas import tpu as pltpu
from jax.sharding import PartitionSpec as P

D = 512
HEADS = 8
HEAD_DIM = 64
FF = 2048
E = 8
TOP = 2
SEQ = 197
CAP = 591
ROWS = 208
SLOTS = 640
WIN = 128
AUX = 128
WIDE = 2 * D + AUX
NORM_EPS = 1e-06
CLIP_LIMIT = 3.0
SCALE = HEAD_DIM ** (-0.5)
LOW = -1e30
F32 = jnp.float32
BF16 = jnp.bfloat16
I32 = jnp.int32


def dot(a, b):
    return lax.dot_general(a, b, (((1,), (0,)), ((), ())), preferred_element_type=F32)


def dot_nt(a, b):
    return lax.dot_general(a, b, (((1,), (1,)), ((), ())), preferred_element_type=F32)


def dot_tn(a, b):
    return lax.dot_general(a, b, (((0,), (0,)), ((), ())), preferred_element_type=F32)


def params(*semantics):
    return pltpu.CompilerParams(dimension_semantics=semantics, vmem_limit_bytes=60 * 1024 * 1024)


def cost(us):
    return pl.CostEstimate(flops=int(us * 4.5e+08), transcendentals=0, bytes_accessed=1)


def lanes(shape):
    return lax.broadcasted_iota(I32, shape, len(shape) - 1)


def subs(shape):
    return lax.broadcasted_iota(I32, shape, len(shape) - 2)


def route_kernel(routes_ref, slot_ref, slot_t_ref, starts_ref, work):
    images = routes_ref.shape[0]
    lane = lanes((ROWS, 128))
    strict = (lanes((ROWS, ROWS)) < subs((ROWS, ROWS))).astype(BF16)
    work[...] = jnp.full_like(work, -100)
    hots = []
    befores = []
    run = jnp.zeros((1, 128), F32)
    for b in range(images):
        work[0:SEQ, 0:TOP] = routes_ref[b]
        both = work[...]
        hot = ((both[:, 0:1] == lane) & (lane < E)) | (both[:, 1:2] + E == lane) & (lane >= E) & (lane < 2 * E)
        hot = hot.astype(F32)
        hots.append(hot)
        befores.append(dot(strict, hot.astype(BF16)) + run)
        run = run + jnp.sum(hot, axis=0, keepdims=True)
    first = jnp.where(lanes((1, 128)) < E, run, 0.0)
    shift = pltpu.roll(first, E, 1)
    base = jnp.zeros((1, 128), F32)
    starts = jnp.zeros((16, 128), F32)
    row = subs((16, 128))
    for b in range(images):
        kept = jnp.where(befores[b] + shift < CAP, hots[b], 0.0)
        kept = kept + pltpu.roll(kept, 128 - E, 1)
        kept = jnp.where(lane < E, kept, 0.0)
        place = dot(strict, kept.astype(BF16)) + base
        slot = jnp.where(kept > 0.0, place, -1000.0)
        slot_ref[b] = slot.astype(I32)
        slot_t_ref[b] = jnp.transpose(slot)[0:E, :].astype(I32)
        starts = jnp.where(row == b, base, starts)
        base = base + jnp.sum(kept, axis=0, keepdims=True)
    starts_ref[...] = jnp.where(row == images, base, starts).astype(I32)


def route_tables(routes):
    images = routes.shape[0]
    return pl.pallas_call(
        route_kernel,
        out_shape=(
            jax.ShapeDtypeStruct((images, ROWS, 128), I32),
            jax.ShapeDtypeStruct((images, E, ROWS), I32),
            jax.ShapeDtypeStruct((16, 128), I32),
        ),
        scratch_shapes=[pltpu.VMEM((ROWS, 128), I32)],
        compiler_params=params(),
        cost_estimate=cost(4),
        name="routing",
    )(routes)


def windows(starts, b):
    firsts, needs = [], []
    passes = jnp.int32(0)
    for e in range(E):
        start = starts[b, e]
        first = (start // 16) * 16
        need = starts[b + 1, e] - first
        firsts.append(first)
        needs.append(need)
        passes = jnp.maximum(passes, (need + WIN - 1) // WIN)
    return firsts, needs, passes


def norm_stats(rows):
    center = jnp.mean(rows, axis=-1, keepdims=True)
    spread = rows - center
    rs = lax.rsqrt(jnp.mean(spread * spread, axis=-1, keepdims=True) + NORM_EPS)
    return spread * rs, rs


def head_lane(half):
    lane = lanes((ROWS, 128))
    return (lane < HEAD_DIM) if half == 0 else (lane >= HEAD_DIM)


def front_kernel(
    starts, img_ref, cot_ref, slot_t_ref, ln_ref, qkvw_ref, outw_ref, rw_ref,
    qkv_ref, mixed_ref, middle_ref, rp_ref, lse_ref, hmax_ref, slots_ref,
    xb, rhs, oh,
):
    b = pl.program_id(0)

    @pl.when(b == 0)
    def _():
        xb[...] = jnp.zeros_like(xb)
        rhs[...] = jnp.zeros_like(rhs)
        slots_ref[...] = jnp.zeros_like(slots_ref)
        hmax_ref[...] = jnp.full_like(hmax_ref, LOW)

    xb[0:SEQ, :] = img_ref[0].astype(F32)
    x = xb[...]
    n1, _ = norm_stats(x)
    normed = (n1 * ln_ref[0:1, :] + ln_ref[1:2, :]).astype(BF16)
    qkv = dot(normed, qkvw_ref[...]).astype(BF16)
    qkv_ref[0] = qkv
    zero = jnp.zeros((ROWS, 128), BF16)
    cols = lanes((ROWS, ROWS))
    real = subs((ROWS, 1)) < SEQ
    lane = lanes((ROWS, 128))
    lse_all = jnp.zeros((ROWS, 128), F32)
    peaks = jnp.full((ROWS, 128), LOW, F32)
    parts = []
    for pair in range(HEADS // 2):
        q = qkv[:, 128 * pair : 128 * pair + 128]
        k = qkv[:, D + 128 * pair : D + 128 * pair + 128]
        v = qkv[:, 2 * D + 128 * pair : 2 * D + 128 * pair + 128]
        total = None
        for half in range(2):
            mine = head_lane(half)
            s = dot_nt(q, jnp.where(mine, k, zero)) * SCALE
            s = jnp.where(cols < SEQ, s, LOW)
            top = jnp.max(s, axis=-1, keepdims=True)
            powers = jnp.exp(s - top)
            norm = jnp.sum(powers, axis=-1, keepdims=True)
            probs = (powers / norm).astype(BF16)
            part = dot(probs, jnp.where(mine, v, zero))
            total = part if total is None else total + part
            h = 2 * pair + half
            lse_all = jnp.where(lane == h, top + jnp.log(norm), lse_all)
            peaks = jnp.where((lane == h) & real, top, peaks)
        parts.append(total.astype(BF16))
    mixed = jnp.concatenate(parts, axis=1)
    mixed_ref[0] = mixed
    lse_ref[0] = jnp.transpose(lse_all)[0:HEADS, :]
    hmax_ref[...] = jnp.maximum(hmax_ref[...], jnp.max(peaks, axis=0, keepdims=True))
    middle = x + dot(mixed, outw_ref[...])
    middle_ref[0] = middle
    n2, _ = norm_stats(middle)
    hidden = (n2 * ln_ref[2:3, :] + ln_ref[3:4, :]).astype(BF16)
    logits = jnp.where(lane < E, dot(hidden, rw_ref[...]), LOW)
    powers = jnp.exp(logits - jnp.max(logits, axis=-1, keepdims=True))
    rp = powers / jnp.sum(powers, axis=-1, keepdims=True)
    rp_ref[0] = rp
    high = rp.astype(BF16).astype(F32)
    rhs[:, 0:D] = hidden
    rhs[0:SEQ, D : 2 * D] = cot_ref[0]
    rhs[:, 2 * D : WIDE] = (high + pltpu.roll(rp - high, E, 1)).astype(BF16)

    firsts, needs, passes = windows(starts, b)
    place = subs((WIN, ROWS))

    def one_pass(p, carry):
        offs = []
        for e in range(E):
            begin = firsts[e] + p * WIN
            off = pl.multiple_of(jnp.minimum(begin, SLOTS - WIN), 16)
            offs.append(off)
            named = slot_t_ref[0, e : e + 1, :]
            ok = (named >= begin) & (named < begin + WIN)
            hit = jnp.where(ok, named - off, -1) == place
            oh[WIN * e : WIN * e + WIN, :] = hit.astype(F32).astype(BF16)
        picked = dot(oh[...], rhs[...]).astype(BF16)
        for e in range(E):

            @pl.when(p * WIN < needs[e])
            def _():
                slots_ref[e, pl.ds(offs[e], WIN), :] += picked[WIN * e : WIN * e + WIN, :]

        return carry

    lax.fori_loop(0, passes, one_pass, 0)


def front(starts, images, cot, slot_t, ln, qkvw, outw, rw):
    n = images.shape[0]
    whole = lambda shape: pl.BlockSpec(shape, lambda b, s: (0,) * len(shape), pipeline_mode=pl.Buffered(1))
    item = lambda *shape: pl.BlockSpec((1,) + shape, lambda b, s: (b,) + (0,) * len(shape))
    return pl.pallas_call(
        front_kernel,
        grid_spec=pltpu.PrefetchScalarGridSpec(
            num_scalar_prefetch=1,
            grid=(n,),
            in_specs=[
                item(SEQ, D), item(SEQ, D), item(E, ROWS), whole((8, D)), whole((D, 3 * D)), whole((D, D)), whole((D, AUX)),
            ],
            out_specs=[
                item(ROWS, 3 * D), item(ROWS, D), item(ROWS, D), item(ROWS, AUX), item(HEADS, ROWS),
                whole((1, 128)), whole((E, SLOTS, WIDE)),
            ],
            scratch_shapes=[
                pltpu.VMEM((ROWS, D), F32), pltpu.VMEM((ROWS, WIDE), BF16), pltpu.VMEM((E * WIN, ROWS), BF16),
            ],
        ),
        out_shape=(
            jax.ShapeDtypeStruct((n, ROWS, 3 * D), BF16),
            jax.ShapeDtypeStruct((n, ROWS, D), BF16),
            jax.ShapeDtypeStruct((n, ROWS, D), F32),
            jax.ShapeDtypeStruct((n, ROWS, AUX), F32),
            jax.ShapeDtypeStruct((n, HEADS, ROWS), F32),
            jax.ShapeDtypeStruct((1, 128), F32),
            jax.ShapeDtypeStruct((E, SLOTS, WIDE), BF16),
        ),
        compiler_params=params("arbitrary"),
        cost_estimate=cost(40),
        name="front",
    )(starts, images, cot, slot_t, ln, qkvw, outw, rw)


def gelu_parts(pre):
    c = math.sqrt(2.0 / math.pi)
    sq = pre * pre
    t = jnp.tanh(c * pre * (1.0 + 0.044715 * sq))
    half = 0.5 * (1.0 + t)
    act = pre * half
    slope = half + 0.5 * pre * (1.0 - t * t) * (c * (1.0 + 3.0 * 0.044715 * sq))
    return act, slope


def expert_kernel(nb, ids, slots_ref, win0_ref, wout0_ref, *refs):
    refs = list(refs)
    other_ref = refs.pop(0) if nb == 2 else None
    out_ref = refs.pop(0)
    act_s, preg_s, view = refs[-3:]
    grads = refs[:-3]
    for c in range(2):
        view[SLOTS * c : SLOTS * c + SLOTS, :] = slots_ref[c, 0]
    e = ids[0]
    me = ids[1]
    hb = win0_ref.shape[1]
    spot = [me, 1 - me] if nb == 2 else [0]

    def at(ref, start, size):
        if isinstance(start, int):
            return ref[:, start : start + size]
        return ref[:, pl.ds(pl.multiple_of(start, 128), size)]

    def win(r, q):
        return win0_ref[0, :, 512 * q : 512 * q + 512] if r == 0 else other_ref[q]

    def win_cols(r, start):
        if isinstance(start, int):
            return win0_ref[0, :, start : start + hb]
        if r == 0:
            return win0_ref[0, :, pl.ds(pl.multiple_of(start, 128), hb)]
        return other_ref[start // 512, :, pl.ds(pl.multiple_of(start % 512, 128), hb)]

    def wout(r, q):
        return wout0_ref[0, hb * q : hb * q + hb, :] if r == 0 else other_ref[4 + q]

    hid = [at(view, spot[r] * hb, hb) for r in range(nb)]
    got = view[:, D : 2 * D].astype(F32)
    aux = view[:, 2 * D : WIDE].astype(F32)
    lane = lanes((2 * SLOTS, AUX))
    gate = jnp.sum(jnp.where((lane == e) | (lane == e + E), aux, 0.0), axis=-1, keepdims=True)
    resg = (gate * got).astype(BF16)
    for r in range(nb):
        for q in range(4):
            start = spot[r] * (4 * hb) + q * hb
            pre = dot(hid[0], win_cols(0, start))
            for o in range(1, nb):
                pre = pre + dot(hid[o], win_cols(o, start))
            act, slope = gelu_parts(pre)
            actg = dot_nt(resg, wout(r, q))
            if isinstance(start, int):
                act_s[:, start : start + hb] = act.astype(BF16)
                preg_s[:, start : start + hb] = (actg * slope).astype(BF16)
            else:
                act_s[:, pl.ds(pl.multiple_of(start, 128), hb)] = act.astype(BF16)
                preg_s[:, pl.ds(pl.multiple_of(start, 128), hb)] = (actg * slope).astype(BF16)
    res = None
    for r in range(nb):
        for q in range(4):
            part = dot(at(act_s, spot[r] * (4 * hb) + q * hb, hb), wout(r, q))
            res = part if res is None else res + part
    gg = jnp.sum(got * res, axis=-1, keepdims=True)
    high = gg.astype(BF16).astype(F32)
    gg = jnp.where(lane == e, high, jnp.where(lane == e + E, gg - high, 0.0)).astype(BF16)
    res = (gate * res).astype(BF16)
    for c in range(2):
        out_ref[c, 0, :, 0:D] = res[SLOTS * c : SLOTS * c + SLOTS]
        out_ref[c, 0, :, 2 * D : WIDE] = gg[SLOTS * c : SLOTS * c + SLOTS]
    for r in range(nb):
        back = None
        for q in range(4):
            part = dot_nt(preg_s[:, 512 * q : 512 * q + 512], win(r, q))
            back = part if back is None else back + part
        back = back.astype(BF16)
        for c in range(2):
            if nb == 1:
                out_ref[c, 0, :, D : 2 * D] = back[SLOTS * c : SLOTS * c + SLOTS]
            else:
                out_ref[c, 0, :, pl.ds(pl.multiple_of(D + spot[r] * hb, 128), hb)] = back[SLOTS * c : SLOTS * c + SLOTS]
    for r in range(nb):
        for q in range(4):
            gin = dot_tn(hid[r], preg_s[:, 512 * q : 512 * q + 512])
            gout = dot_tn(at(act_s, spot[r] * (4 * hb) + q * hb, hb), resg)
            grads[r][q] = gin.astype(BF16)
            grads[r][4 + q] = gout.astype(BF16)


def expert_call(ids, slots, win0, wout0, other):
    nb = 1 if other is None else 2
    hb = win0.shape[1]
    once = pl.BlockSpec((8, hb, 512), lambda i, s: (0, 0, 0))
    both = pl.BlockSpec((2, 1, SLOTS, WIDE), lambda i, s: (0, s[2], 0, 0))
    pick = lambda *shape: pl.BlockSpec((1,) + shape, lambda i, s: (s[0],) + (0,) * len(shape))
    return pl.pallas_call(
        functools.partial(expert_kernel, nb),
        grid_spec=pltpu.PrefetchScalarGridSpec(
            num_scalar_prefetch=1,
            grid=(1,),
            in_specs=[both, pick(hb, FF), pick(4 * hb, D)] + [once] * (nb == 2),
            out_specs=[both] + [once] * nb,
            scratch_shapes=[
                pltpu.VMEM((2 * SLOTS, FF), BF16), pltpu.VMEM((2 * SLOTS, FF), BF16), pltpu.VMEM((2 * SLOTS, WIDE), BF16),
            ],
        ),
        out_shape=[jax.ShapeDtypeStruct(slots.shape, BF16)] + [jax.ShapeDtypeStruct((8, hb, 512), BF16)] * nb,
        input_output_aliases={1: 0},
        compiler_params=params("arbitrary"),
        cost_estimate=cost(31),
        name="expert",
    )(ids, slots, win0, wout0, *([other] if nb == 2 else []))


def norm_back(grad, n, rs, gain):
    u = grad * gain
    return rs * (u - jnp.mean(u, axis=-1, keepdims=True) - n * jnp.mean(u * n, axis=-1, keepdims=True))


def back_kernel(
    base, sums, starts, ys_ref, slot_ref, middle_ref, img_ref, cot_ref, rp_ref, mixed_ref, qkv_ref, lse_ref, ln_ref, qkvw_ref, outw_ref, rw_ref,
    layer_ref, ingrad_ref, gqkv_ref, gout_ref, gmisc_ref,
    xb, gb, rhs, oh, comb, qg, lnacc,
):
    b = pl.program_id(0)

    @pl.when(b == 0)
    def _():
        xb[...] = jnp.zeros_like(xb)
        gb[...] = jnp.zeros_like(gb)
        for i, ref in enumerate((gqkv_ref, gout_ref, gmisc_ref)):
            ref[...] = sums[i][...] if sums else jnp.zeros_like(ref)
        lnacc[...] = jnp.zeros_like(lnacc)

    firsts, needs, passes = windows(starts, base + b)
    lane = lanes((ROWS, 128))
    comb[...] = jnp.zeros_like(comb)

    def one_pass(p, carry):
        for e in range(E):
            begin = firsts[e] + p * WIN
            off = pl.multiple_of(jnp.minimum(begin, SLOTS - WIN), 16)
            rhs[WIN * e : WIN * e + WIN, :] = ys_ref[e, pl.ds(off, WIN), :]
            named = slot_ref[0, :, e : e + 1]
            ok = (named >= begin) & (named < begin + WIN)
            hit = jnp.where(ok, named - off, -1) == lane
            oh[:, WIN * e : WIN * e + WIN] = hit.astype(F32).astype(BF16)
        comb[...] += dot(oh[...], rhs[...])
        return carry

    lax.fori_loop(0, passes, one_pass, 0)

    middle = middle_ref[0]
    layer_ref[0] = (middle + comb[:, 0:D])[0:SEQ, :].astype(BF16)
    pg = comb[:, 2 * D : WIDE]
    rp = rp_ref[0]
    pg = jnp.where(lane < E, pg + pltpu.roll(pg, 128 - E, 1), 0.0)
    lg = (rp * (pg - jnp.sum(rp * pg, axis=-1, keepdims=True))).astype(BF16)
    n2, rs2 = norm_stats(middle)
    g2 = ln_ref[2:3, :]
    hidden = (n2 * g2 + ln_ref[3:4, :]).astype(BF16)
    gmisc_ref[...] += dot_tn(hidden, lg)
    hg = comb[:, D : 2 * D] + dot_nt(lg, rw_ref[...])
    gb[0:SEQ, :] = cot_ref[0].astype(F32)
    lnacc[10:11, :] += jnp.sum(hg * n2, axis=0, keepdims=True)
    lnacc[11:12, :] += jnp.sum(hg, axis=0, keepdims=True)
    mid_grad = gb[...] + norm_back(hg, n2, rs2, g2)
    bg = mid_grad.astype(BF16)
    gout_ref[...] += dot_tn(mixed_ref[0], bg)
    mg = dot_nt(bg, outw_ref[...]).astype(BF16)
    zero = jnp.zeros((ROWS, 128), BF16)
    keys = subs((ROWS, ROWS))
    for pair in range(HEADS // 2):
        lo = 128 * pair
        q = qkv_ref[0, :, lo : lo + 128]
        k = qkv_ref[0, :, D + lo : D + lo + 128]
        v = qkv_ref[0, :, 2 * D + lo : 2 * D + lo + 128]
        m = mg[:, lo : lo + 128]
        dq = dk = dv = None
        for half in range(2):
            mine = head_lane(half)
            kh = jnp.where(mine, k, zero)
            h = 2 * pair + half
            st = dot_nt(kh, q) * SCALE
            pt = jnp.where(keys < SEQ, jnp.exp(st - lse_ref[0, h : h + 1, :]), 0.0)
            dp = dot_nt(jnp.where(mine, v, zero), m)
            delta = jnp.sum(pt * dp, axis=0, keepdims=True)
            ds = (pt * (dp - delta)).astype(BF16)
            a = dot(pt.astype(BF16), jnp.where(mine, m, zero))
            c = dot(ds, jnp.where(mine, q, zero))
            d = dot_tn(ds, kh)
            dv = a if dv is None else dv + a
            dk = c if dk is None else dk + c
            dq = d if dq is None else dq + d
        qg[:, lo : lo + 128] = (dq * SCALE).astype(BF16)
        qg[:, D + lo : D + lo + 128] = (dk * SCALE).astype(BF16)
        qg[:, 2 * D + lo : 2 * D + lo + 128] = dv.astype(BF16)
    xb[0:SEQ, :] = img_ref[0].astype(F32)
    n1, rs1 = norm_stats(xb[...])
    g1 = ln_ref[0:1, :]
    normed = (n1 * g1 + ln_ref[1:2, :]).astype(BF16)
    gqkv_ref[...] += dot_tn(normed, qg[...])
    ng = dot_nt(qg[...], qkvw_ref[...])
    lnacc[8:9, :] += jnp.sum(ng * n1, axis=0, keepdims=True)
    lnacc[9:10, :] += jnp.sum(ng, axis=0, keepdims=True)
    ingrad_ref[0] = (mid_grad + norm_back(ng, n1, rs1, g1))[0:SEQ, :].astype(BF16)

    @pl.when(b == pl.num_programs(0) - 1)
    def _():
        gmisc_ref[...] += jnp.transpose(lnacc[...])


def back(base, count, starts, ys, slot, middle, images, cot, rp, mixed, qkv, lse, ln, qkvw, outw, rw, olds):
    whole = lambda shape: pl.BlockSpec(shape, lambda b, s: (0,) * len(shape), pipeline_mode=pl.Buffered(1))
    item = lambda *shape: pl.BlockSpec((1,) + shape, lambda b, s: (base + b,) + (0,) * len(shape))
    keep = pl.BlockSpec(memory_space=pl.ANY)

    def kernel(*refs):
        back_kernel(base, refs[16 : 14 + len(olds)], *refs[:14], *refs[14 + len(olds) :])

    return pl.pallas_call(
        kernel,
        grid_spec=pltpu.PrefetchScalarGridSpec(
            num_scalar_prefetch=1,
            grid=(count,),
            in_specs=[
                whole((E, SLOTS, WIDE)), item(ROWS, 128), item(ROWS, D), item(SEQ, D), item(SEQ, D), item(ROWS, AUX), item(ROWS, D),
                item(ROWS, 3 * D), item(HEADS, ROWS), whole((8, D)), whole((D, 3 * D)), whole((D, D)), whole((D, AUX)),
            ] + ([keep, keep, whole((D, 3 * D)), whole((D, D)), whole((D, AUX))] if olds else []),
            out_specs=[item(SEQ, D), item(SEQ, D), whole((D, 3 * D)), whole((D, D)), whole((D, AUX))],
            scratch_shapes=[
                pltpu.VMEM((ROWS, D), F32), pltpu.VMEM((ROWS, D), F32), pltpu.VMEM((E * WIN, WIDE), BF16),
                pltpu.VMEM((ROWS, E * WIN), BF16), pltpu.VMEM((ROWS, WIDE), F32), pltpu.VMEM((ROWS, 3 * D), BF16),
                pltpu.VMEM((AUX, D), F32),
            ],
        ),
        out_shape=(
            jax.ShapeDtypeStruct(images.shape, BF16),
            jax.ShapeDtypeStruct(images.shape, BF16),
            jax.ShapeDtypeStruct((D, 3 * D), F32),
            jax.ShapeDtypeStruct((D, D), F32),
            jax.ShapeDtypeStruct((D, AUX), F32),
        ),
        input_output_aliases={14 + i: i for i in range(len(olds))},
        compiler_params=params("arbitrary"),
        cost_estimate=cost(17),
        name="back",
    )(starts, ys, slot, middle, images, cot, rp, mixed, qkv, lse, ln, qkvw, outw, rw, *olds)


def place_kernel(ids, *refs):
    in_ref, out_ref = refs[-2:]
    hb = in_ref.shape[1]

    def put(win_ref, wout_ref):
        for q in range(4):
            in_ref[0, :, 512 * q : 512 * q + 512] = win_ref[q].astype(F32)
            out_ref[0, hb * q : hb * q + hb, :] = wout_ref[q].astype(F32)

    for i in range(2):
        pl.when(pl.program_id(0) == i)(functools.partial(put, *refs[2 * i : 2 * i + 2]))


def place(ids, a, b, gin, gout):
    hb = a[0].shape[1]
    quad = lambda at: pl.BlockSpec((4, hb, 512), lambda i, s: (at, 0, 0))
    keep = pl.BlockSpec(memory_space=pl.ANY)
    fresh = gin is None
    olds = () if fresh else (gin, gout)
    args = (a[0], a[-1], b[0], b[-1], *olds)
    last = 1 if len(a) == 1 else 0
    return pl.pallas_call(
        place_kernel,
        grid_spec=pltpu.PrefetchScalarGridSpec(
            num_scalar_prefetch=1,
            grid=(2,),
            in_specs=[quad(0), quad(last), quad(0), quad(last)] + [keep] * len(olds),
            out_specs=[
                pl.BlockSpec((1, hb, FF), lambda i, s: (s[i], 0, 0)),
                pl.BlockSpec((1, 4 * hb, D), lambda i, s: (s[i], 0, 0)),
            ],
        ),
        out_shape=[jax.ShapeDtypeStruct((E, hb, FF), F32), jax.ShapeDtypeStruct((E, 4 * hb, D), F32)],
        input_output_aliases={} if fresh else {5: 0, 6: 1},
        compiler_params=params("arbitrary"),
        cost_estimate=cost(7),
        name="place",
    )(ids, *args)


def swap(value, axis, size, bit, name):
    with jax.named_scope(name):
        return lax.ppermute(value, axis, [(i, i ^ (1 << bit)) for i in range(size)])


def halves(value, flag, axis):
    size = value.shape[axis] // 2
    mine = lax.dynamic_slice_in_dim(value, flag * size, size, axis)
    other = lax.dynamic_slice_in_dim(value, (1 - flag) * size, size, axis)
    return mine, other


def joined(mine, other, flag, axis):
    return jnp.where(flag == 0, jnp.concatenate([mine, other], axis), jnp.concatenate([other, mine], axis))


def add(a, b):
    return (a.astype(F32) + b.astype(F32)).astype(BF16)


def pack(win, wout):
    hb = win.shape[0]
    return jnp.concatenate([jnp.transpose(win.reshape(hb, 4, 512), (1, 0, 2)), wout.reshape(4, hb, 512)], axis=0)


def cut_kernel(ids, win_ref, wout_ref, out_ref):
    for q in range(4):
        out_ref[q] = win_ref[0, :, 512 * q : 512 * q + 512]
        out_ref[4 + q] = wout_ref[0, q]


def cut(expert, piece, size, win, wout):
    hb = win.shape[1]
    return pl.pallas_call(
        cut_kernel,
        grid_spec=pltpu.PrefetchScalarGridSpec(
            num_scalar_prefetch=1,
            grid=(1,),
            in_specs=[
                pl.BlockSpec((1, size, FF), lambda i, s: (s[0], s[1], 0)),
                pl.BlockSpec((1, 4, size, D), lambda i, s: (s[0], 0, s[1], 0)),
            ],
            out_specs=pl.BlockSpec((8, size, 512), lambda i, s: (0, 0, 0)),
        ),
        out_shape=jax.ShapeDtypeStruct((8, size, 512), BF16),
        compiler_params=params("arbitrary"),
        cost_estimate=cost(2),
        name="cut",
    )(jnp.stack([expert, piece]).astype(I32), win, wout.reshape(E, 4, hb, D))


def gather_kernel(ids, qkv_ref, out_ref, near_ref, far_ref, small_ref, qkvw_ref, outw_ref, ln_ref, rw_ref, work):
    grp = ids[0]
    core = ids[1]
    hb = qkv_ref.shape[0]
    part = hb // 2
    rows = lambda start, size: pl.ds(pl.multiple_of(start, 128), size)
    mine = grp * hb
    other = (1 - grp) * hb
    qkvw_ref[rows(mine, hb), :] = qkv_ref[...]
    outw_ref[rows(mine, hb), :] = out_ref[...]
    for ref, at in ((near_ref, other + core * part), (far_ref, other + (1 - core) * part)):
        qkvw_ref[rows(at, part), :] = ref[:, 0 : 3 * D]
        outw_ref[rows(at, part), :] = ref[:, 3 * D : 4 * D]
    ln_ref[...] = jnp.zeros_like(ln_ref)
    work[...] = jnp.zeros_like(work)
    lane = lanes((hb, AUX))
    for these, at in ((small_ref[...], mine), (near_ref[0:16, 4 * D :], other)):
        work[0:16, :] = these.astype(F32)
        ln_ref[0:4, rows(at, hb)] = work[0:4, :]
        router = pltpu.roll(jnp.transpose(work[...]), AUX - 4, 1)
        rw_ref[rows(at, hb), :] = jnp.where(lane < E, router, 0.0).astype(BF16)


def gathered(ids, qkv_weight, out_weight, near, far, small):
    return pl.pallas_call(
        gather_kernel,
        grid_spec=pltpu.PrefetchScalarGridSpec(
            num_scalar_prefetch=1,
            grid=(1,),
            in_specs=[pl.BlockSpec(a.shape, lambda i, s: (0, 0)) for a in (qkv_weight, out_weight, near, far, small)],
            out_specs=[pl.BlockSpec(shape, lambda i, s: (0, 0)) for shape in ((D, 3 * D), (D, D), (8, D), (D, AUX))],
            scratch_shapes=[pltpu.VMEM((AUX, qkv_weight.shape[0]), F32)],
        ),
        out_shape=[
            jax.ShapeDtypeStruct((D, 3 * D), BF16),
            jax.ShapeDtypeStruct((D, D), BF16),
            jax.ShapeDtypeStruct((8, D), F32),
            jax.ShapeDtypeStruct((D, AUX), BF16),
        ],
        compiler_params=params("arbitrary"),
        cost_estimate=cost(3),
        name="gathered",
    )(ids, qkv_weight, out_weight, near, far, small)


class Order:
    def __init__(self):
        self.last = None

    def __call__(self, *values):
        if self.last is None:
            return values
        return lax.optimization_barrier((*values, self.last))[:-1]

    def done(self, value):
        self.last = value
        return value

    def pass_on(self, value):
        (value,) = self(value)
        return self.done(value)


def per_device(
    reps, groups, images, ln1_gain, ln1_bias, qkv_weight, out_weight, ln2_gain, ln2_bias, router_weight, expert_in, expert_out, routes, cotangent
):
    rep = lax.axis_index("rep")
    grp = lax.axis_index("grp")
    bits = reps.bit_length() - 1
    rbit = [(rep >> i) & 1 for i in range(bits)]
    core = rbit[0]
    rswap = lambda value, bit, name: swap(value, "rep", reps, bit, f"{name}_rep{bit}")
    gswap = lambda value, name: swap(value, "grp", 2, 0, f"{name}_grp")
    pairs = groups == 2
    hb = expert_in.shape[1]
    order = Order()
    chunks = E // 2
    near_ids = [j + chunks * core for j in range(chunks)]
    far_ids = [j + chunks * (1 - core) for j in range(chunks)]
    spread = [bit for bit in (2, 1) if bit < bits]
    ways = [spread if j % 2 == 0 else spread[::-1] for j in range(chunks)]

    def first_cut(j):
        piece, size = 0, hb
        for bit in ways[j][::-1]:
            size = size // 2
            piece = piece * 2 + rbit[bit]
        win, wout = order(expert_in, expert_out)
        return order.done(cut(near_ids[j], piece, size, win, wout))

    weights = [None] * chunks
    step = [0] * chunks

    def weights_out(j):
        if not pairs:
            return
        at = step[j]
        step[j] += 1
        if at == 0:
            weights[j] = (None, gswap(first_cut(j), f"weights{j}"))
            return
        mine, other = weights[j]
        if at == 1:
            mine = order.pass_on(other)
        else:
            mine, other = order(mine, other)
            mine = order.done(joined(mine, other, rbit[ways[j][at - 2]], 1))
        weights[j] = (mine, rswap(mine, ways[j][at - 1], f"weights{j}") if at <= len(spread) else None)

    peak = [None, 0]
    last_peak = bits + groups.bit_length() - 1
    clipped = None

    def peak_more():
        nonlocal clipped
        value, at = peak
        if at > last_peak + 1:
            return
        if at > 0:
            value = order(*value)
            value = order.done(jnp.maximum(*value))
        if at < last_peak - bits:
            peak[0] = (value, swap(value, "grp", groups, at, "peak_grp"))
        elif at < last_peak:
            peak[0] = (value, rswap(value, at - (last_peak - bits), "peak"))
        else:
            clip = jnp.sqrt(CLIP_LIMIT / jnp.maximum(value[0, :HEADS], CLIP_LIMIT))
            column_scale = jnp.tile(jnp.repeat(clip, HEAD_DIM), 2)
            clipped = order.done(qkv_weight[:, : 2 * D].astype(F32) * column_scale[None, :])
            peak[1] = last_peak + 2
            return
        peak[1] += 1

    width = ln1_gain.shape[0]
    small = jnp.concatenate(
        [jnp.stack([ln1_gain, ln1_bias, ln2_gain, ln2_bias]), jnp.transpose(router_weight), jnp.zeros((4, width), BF16)], axis=0
    )
    win0, wout0 = expert_in, expert_out
    if pairs:
        weights_out(0)
        dense = [lax.dynamic_slice_in_dim(w, core * (hb // 2), hb // 2, 0) for w in order(qkv_weight, out_weight)]
        dense = jnp.concatenate([*dense, jnp.pad(small, ((0, hb // 2 - 16), (0, 0)))], axis=1)
        near = gswap(order.done(dense), "dense")
        for j in range(1, chunks):
            weights_out(j)
        slot, slot_t, starts = route_tables(*order(routes))
        order.done(starts)
        weights_out(0)
        near = order.pass_on(near)
        far = rswap(near, 0, "dense")
        weights_out(0)
        ids = jnp.stack([grp, core]).astype(I32)
        qkvw, outw, ln, rw = gathered(ids, qkv_weight, out_weight, *order(near, far, small))
        order.done(ln)
    else:
        dense = jnp.concatenate([qkv_weight, out_weight], axis=1)
        small = lax.all_gather(small, "grp", axis=1, tiled=True)
        dense = lax.all_gather(dense, "grp", axis=0, tiled=True)
        slot, slot_t, starts = route_tables(routes)
        ln = jnp.concatenate([small[0:4].astype(F32), jnp.zeros((4, D), F32)], axis=0)
        rw = jnp.pad(jnp.transpose(small[4 : 4 + E]), ((0, 0), (0, AUX - E)))
        qkvw = dense[:, : 3 * D]
        outw = dense[:, 3 * D :]
        win0 = lax.all_gather(expert_in, "grp", axis=1, tiled=True)
        wout0 = lax.all_gather(expert_out, "grp", axis=1, tiled=True)
        weights = [(None, None)] * chunks

    (ln,) = order(ln)
    qkv, mixed, middle, rp, lse, hmax, slots = front(starts, images, cotangent, slot_t, ln, qkvw, outw, rw)
    peak[0] = order.done(hmax)

    couples = [[i, i + 1] for i in range(0, reps, 2)]

    def between_cores(value, name):
        (value,) = order(value)
        with jax.named_scope(name):
            return order.done(lax.all_to_all(value, "rep", 0, 0, axis_index_groups=couples, tiled=True))

    state = {}

    def expert(j):
        nonlocal slots
        ids = jnp.stack([near_ids[j], grp, j]).astype(I32)
        (held,) = order(slots)
        slots, *grads = expert_call(ids, held, win0, wout0, weights[j][0])
        order.done(grads[0])
        if pairs:
            state[j] = (0, grads[0], gswap(grads[1], f"grad{j}"))
        else:
            full = grads[0]
            gin = lax.psum_scatter(jnp.transpose(full[0:4], (1, 0, 2)).reshape(D, FF), "grp", scatter_dimension=0, tiled=True)
            gout = lax.psum_scatter(full[4:8].reshape(FF, D), "grp", scatter_dimension=0, tiled=True)
            part = pack(gin, gout)
            state[j] = (0, part, jnp.zeros_like(part))

    down = list(range(1, bits))
    up = down[::-1] + [0]
    placed = [None, None]
    ends = len(down) + len(up)

    def more(j):
        at, keep, recv = state[j]
        if at > ends:
            return
        keep, recv = order(keep, recv)
        n = len(down)
        if at < n:
            bit = down[at]
            keep_mine, keep_other = halves(keep, rbit[bit], 1)
            recv_mine, recv_other = halves(recv, rbit[bit], 1)
            send = add(keep_other, recv_other)
            keep = order.done(add(keep_mine, recv_mine))
            state[j] = (at + 1, keep, rswap(send, bit, f"grad{j}_down"))
        elif at < ends:
            bit = up[at - n]
            total = add(keep, recv) if at == n else joined(keep, recv, rbit[up[at - n - 1]], 1)
            order.done(total)
            state[j] = (at + 1, total, rswap(total, bit, f"grad{j}_up"))
        else:
            ids = jnp.stack([near_ids[j], far_ids[j]]).astype(I32)
            placed[0], placed[1] = place(ids, [keep], [recv], placed[0], placed[1])
            order.done(placed[0])
            state[j] = (at + 1, None, None)

    peak_more()
    weights_out(1)
    weights_out(2)
    weights_out(3)
    slots = between_cores(slots.reshape(2, chunks, SLOTS, WIDE), "slots")
    weights_out(0)
    weights_out(1)
    weights_out(2)
    peak_more()
    expert(0)
    weights_out(1)
    weights_out(3)
    peak_more()
    expert(1)
    weights_out(2)
    peak_more()
    expert(2)
    weights_out(3)
    more(0)
    peak_more()
    expert(3)
    more(0)
    more(1)
    peak_more()
    slots = between_cores(slots, "results").reshape(E, SLOTS, WIDE)
    while clipped is None:
        peak_more()
    more(0)
    more(1)
    more(2)

    n = images.shape[0]
    parts = 4
    outs, accs = [], []
    between = [
        [lambda: more(0), lambda: more(1)],
        [lambda: more(0), lambda: more(1), lambda: more(2), lambda: more(3)],
        [lambda: more(0), lambda: more(1), lambda: more(2), lambda: more(3)],
        [],
    ]
    for i in range(parts):
        (held,) = order(slots)
        *outs, gqkv, gout, gmisc = back(
            i * (n // parts), n // parts, starts, held, slot, middle, images, cotangent, rp, mixed, qkv, lse, ln, qkvw, outw, rw, [*outs, *accs]
        )
        order.done(gmisc)
        accs = [gqkv, gout, gmisc]
        for step in between[i]:
            step()

    dense_at = [0]
    acc = jnp.concatenate(order(*accs), axis=1).astype(BF16)
    dense_state = [acc.reshape(groups, D // groups, -1), None]
    final = None

    def dense_more():
        nonlocal final
        at = dense_at[0]
        dense_at[0] += 1
        keep, recv = dense_state
        n = len(down)
        if at == 0:
            (keep,) = order(keep)
            mine, send = halves(keep, core, 1)
            order.done(send)
            dense_state[:] = [mine, rswap(send, 0, "dense_down")]
        elif at == 1:
            total = order.done(add(*order(keep, recv)))
            if pairs:
                mine = lax.dynamic_slice_in_dim(total, grp, 1, 0)[0]
                send = lax.dynamic_slice_in_dim(total, 1 - grp, 1, 0)[0]
                dense_state[:] = [mine, gswap(send, "dense_down")]
            else:
                total = lax.psum_scatter(total, "grp", scatter_dimension=0, tiled=True)[0]
                dense_state[:] = [total, jnp.zeros_like(total)]
        elif at < 2 + n:
            total = order.done(add(*order(keep, recv)))
            bit = down[at - 2]
            mine, send = halves(total, rbit[bit], 0)
            dense_state[:] = [mine, rswap(send, bit, "dense_down")]
        elif at < 2 + n + len(up):
            bit = up[at - 2 - n]
            keep, recv = order(keep, recv)
            total = add(keep, recv) if at == 2 + n else joined(keep, recv, rbit[up[at - 3 - n]], 0)
            dense_state[:] = [order.done(total), rswap(total, bit, "dense_up")]
        elif at == 2 + n + len(up):
            total = joined(*order(keep, recv), core, 0).astype(F32)
            misc = total[:, 4 * D :]
            final = (
                misc[:, 8], misc[:, 9], total[:, : 3 * D], total[:, 3 * D : 4 * D], misc[:, 10], misc[:, 11], misc[:, :E],
            )
            order.done(final[2])

    for key in (2, 1, 3, 0, -1, -1, 2, 0, 3, -1, 1, 2, -1, 1, 3, -1, 3, -1, 2, -1, 2, -1, -1, 3, -1, 3):
        if key >= 0:
            more(key)
        elif final is None:
            dense_more()
    while any(state[key][0] <= ends for key in state):
        for key in state:
            more(key)
    while final is None:
        dense_more()
    return (outs[0], outs[1], clipped, *final, placed[0], placed[1])


def solution(mesh):
    rows = P(("rep", "grp"), None, None)
    line = P("grp")
    table = P("grp", None)
    cube = P(None, "grp", None)
    in_specs = (rows, line, line, table, table, line, line, table, cube, cube, rows, rows)
    out_specs = (rows, rows, table, line, line, table, table, line, line, table, cube, cube)
    body = functools.partial(per_device, mesh.shape["rep"], mesh.shape["grp"])
    return jax.shard_map(body, mesh=mesh, in_specs=in_specs, out_specs=out_specs, check_vma=False)
```

```python
import functools
import math

import jax
import jax.numpy as jnp
from jax import lax
from jax.experimental import pallas as pl
from jax.experimental.pallas import tpu as pltpu
from jax.sharding import PartitionSpec as P

D = 512
HEADS = 8
HEAD_DIM = 64
FF = 2048
E = 8
TOP = 2
SEQ = 197
CAP = 591
ROWS = 208
SLOTS = 640
WIN = 128
AUX = 128
WIDE = 2 * D + AUX
NORM_EPS = 1e-06
CLIP_LIMIT = 3.0
SCALE = HEAD_DIM ** (-0.5)
LOW = -1e30
F32 = jnp.float32
BF16 = jnp.bfloat16
I32 = jnp.int32


def dot(a, b):
    return lax.dot_general(a, b, (((1,), (0,)), ((), ())), preferred_element_type=F32)


def dot_nt(a, b):
    return lax.dot_general(a, b, (((1,), (1,)), ((), ())), preferred_element_type=F32)


def dot_tn(a, b):
    return lax.dot_general(a, b, (((0,), (0,)), ((), ())), preferred_element_type=F32)


def params(*semantics):
    return pltpu.CompilerParams(dimension_semantics=semantics, vmem_limit_bytes=60 * 1024 * 1024)


def cost(us):
    return pl.CostEstimate(flops=int(us * 4.5e+08), transcendentals=0, bytes_accessed=1)


def lanes(shape):
    return lax.broadcasted_iota(I32, shape, len(shape) - 1)


def subs(shape):
    return lax.broadcasted_iota(I32, shape, len(shape) - 2)


def route_kernel(routes_ref, slot_ref, slot_t_ref, starts_ref, work):
    images = routes_ref.shape[0]
    lane = lanes((ROWS, 128))
    strict = (lanes((ROWS, ROWS)) < subs((ROWS, ROWS))).astype(BF16)
    work[...] = jnp.full_like(work, -100)
    hots = []
    befores = []
    run = jnp.zeros((1, 128), F32)
    for b in range(images):
        work[0:SEQ, 0:TOP] = routes_ref[b]
        both = work[...]
        hot = ((both[:, 0:1] == lane) & (lane < E)) | (both[:, 1:2] + E == lane) & (lane >= E) & (lane < 2 * E)
        hot = hot.astype(F32)
        hots.append(hot)
        befores.append(dot(strict, hot.astype(BF16)) + run)
        run = run + jnp.sum(hot, axis=0, keepdims=True)
    first = jnp.where(lanes((1, 128)) < E, run, 0.0)
    shift = pltpu.roll(first, E, 1)
    base = jnp.zeros((1, 128), F32)
    starts = jnp.zeros((16, 128), F32)
    row = subs((16, 128))
    for b in range(images):
        kept = jnp.where(befores[b] + shift < CAP, hots[b], 0.0)
        kept = kept + pltpu.roll(kept, 128 - E, 1)
        kept = jnp.where(lane < E, kept, 0.0)
        place = dot(strict, kept.astype(BF16)) + base
        slot = jnp.where(kept > 0.0, place, -1000.0)
        slot_ref[b] = slot.astype(I32)
        slot_t_ref[b] = jnp.transpose(slot)[0:E, :].astype(I32)
        starts = jnp.where(row == b, base, starts)
        base = base + jnp.sum(kept, axis=0, keepdims=True)
    starts_ref[...] = jnp.where(row == images, base, starts).astype(I32)


def route_tables(routes):
    images = routes.shape[0]
    return pl.pallas_call(
        route_kernel,
        out_shape=(
            jax.ShapeDtypeStruct((images, ROWS, 128), I32),
            jax.ShapeDtypeStruct((images, E, ROWS), I32),
            jax.ShapeDtypeStruct((16, 128), I32),
        ),
        scratch_shapes=[pltpu.VMEM((ROWS, 128), I32)],
        compiler_params=params(),
        cost_estimate=cost(4),
        name="routing",
    )(routes)


def windows(starts, b):
    firsts, needs = [], []
    passes = jnp.int32(0)
    for e in range(E):
        start = starts[b, e]
        first = (start // 16) * 16
        need = starts[b + 1, e] - first
        firsts.append(first)
        needs.append(need)
        passes = jnp.maximum(passes, (need + WIN - 1) // WIN)
    return firsts, needs, passes


def norm_stats(rows):
    center = jnp.mean(rows, axis=-1, keepdims=True)
    spread = rows - center
    rs = lax.rsqrt(jnp.mean(spread * spread, axis=-1, keepdims=True) + NORM_EPS)
    return spread * rs, rs


def head_lane(half):
    lane = lanes((ROWS, 128))
    return (lane < HEAD_DIM) if half == 0 else (lane >= HEAD_DIM)


def front_kernel(
    starts, img_ref, cot_ref, slot_t_ref, ln_ref, qkvw_ref, outw_ref, rw_ref,
    qkv_ref, mixed_ref, middle_ref, rp_ref, lse_ref, hmax_ref, slots_ref,
    xb, rhs, oh,
):
    b = pl.program_id(0)

    @pl.when(b == 0)
    def _():
        xb[...] = jnp.zeros_like(xb)
        rhs[...] = jnp.zeros_like(rhs)
        slots_ref[...] = jnp.zeros_like(slots_ref)
        hmax_ref[...] = jnp.full_like(hmax_ref, LOW)

    xb[0:SEQ, :] = img_ref[0].astype(F32)
    x = xb[...]
    n1, _ = norm_stats(x)
    normed = (n1 * ln_ref[0:1, :] + ln_ref[1:2, :]).astype(BF16)
    qkv = dot(normed, qkvw_ref[...]).astype(BF16)
    qkv_ref[0] = qkv
    zero = jnp.zeros((ROWS, 128), BF16)
    cols = lanes((ROWS, ROWS))
    real = subs((ROWS, 1)) < SEQ
    lane = lanes((ROWS, 128))
    lse_all = jnp.zeros((ROWS, 128), F32)
    peaks = jnp.full((ROWS, 128), LOW, F32)
    parts = []
    for pair in range(HEADS // 2):
        q = qkv[:, 128 * pair : 128 * pair + 128]
        k = qkv[:, D + 128 * pair : D + 128 * pair + 128]
        v = qkv[:, 2 * D + 128 * pair : 2 * D + 128 * pair + 128]
        total = None
        for half in range(2):
            mine = head_lane(half)
            s = dot_nt(q, jnp.where(mine, k, zero)) * SCALE
            s = jnp.where(cols < SEQ, s, LOW)
            top = jnp.max(s, axis=-1, keepdims=True)
            powers = jnp.exp(s - top)
            norm = jnp.sum(powers, axis=-1, keepdims=True)
            probs = (powers / norm).astype(BF16)
            part = dot(probs, jnp.where(mine, v, zero))
            total = part if total is None else total + part
            h = 2 * pair + half
            lse_all = jnp.where(lane == h, top + jnp.log(norm), lse_all)
            peaks = jnp.where((lane == h) & real, top, peaks)
        parts.append(total.astype(BF16))
    mixed = jnp.concatenate(parts, axis=1)
    mixed_ref[0] = mixed
    lse_ref[0] = jnp.transpose(lse_all)[0:HEADS, :]
    hmax_ref[...] = jnp.maximum(hmax_ref[...], jnp.max(peaks, axis=0, keepdims=True))
    middle = x + dot(mixed, outw_ref[...])
    middle_ref[0] = middle
    n2, _ = norm_stats(middle)
    hidden = (n2 * ln_ref[2:3, :] + ln_ref[3:4, :]).astype(BF16)
    logits = jnp.where(lane < E, dot(hidden, rw_ref[...]), LOW)
    powers = jnp.exp(logits - jnp.max(logits, axis=-1, keepdims=True))
    rp = powers / jnp.sum(powers, axis=-1, keepdims=True)
    rp_ref[0] = rp
    high = rp.astype(BF16).astype(F32)
    rhs[:, 0:D] = hidden
    rhs[0:SEQ, D : 2 * D] = cot_ref[0]
    rhs[:, 2 * D : WIDE] = (high + pltpu.roll(rp - high, E, 1)).astype(BF16)

    firsts, needs, passes = windows(starts, b)
    place = subs((WIN, ROWS))

    def one_pass(p, carry):
        offs = []
        for e in range(E):
            begin = firsts[e] + p * WIN
            off = pl.multiple_of(jnp.minimum(begin, SLOTS - WIN), 16)
            offs.append(off)
            named = slot_t_ref[0, e : e + 1, :]
            ok = (named >= begin) & (named < begin + WIN)
            hit = jnp.where(ok, named - off, -1) == place
            oh[WIN * e : WIN * e + WIN, :] = hit.astype(F32).astype(BF16)
        picked = dot(oh[...], rhs[...]).astype(BF16)
        for e in range(E):

            @pl.when(p * WIN < needs[e])
            def _():
                slots_ref[e, pl.ds(offs[e], WIN), :] += picked[WIN * e : WIN * e + WIN, :]

        return carry

    lax.fori_loop(0, passes, one_pass, 0)


def front(starts, images, cot, slot_t, ln, qkvw, outw, rw):
    n = images.shape[0]
    whole = lambda shape: pl.BlockSpec(shape, lambda b, s: (0,) * len(shape), pipeline_mode=pl.Buffered(1))
    item = lambda *shape: pl.BlockSpec((1,) + shape, lambda b, s: (b,) + (0,) * len(shape))
    return pl.pallas_call(
        front_kernel,
        grid_spec=pltpu.PrefetchScalarGridSpec(
            num_scalar_prefetch=1,
            grid=(n,),
            in_specs=[
                item(SEQ, D), item(SEQ, D), item(E, ROWS), whole((8, D)), whole((D, 3 * D)), whole((D, D)), whole((D, AUX)),
            ],
            out_specs=[
                item(ROWS, 3 * D), item(ROWS, D), item(ROWS, D), item(ROWS, AUX), item(HEADS, ROWS),
                whole((1, 128)), whole((E, SLOTS, WIDE)),
            ],
            scratch_shapes=[
                pltpu.VMEM((ROWS, D), F32), pltpu.VMEM((ROWS, WIDE), BF16), pltpu.VMEM((E * WIN, ROWS), BF16),
            ],
        ),
        out_shape=(
            jax.ShapeDtypeStruct((n, ROWS, 3 * D), BF16),
            jax.ShapeDtypeStruct((n, ROWS, D), BF16),
            jax.ShapeDtypeStruct((n, ROWS, D), F32),
            jax.ShapeDtypeStruct((n, ROWS, AUX), F32),
            jax.ShapeDtypeStruct((n, HEADS, ROWS), F32),
            jax.ShapeDtypeStruct((1, 128), F32),
            jax.ShapeDtypeStruct((E, SLOTS, WIDE), BF16),
        ),
        compiler_params=params("arbitrary"),
        cost_estimate=cost(40),
        name="front",
    )(starts, images, cot, slot_t, ln, qkvw, outw, rw)


def gelu_parts(pre):
    c = math.sqrt(2.0 / math.pi)
    sq = pre * pre
    t = jnp.tanh(c * pre * (1.0 + 0.044715 * sq))
    half = 0.5 * (1.0 + t)
    act = pre * half
    slope = half + 0.5 * pre * (1.0 - t * t) * (c * (1.0 + 3.0 * 0.044715 * sq))
    return act, slope


def expert_kernel(nb, ids, slots_ref, win0_ref, wout0_ref, *refs):
    refs = list(refs)
    other_ref = refs.pop(0) if nb == 2 else None
    out_ref = refs.pop(0)
    act_s, preg_s, view = refs[-3:]
    grads = refs[:-3]
    for c in range(2):
        view[SLOTS * c : SLOTS * c + SLOTS, :] = slots_ref[c, 0]
    e = ids[0]
    me = ids[1]
    hb = win0_ref.shape[1]
    spot = [me, 1 - me] if nb == 2 else [0]

    def at(ref, start, size):
        if isinstance(start, int):
            return ref[:, start : start + size]
        return ref[:, pl.ds(pl.multiple_of(start, 128), size)]

    def win(r, q):
        return win0_ref[0, :, 512 * q : 512 * q + 512] if r == 0 else other_ref[q]

    def win_cols(r, start):
        if isinstance(start, int):
            return win0_ref[0, :, start : start + hb]
        if r == 0:
            return win0_ref[0, :, pl.ds(pl.multiple_of(start, 128), hb)]
        return other_ref[start // 512, :, pl.ds(pl.multiple_of(start % 512, 128), hb)]

    def wout(r, q):
        return wout0_ref[0, hb * q : hb * q + hb, :] if r == 0 else other_ref[4 + q]

    hid = [at(view, spot[r] * hb, hb) for r in range(nb)]
    got = view[:, D : 2 * D].astype(F32)
    aux = view[:, 2 * D : WIDE].astype(F32)
    lane = lanes((2 * SLOTS, AUX))
    gate = jnp.sum(jnp.where((lane == e) | (lane == e + E), aux, 0.0), axis=-1, keepdims=True)
    resg = (gate * got).astype(BF16)
    for r in range(nb):
        for q in range(4):
            start = spot[r] * (4 * hb) + q * hb
            pre = dot(hid[0], win_cols(0, start))
            for o in range(1, nb):
                pre = pre + dot(hid[o], win_cols(o, start))
            act, slope = gelu_parts(pre)
            actg = dot_nt(resg, wout(r, q))
            if isinstance(start, int):
                act_s[:, start : start + hb] = act.astype(BF16)
                preg_s[:, start : start + hb] = (actg * slope).astype(BF16)
            else:
                act_s[:, pl.ds(pl.multiple_of(start, 128), hb)] = act.astype(BF16)
                preg_s[:, pl.ds(pl.multiple_of(start, 128), hb)] = (actg * slope).astype(BF16)
    res = None
    for r in range(nb):
        for q in range(4):
            part = dot(at(act_s, spot[r] * (4 * hb) + q * hb, hb), wout(r, q))
            res = part if res is None else res + part
    gg = jnp.sum(got * res, axis=-1, keepdims=True)
    high = gg.astype(BF16).astype(F32)
    gg = jnp.where(lane == e, high, jnp.where(lane == e + E, gg - high, 0.0)).astype(BF16)
    res = (gate * res).astype(BF16)
    for c in range(2):
        out_ref[c, 0, :, 0:D] = res[SLOTS * c : SLOTS * c + SLOTS]
        out_ref[c, 0, :, 2 * D : WIDE] = gg[SLOTS * c : SLOTS * c + SLOTS]
    for r in range(nb):
        back = None
        for q in range(4):
            part = dot_nt(preg_s[:, 512 * q : 512 * q + 512], win(r, q))
            back = part if back is None else back + part
        back = back.astype(BF16)
        for c in range(2):
            if nb == 1:
                out_ref[c, 0, :, D : 2 * D] = back[SLOTS * c : SLOTS * c + SLOTS]
            else:
                out_ref[c, 0, :, pl.ds(pl.multiple_of(D + spot[r] * hb, 128), hb)] = back[SLOTS * c : SLOTS * c + SLOTS]
    for r in range(nb):
        for q in range(4):
            gin = dot_tn(hid[r], preg_s[:, 512 * q : 512 * q + 512])
            gout = dot_tn(at(act_s, spot[r] * (4 * hb) + q * hb, hb), resg)
            grads[r][q] = gin.astype(BF16)
            grads[r][4 + q] = gout.astype(BF16)


def expert_call(ids, slots, win0, wout0, other):
    nb = 1 if other is None else 2
    hb = win0.shape[1]
    once = pl.BlockSpec((8, hb, 512), lambda i, s: (0, 0, 0))
    both = pl.BlockSpec((2, 1, SLOTS, WIDE), lambda i, s: (0, s[2], 0, 0))
    pick = lambda *shape: pl.BlockSpec((1,) + shape, lambda i, s: (s[0],) + (0,) * len(shape))
    return pl.pallas_call(
        functools.partial(expert_kernel, nb),
        grid_spec=pltpu.PrefetchScalarGridSpec(
            num_scalar_prefetch=1,
            grid=(1,),
            in_specs=[both, pick(hb, FF), pick(4 * hb, D)] + [once] * (nb == 2),
            out_specs=[both] + [once] * nb,
            scratch_shapes=[
                pltpu.VMEM((2 * SLOTS, FF), BF16), pltpu.VMEM((2 * SLOTS, FF), BF16), pltpu.VMEM((2 * SLOTS, WIDE), BF16),
            ],
        ),
        out_shape=[jax.ShapeDtypeStruct(slots.shape, BF16)] + [jax.ShapeDtypeStruct((8, hb, 512), BF16)] * nb,
        input_output_aliases={1: 0},
        compiler_params=params("arbitrary"),
        cost_estimate=cost(31),
        name="expert",
    )(ids, slots, win0, wout0, *([other] if nb == 2 else []))


def norm_back(grad, n, rs, gain):
    u = grad * gain
    return rs * (u - jnp.mean(u, axis=-1, keepdims=True) - n * jnp.mean(u * n, axis=-1, keepdims=True))


def back_kernel(
    base, sums, starts, ys_ref, slot_ref, middle_ref, img_ref, cot_ref, rp_ref, mixed_ref, qkv_ref, lse_ref, ln_ref, qkvw_ref, outw_ref, rw_ref,
    layer_ref, ingrad_ref, gqkv_ref, gout_ref, gmisc_ref,
    xb, gb, rhs, oh, comb, qg, lnacc,
):
    b = pl.program_id(0)

    @pl.when(b == 0)
    def _():
        xb[...] = jnp.zeros_like(xb)
        gb[...] = jnp.zeros_like(gb)
        for i, ref in enumerate((gqkv_ref, gout_ref, gmisc_ref)):
            ref[...] = sums[i][...] if sums else jnp.zeros_like(ref)
        lnacc[...] = jnp.zeros_like(lnacc)

    firsts, needs, passes = windows(starts, base + b)
    lane = lanes((ROWS, 128))
    comb[...] = jnp.zeros_like(comb)

    def one_pass(p, carry):
        for e in range(E):
            begin = firsts[e] + p * WIN
            off = pl.multiple_of(jnp.minimum(begin, SLOTS - WIN), 16)
            rhs[WIN * e : WIN * e + WIN, :] = ys_ref[e, pl.ds(off, WIN), :]
            named = slot_ref[0, :, e : e + 1]
            ok = (named >= begin) & (named < begin + WIN)
            hit = jnp.where(ok, named - off, -1) == lane
            oh[:, WIN * e : WIN * e + WIN] = hit.astype(F32).astype(BF16)
        comb[...] += dot(oh[...], rhs[...])
        return carry

    lax.fori_loop(0, passes, one_pass, 0)

    middle = middle_ref[0]
    layer_ref[0] = (middle + comb[:, 0:D])[0:SEQ, :].astype(BF16)
    pg = comb[:, 2 * D : WIDE]
    rp = rp_ref[0]
    pg = jnp.where(lane < E, pg + pltpu.roll(pg, 128 - E, 1), 0.0)
    lg = (rp * (pg - jnp.sum(rp * pg, axis=-1, keepdims=True))).astype(BF16)
    n2, rs2 = norm_stats(middle)
    g2 = ln_ref[2:3, :]
    hidden = (n2 * g2 + ln_ref[3:4, :]).astype(BF16)
    gmisc_ref[...] += dot_tn(hidden, lg)
    hg = comb[:, D : 2 * D] + dot_nt(lg, rw_ref[...])
    gb[0:SEQ, :] = cot_ref[0].astype(F32)
    lnacc[10:11, :] += jnp.sum(hg * n2, axis=0, keepdims=True)
    lnacc[11:12, :] += jnp.sum(hg, axis=0, keepdims=True)
    mid_grad = gb[...] + norm_back(hg, n2, rs2, g2)
    bg = mid_grad.astype(BF16)
    gout_ref[...] += dot_tn(mixed_ref[0], bg)
    mg = dot_nt(bg, outw_ref[...]).astype(BF16)
    zero = jnp.zeros((ROWS, 128), BF16)
    keys = subs((ROWS, ROWS))
    for pair in range(HEADS // 2):
        lo = 128 * pair
        q = qkv_ref[0, :, lo : lo + 128]
        k = qkv_ref[0, :, D + lo : D + lo + 128]
        v = qkv_ref[0, :, 2 * D + lo : 2 * D + lo + 128]
        m = mg[:, lo : lo + 128]
        dq = dk = dv = None
        for half in range(2):
            mine = head_lane(half)
            kh = jnp.where(mine, k, zero)
            h = 2 * pair + half
            st = dot_nt(kh, q) * SCALE
            pt = jnp.where(keys < SEQ, jnp.exp(st - lse_ref[0, h : h + 1, :]), 0.0)
            dp = dot_nt(jnp.where(mine, v, zero), m)
            delta = jnp.sum(pt * dp, axis=0, keepdims=True)
            ds = (pt * (dp - delta)).astype(BF16)
            a = dot(pt.astype(BF16), jnp.where(mine, m, zero))
            c = dot(ds, jnp.where(mine, q, zero))
            d = dot_tn(ds, kh)
            dv = a if dv is None else dv + a
            dk = c if dk is None else dk + c
            dq = d if dq is None else dq + d
        qg[:, lo : lo + 128] = (dq * SCALE).astype(BF16)
        qg[:, D + lo : D + lo + 128] = (dk * SCALE).astype(BF16)
        qg[:, 2 * D + lo : 2 * D + lo + 128] = dv.astype(BF16)
    xb[0:SEQ, :] = img_ref[0].astype(F32)
    n1, rs1 = norm_stats(xb[...])
    g1 = ln_ref[0:1, :]
    normed = (n1 * g1 + ln_ref[1:2, :]).astype(BF16)
    gqkv_ref[...] += dot_tn(normed, qg[...])
    ng = dot_nt(qg[...], qkvw_ref[...])
    lnacc[8:9, :] += jnp.sum(ng * n1, axis=0, keepdims=True)
    lnacc[9:10, :] += jnp.sum(ng, axis=0, keepdims=True)
    ingrad_ref[0] = (mid_grad + norm_back(ng, n1, rs1, g1))[0:SEQ, :].astype(BF16)

    @pl.when(b == pl.num_programs(0) - 1)
    def _():
        gmisc_ref[...] += jnp.transpose(lnacc[...])


def back(base, count, starts, ys, slot, middle, images, cot, rp, mixed, qkv, lse, ln, qkvw, outw, rw, olds):
    whole = lambda shape: pl.BlockSpec(shape, lambda b, s: (0,) * len(shape), pipeline_mode=pl.Buffered(1))
    item = lambda *shape: pl.BlockSpec((1,) + shape, lambda b, s: (base + b,) + (0,) * len(shape))
    keep = pl.BlockSpec(memory_space=pl.ANY)

    def kernel(*refs):
        back_kernel(base, refs[16 : 14 + len(olds)], *refs[:14], *refs[14 + len(olds) :])

    return pl.pallas_call(
        kernel,
        grid_spec=pltpu.PrefetchScalarGridSpec(
            num_scalar_prefetch=1,
            grid=(count,),
            in_specs=[
                whole((E, SLOTS, WIDE)), item(ROWS, 128), item(ROWS, D), item(SEQ, D), item(SEQ, D), item(ROWS, AUX), item(ROWS, D),
                item(ROWS, 3 * D), item(HEADS, ROWS), whole((8, D)), whole((D, 3 * D)), whole((D, D)), whole((D, AUX)),
            ] + ([keep, keep, whole((D, 3 * D)), whole((D, D)), whole((D, AUX))] if olds else []),
            out_specs=[item(SEQ, D), item(SEQ, D), whole((D, 3 * D)), whole((D, D)), whole((D, AUX))],
            scratch_shapes=[
                pltpu.VMEM((ROWS, D), F32), pltpu.VMEM((ROWS, D), F32), pltpu.VMEM((E * WIN, WIDE), BF16),
                pltpu.VMEM((ROWS, E * WIN), BF16), pltpu.VMEM((ROWS, WIDE), F32), pltpu.VMEM((ROWS, 3 * D), BF16),
                pltpu.VMEM((AUX, D), F32),
            ],
        ),
        out_shape=(
            jax.ShapeDtypeStruct(images.shape, BF16),
            jax.ShapeDtypeStruct(images.shape, BF16),
            jax.ShapeDtypeStruct((D, 3 * D), F32),
            jax.ShapeDtypeStruct((D, D), F32),
            jax.ShapeDtypeStruct((D, AUX), F32),
        ),
        input_output_aliases={14 + i: i for i in range(len(olds))},
        compiler_params=params("arbitrary"),
        cost_estimate=cost(17),
        name="back",
    )(starts, ys, slot, middle, images, cot, rp, mixed, qkv, lse, ln, qkvw, outw, rw, *olds)


def place_kernel(ids, *refs):
    in_ref, out_ref = refs[-2:]
    hb = in_ref.shape[1]

    def put(win_ref, wout_ref):
        for q in range(4):
            in_ref[0, :, 512 * q : 512 * q + 512] = win_ref[q].astype(F32)
            out_ref[0, hb * q : hb * q + hb, :] = wout_ref[q].astype(F32)

    for i in range(2):
        pl.when(pl.program_id(0) == i)(functools.partial(put, *refs[2 * i : 2 * i + 2]))


def place(ids, a, b, gin, gout):
    hb = a[0].shape[1]
    quad = lambda at: pl.BlockSpec((4, hb, 512), lambda i, s: (at, 0, 0))
    keep = pl.BlockSpec(memory_space=pl.ANY)
    fresh = gin is None
    olds = () if fresh else (gin, gout)
    args = (a[0], a[-1], b[0], b[-1], *olds)
    last = 1 if len(a) == 1 else 0
    return pl.pallas_call(
        place_kernel,
        grid_spec=pltpu.PrefetchScalarGridSpec(
            num_scalar_prefetch=1,
            grid=(2,),
            in_specs=[quad(0), quad(last), quad(0), quad(last)] + [keep] * len(olds),
            out_specs=[
                pl.BlockSpec((1, hb, FF), lambda i, s: (s[i], 0, 0)),
                pl.BlockSpec((1, 4 * hb, D), lambda i, s: (s[i], 0, 0)),
            ],
        ),
        out_shape=[jax.ShapeDtypeStruct((E, hb, FF), F32), jax.ShapeDtypeStruct((E, 4 * hb, D), F32)],
        input_output_aliases={} if fresh else {5: 0, 6: 1},
        compiler_params=params("arbitrary"),
        cost_estimate=cost(7),
        name="place",
    )(ids, *args)


def swap(value, axis, size, bit, name):
    with jax.named_scope(name):
        return lax.ppermute(value, axis, [(i, i ^ (1 << bit)) for i in range(size)])


def halves(value, flag, axis):
    size = value.shape[axis] // 2
    mine = lax.dynamic_slice_in_dim(value, flag * size, size, axis)
    other = lax.dynamic_slice_in_dim(value, (1 - flag) * size, size, axis)
    return mine, other


def joined(mine, other, flag, axis):
    return jnp.where(flag == 0, jnp.concatenate([mine, other], axis), jnp.concatenate([other, mine], axis))


def add(a, b):
    return (a.astype(F32) + b.astype(F32)).astype(BF16)


def pack(win, wout):
    hb = win.shape[0]
    return jnp.concatenate([jnp.transpose(win.reshape(hb, 4, 512), (1, 0, 2)), wout.reshape(4, hb, 512)], axis=0)


def cut_kernel(ids, win_ref, wout_ref, out_ref):
    for q in range(4):
        out_ref[q] = win_ref[0, :, 512 * q : 512 * q + 512]
        out_ref[4 + q] = wout_ref[0, q]


def cut(expert, piece, size, win, wout):
    hb = win.shape[1]
    return pl.pallas_call(
        cut_kernel,
        grid_spec=pltpu.PrefetchScalarGridSpec(
            num_scalar_prefetch=1,
            grid=(1,),
            in_specs=[
                pl.BlockSpec((1, size, FF), lambda i, s: (s[0], s[1], 0)),
                pl.BlockSpec((1, 4, size, D), lambda i, s: (s[0], 0, s[1], 0)),
            ],
            out_specs=pl.BlockSpec((8, size, 512), lambda i, s: (0, 0, 0)),
        ),
        out_shape=jax.ShapeDtypeStruct((8, size, 512), BF16),
        compiler_params=params("arbitrary"),
        cost_estimate=cost(2),
        name="cut",
    )(jnp.stack([expert, piece]).astype(I32), win, wout.reshape(E, 4, hb, D))


def gather_kernel(ids, qkv_ref, out_ref, near_ref, far_ref, small_ref, qkvw_ref, outw_ref, ln_ref, rw_ref, work):
    grp = ids[0]
    core = ids[1]
    hb = qkv_ref.shape[0]
    part = hb // 2
    rows = lambda start, size: pl.ds(pl.multiple_of(start, 128), size)
    mine = grp * hb
    other = (1 - grp) * hb
    qkvw_ref[rows(mine, hb), :] = qkv_ref[...]
    outw_ref[rows(mine, hb), :] = out_ref[...]
    for ref, at in ((near_ref, other + core * part), (far_ref, other + (1 - core) * part)):
        qkvw_ref[rows(at, part), :] = ref[:, 0 : 3 * D]
        outw_ref[rows(at, part), :] = ref[:, 3 * D : 4 * D]
    ln_ref[...] = jnp.zeros_like(ln_ref)
    work[...] = jnp.zeros_like(work)
    lane = lanes((hb, AUX))
    for these, at in ((small_ref[...], mine), (near_ref[0:16, 4 * D :], other)):
        work[0:16, :] = these.astype(F32)
        ln_ref[0:4, rows(at, hb)] = work[0:4, :]
        router = pltpu.roll(jnp.transpose(work[...]), AUX - 4, 1)
        rw_ref[rows(at, hb), :] = jnp.where(lane < E, router, 0.0).astype(BF16)


def gathered(ids, qkv_weight, out_weight, near, far, small):
    return pl.pallas_call(
        gather_kernel,
        grid_spec=pltpu.PrefetchScalarGridSpec(
            num_scalar_prefetch=1,
            grid=(1,),
            in_specs=[pl.BlockSpec(a.shape, lambda i, s: (0, 0)) for a in (qkv_weight, out_weight, near, far, small)],
            out_specs=[pl.BlockSpec(shape, lambda i, s: (0, 0)) for shape in ((D, 3 * D), (D, D), (8, D), (D, AUX))],
            scratch_shapes=[pltpu.VMEM((AUX, qkv_weight.shape[0]), F32)],
        ),
        out_shape=[
            jax.ShapeDtypeStruct((D, 3 * D), BF16),
            jax.ShapeDtypeStruct((D, D), BF16),
            jax.ShapeDtypeStruct((8, D), F32),
            jax.ShapeDtypeStruct((D, AUX), BF16),
        ],
        compiler_params=params("arbitrary"),
        cost_estimate=cost(3),
        name="gathered",
    )(ids, qkv_weight, out_weight, near, far, small)


class Order:
    def __init__(self):
        self.last = None

    def __call__(self, *values):
        if self.last is None:
            return values
        return lax.optimization_barrier((*values, self.last))[:-1]

    def done(self, value):
        self.last = value
        return value

    def pass_on(self, value):
        (value,) = self(value)
        return self.done(value)


def per_device(
    reps, groups, images, ln1_gain, ln1_bias, qkv_weight, out_weight, ln2_gain, ln2_bias, router_weight, expert_in, expert_out, routes, cotangent
):
    rep = lax.axis_index("rep")
    grp = lax.axis_index("grp")
    bits = reps.bit_length() - 1
    rbit = [(rep >> i) & 1 for i in range(bits)]
    core = rbit[0]
    rswap = lambda value, bit, name: swap(value, "rep", reps, bit, f"{name}_rep{bit}")
    gswap = lambda value, name: swap(value, "grp", 2, 0, f"{name}_grp")
    pairs = groups == 2
    hb = expert_in.shape[1]
    order = Order()
    chunks = E // 2
    near_ids = [j + chunks * core for j in range(chunks)]
    far_ids = [j + chunks * (1 - core) for j in range(chunks)]
    spread = [bit for bit in (2, 1) if bit < bits]
    ways = [spread if j % 2 == 0 else spread[::-1] for j in range(chunks)]

    def first_cut(j):
        piece, size = 0, hb
        for bit in ways[j][::-1]:
            size = size // 2
            piece = piece * 2 + rbit[bit]
        win, wout = order(expert_in, expert_out)
        return order.done(cut(near_ids[j], piece, size, win, wout))

    weights = [None] * chunks
    step = [0] * chunks

    def weights_out(j):
        if not pairs:
            return
        at = step[j]
        step[j] += 1
        if at == 0:
            weights[j] = (None, gswap(first_cut(j), f"weights{j}"))
            return
        mine, other = weights[j]
        if at == 1:
            mine = order.pass_on(other)
        else:
            mine, other = order(mine, other)
            mine = order.done(joined(mine, other, rbit[ways[j][at - 2]], 1))
        weights[j] = (mine, rswap(mine, ways[j][at - 1], f"weights{j}") if at <= len(spread) else None)

    peak = [None, 0]
    last_peak = bits + groups.bit_length() - 1
    clipped = None

    def peak_more():
        nonlocal clipped
        value, at = peak
        if at > last_peak + 1:
            return
        if at > 0:
            value = order(*value)
            value = order.done(jnp.maximum(*value))
        if at < last_peak - bits:
            peak[0] = (value, swap(value, "grp", groups, at, "peak_grp"))
        elif at < last_peak:
            peak[0] = (value, rswap(value, at - (last_peak - bits), "peak"))
        else:
            clip = jnp.sqrt(CLIP_LIMIT / jnp.maximum(value[0, :HEADS], CLIP_LIMIT))
            column_scale = jnp.tile(jnp.repeat(clip, HEAD_DIM), 2)
            clipped = order.done(qkv_weight[:, : 2 * D].astype(F32) * column_scale[None, :])
            peak[1] = last_peak + 2
            return
        peak[1] += 1

    width = ln1_gain.shape[0]
    small = jnp.concatenate(
        [jnp.stack([ln1_gain, ln1_bias, ln2_gain, ln2_bias]), jnp.transpose(router_weight), jnp.zeros((4, width), BF16)], axis=0
    )
    win0, wout0 = expert_in, expert_out
    if pairs:
        weights_out(0)
        dense = [lax.dynamic_slice_in_dim(w, core * (hb // 2), hb // 2, 0) for w in order(qkv_weight, out_weight)]
        dense = jnp.concatenate([*dense, jnp.pad(small, ((0, hb // 2 - 16), (0, 0)))], axis=1)
        near = gswap(order.done(dense), "dense")
        for j in range(1, chunks):
            weights_out(j)
        slot, slot_t, starts = route_tables(*order(routes))
        order.done(starts)
        weights_out(0)
        near = order.pass_on(near)
        far = rswap(near, 0, "dense")
        weights_out(0)
        ids = jnp.stack([grp, core]).astype(I32)
        qkvw, outw, ln, rw = gathered(ids, qkv_weight, out_weight, *order(near, far, small))
        order.done(ln)
    else:
        dense = jnp.concatenate([qkv_weight, out_weight], axis=1)
        small = lax.all_gather(small, "grp", axis=1, tiled=True)
        dense = lax.all_gather(dense, "grp", axis=0, tiled=True)
        slot, slot_t, starts = route_tables(routes)
        ln = jnp.concatenate([small[0:4].astype(F32), jnp.zeros((4, D), F32)], axis=0)
        rw = jnp.pad(jnp.transpose(small[4 : 4 + E]), ((0, 0), (0, AUX - E)))
        qkvw = dense[:, : 3 * D]
        outw = dense[:, 3 * D :]
        win0 = lax.all_gather(expert_in, "grp", axis=1, tiled=True)
        wout0 = lax.all_gather(expert_out, "grp", axis=1, tiled=True)
        weights = [(None, None)] * chunks

    (ln,) = order(ln)
    qkv, mixed, middle, rp, lse, hmax, slots = front(starts, images, cotangent, slot_t, ln, qkvw, outw, rw)
    peak[0] = order.done(hmax)

    couples = [[i, i + 1] for i in range(0, reps, 2)]

    def between_cores(value, name):
        (value,) = order(value)
        with jax.named_scope(name):
            return order.done(lax.all_to_all(value, "rep", 0, 0, axis_index_groups=couples, tiled=True))

    state = {}

    def expert(j):
        nonlocal slots
        ids = jnp.stack([near_ids[j], grp, j]).astype(I32)
        (held,) = order(slots)
        slots, *grads = expert_call(ids, held, win0, wout0, weights[j][0])
        order.done(grads[0])
        if pairs:
            state[j] = (0, grads[0], gswap(grads[1], f"grad{j}"))
        else:
            full = grads[0]
            gin = lax.psum_scatter(jnp.transpose(full[0:4], (1, 0, 2)).reshape(D, FF), "grp", scatter_dimension=0, tiled=True)
            gout = lax.psum_scatter(full[4:8].reshape(FF, D), "grp", scatter_dimension=0, tiled=True)
            part = pack(gin, gout)
            state[j] = (0, part, jnp.zeros_like(part))

    down = list(range(1, bits))
    up = down[::-1] + [0]
    placed = [None, None]
    ends = len(down) + len(up)

    def more(j):
        at, keep, recv = state[j]
        if at > ends:
            return
        keep, recv = order(keep, recv)
        n = len(down)
        if at < n:
            bit = down[at]
            keep_mine, keep_other = halves(keep, rbit[bit], 1)
            recv_mine, recv_other = halves(recv, rbit[bit], 1)
            send = add(keep_other, recv_other)
            keep = order.done(add(keep_mine, recv_mine))
            state[j] = (at + 1, keep, rswap(send, bit, f"grad{j}_down"))
        elif at < ends:
            bit = up[at - n]
            total = add(keep, recv) if at == n else joined(keep, recv, rbit[up[at - n - 1]], 1)
            order.done(total)
            state[j] = (at + 1, total, rswap(total, bit, f"grad{j}_up"))
        else:
            ids = jnp.stack([near_ids[j], far_ids[j]]).astype(I32)
            placed[0], placed[1] = place(ids, [keep], [recv], placed[0], placed[1])
            order.done(placed[0])
            state[j] = (at + 1, None, None)

    peak_more()
    weights_out(1)
    weights_out(2)
    weights_out(3)
    slots = between_cores(slots.reshape(2, chunks, SLOTS, WIDE), "slots")
    weights_out(0)
    weights_out(1)
    weights_out(2)
    peak_more()
    expert(0)
    weights_out(1)
    weights_out(3)
    peak_more()
    expert(1)
    weights_out(2)
    peak_more()
    expert(2)
    weights_out(3)
    more(0)
    peak_more()
    expert(3)
    more(0)
    more(1)
    peak_more()
    slots = between_cores(slots, "results").reshape(E, SLOTS, WIDE)
    while clipped is None:
        peak_more()
    more(0)
    more(1)
    more(2)

    n = images.shape[0]
    parts = 4
    outs, accs = [], []
    between = [
        [lambda: more(0), lambda: more(1)],
        [lambda: more(0), lambda: more(1), lambda: more(2), lambda: more(3)],
        [lambda: more(0), lambda: more(1), lambda: more(2), lambda: more(3)],
        [],
    ]
    for i in range(parts):
        (held,) = order(slots)
        *outs, gqkv, gout, gmisc = back(
            i * (n // parts), n // parts, starts, held, slot, middle, images, cotangent, rp, mixed, qkv, lse, ln, qkvw, outw, rw, [*outs, *accs]
        )
        order.done(gmisc)
        accs = [gqkv, gout, gmisc]
        for step in between[i]:
            step()

    dense_at = [0]
    acc = jnp.concatenate(order(*accs), axis=1).astype(BF16)
    dense_state = [acc.reshape(groups, D // groups, -1), None]
    final = None

    def dense_more():
        nonlocal final
        at = dense_at[0]
        dense_at[0] += 1
        keep, recv = dense_state
        n = len(down)
        if at == 0:
            (keep,) = order(keep)
            mine, send = halves(keep, core, 1)
            order.done(send)
            dense_state[:] = [mine, rswap(send, 0, "dense_down")]
        elif at == 1:
            total = order.done(add(*order(keep, recv)))
            if pairs:
                mine = lax.dynamic_slice_in_dim(total, grp, 1, 0)[0]
                send = lax.dynamic_slice_in_dim(total, 1 - grp, 1, 0)[0]
                dense_state[:] = [mine, gswap(send, "dense_down")]
            else:
                total = lax.psum_scatter(total, "grp", scatter_dimension=0, tiled=True)[0]
                dense_state[:] = [total, jnp.zeros_like(total)]
        elif at < 2 + n:
            total = order.done(add(*order(keep, recv)))
            bit = down[at - 2]
            mine, send = halves(total, rbit[bit], 0)
            dense_state[:] = [mine, rswap(send, bit, "dense_down")]
        elif at < 2 + n + len(up):
            bit = up[at - 2 - n]
            keep, recv = order(keep, recv)
            total = add(keep, recv) if at == 2 + n else joined(keep, recv, rbit[up[at - 3 - n]], 0)
            dense_state[:] = [order.done(total), rswap(total, bit, "dense_up")]
        elif at == 2 + n + len(up):
            total = joined(*order(keep, recv), core, 0).astype(F32)
            misc = total[:, 4 * D :]
            final = (
                misc[:, 8], misc[:, 9], total[:, : 3 * D], total[:, 3 * D : 4 * D], misc[:, 10], misc[:, 11], misc[:, :E],
            )
            order.done(final[2])

    for key in (2, 3, 1, 0, -1, -1, 2, 0, 3, -1, 1, 2, -1, 1, 3, -1, 3, -1, 2, -1, 2, -1, -1, 3, -1, 3):
        if key >= 0:
            more(key)
        elif final is None:
            dense_more()
    while any(state[key][0] <= ends for key in state):
        for key in state:
            more(key)
    while final is None:
        dense_more()
    return (outs[0], outs[1], clipped, *final, placed[0], placed[1])


def solution(mesh):
    rows = P(("rep", "grp"), None, None)
    line = P("grp")
    table = P("grp", None)
    cube = P(None, "grp", None)
    in_specs = (rows, line, line, table, table, line, line, table, cube, cube, rows, rows)
    out_specs = (rows, rows, table, line, line, table, table, line, line, table, cube, cube)
    body = functools.partial(per_device, mesh.shape["rep"], mesh.shape["grp"])
    return jax.shard_map(body, mesh=mesh, in_specs=in_specs, out_specs=out_specs, check_vma=False)
```
